32 devices in a mesh: gx: 8 (over z, y), gy: 4 (over x, core).
Axes of the slice: x: 2, y: 2, z: 4, core: 2. Of those that a mesh axis runs over, the one named last changes fastest.
Arguments:
- water_depth: float32 [1024, 2048], P('gx', 'gy'), may hold values from 0.5 to 2
- momentum_x: float32 [1024, 2048], P('gx', 'gy'), may hold values from -1.5 to 1.5
- momentum_y: float32 [1024, 2048], P('gx', 'gy'), may hold values from -1.5 to 1.5
- wet_mask: int32 [1024, 2048], P('gx', 'gy'), may hold values from 0 to 1, as said below
- damage_class: int32 [1024, 2048], P('gx', 'gy'), may hold values from 0 to 7
- damage_rates: float32 [8], replicated, may hold values from 0.2 to 2
- dam_cell: int32 [64], replicated, may hold values from 0 to 2097151, as said below
- releases: float32 [64, 2], replicated, may hold values from 0.5 to 4
Outputs:
- final_depth: float32 [1024, 2048], P('gx', 'gy')
- depth_adjoint: float32 [1024, 2048], P('gx', 'gy')
- release_grad: float32 [64, 2], replicated
The draws below stay inside these ranges and needn't reach their ends.
Inputs may be any that keep to these rules, and one draw needn't show every extreme that they name: Every dam's inflow cell has wet_mask 1. `dam_cell`: a cell index row * 2048 + column.
All inputs are finite; a program needn't handle non-finite values.
Results may differ from the reference program's by a relative error of at most 0.0003.
Values sent between devices are 32-bit elements; how exact they have to be, the bound alone decides.
A program may use at most 64 MiB of HBM per device.

```python
import math
import jax
import jax.numpy as jnp
from jax import lax

STEPS = 2
DAMS = 64
CLASSES = 8
NX = 1024
NY = 2048
N_GX = 8


def dam_sites(key):
    return jax.random.randint(jax.random.fold_in(key, 41), (DAMS,), 0, NX * NY).astype(jnp.int32)


def draw_dam_cell(key, part):
    return dam_sites(key)


def draw_wet_mask(key, part):
    cells = dam_sites(key)
    levels = jax.random.randint(jax.random.fold_in(key, 42), (NX, NY), 0, 100)
    wet = jnp.where(levels < 88, 1, 0).astype(jnp.int32)
    return wet.at[cells // NY, cells % NY].set(1)


def place_ends(entries, rng, smallest, high):
    longest = entries.shape.index(max(entries.shape))
    spots = []
    for shift in (0, 1):
        where = [jax.random.randint(jax.random.fold_in(rng, axis), (), 0, length) for axis, length in enumerate(entries.shape)]
        where[longest] = (where[longest] + shift) % entries.shape[longest]
        spots.append(tuple(where))
    return entries.at[spots[0]].set(smallest).at[spots[1]].set(high)


def level_of(own_key, extent, shards, smallest, high):
    loudness, own = 1.0, jax.random.fold_in(own_key, 6)
    for axis_at, parts in shards:
        draws = jnp.exp(jax.random.uniform(jax.random.fold_in(own, axis_at), (parts,), jnp.float32, smallest / len(shards), high / len(shards)))
        loudness = loudness * jnp.repeat(draws, extent[axis_at] // parts).reshape([-1 if axis == axis_at else 1 for axis in range(len(extent))])
    return loudness


def gaussian(key, extent, deviation, bound, shards=(), kind=jnp.bfloat16):
    entries = deviation * jax.random.normal(key, extent, jnp.float32)
    if shards:
        entries = entries * level_of(key, extent, shards, -0.22, 0.18)
    return jnp.clip(entries, -bound, bound).astype(kind)


def setup_inputs(seed: int = 0) -> dict:
    seeds = jax.random.split(jax.random.key(seed), 9)
    water_depth = jnp.clip(0.5 + 1.5 * jax.random.uniform(seeds[0], (NX, NY), jnp.float32) ** level_of(seeds[0], (NX, NY), ((0, 8), (1, 4)), -0.2, 0.2), 0.5, 2.0)
    momentum_x = gaussian(seeds[1], (NX, NY), 0.6, 1.5, ((0, 8), (1, 4)), jnp.float32)
    momentum_y = gaussian(seeds[2], (NX, NY), 0.6, 1.5, ((0, 8), (1, 4)), jnp.float32)
    wet_mask = draw_wet_mask(jax.random.fold_in(seeds[8], 71), 0)
    damage_class = place_ends(jax.random.randint(seeds[4], (NX, NY), 0, CLASSES), jax.random.fold_in(seeds[4], 1), 0, CLASSES - 1).astype(jnp.int32)
    damage_rates = jnp.clip(jnp.exp(jax.random.uniform(seeds[5], (CLASSES,), jnp.float32, math.log(0.2), math.log(2.0))), 0.2, 2.0)
    dam_cell = draw_dam_cell(jax.random.fold_in(seeds[8], 71), 0)
    releases = jnp.clip(jnp.exp(jax.random.uniform(seeds[7], (DAMS, STEPS), jnp.float32, math.log(0.5), math.log(4.0))), 0.5, 4.0)
    return dict(water_depth=water_depth, momentum_x=momentum_x, momentum_y=momentum_y, wet_mask=wet_mask, damage_class=damage_class, damage_rates=damage_rates, dam_cell=dam_cell, releases=releases)


GRAVITY = 9.81
TIME_RATIO = 0.05
INFLOW_GAIN = 0.25

def face_flux(h_left, n_left, t_left, h_right, n_right, t_right):
    u_left = n_left / h_left
    u_right = n_right / h_right
    c_left = jnp.sqrt(GRAVITY * h_left)
    c_right = jnp.sqrt(GRAVITY * h_right)
    slowest = jnp.minimum(jnp.minimum(u_left - c_left, u_right - c_right), 0.0)
    fastest = jnp.maximum(jnp.maximum(u_left + c_left, u_right + c_right), 0.0)
    inverse = 1.0 / (fastest - slowest)
    left_flux = (n_left, n_left * u_left + 0.5 * GRAVITY * h_left * h_left, t_left * u_left)
    right_flux = (n_right, n_right * u_right + 0.5 * GRAVITY * h_right * h_right, t_right * u_right)
    jumps = (h_right - h_left, n_right - n_left, t_right - t_left)
    return tuple(((fastest * a - slowest * b + slowest * fastest * c) * inverse for a, b, c in zip(left_flux, right_flux, jumps)))

def walled(h_low, n_low, t_low, wet_low, h_high, n_high, t_high, wet_high):
    return (jnp.where(wet_low, h_low, h_high), jnp.where(wet_low, n_low, -n_high), jnp.where(wet_low, t_low, t_high), jnp.where(wet_high, h_high, h_low), jnp.where(wet_high, n_high, -n_low), jnp.where(wet_high, t_high, t_low))

def advance(fields, wetness):
    height = jnp.where(wetness, fields[0], 1.0)
    flow_x = jnp.where(wetness, fields[1], 0.0)
    flow_y = jnp.where(wetness, fields[2], 0.0)
    flux_rows = face_flux(*walled(height[:-1, 1:-1], flow_x[:-1, 1:-1], flow_y[:-1, 1:-1], wetness[:-1, 1:-1], height[1:, 1:-1], flow_x[1:, 1:-1], flow_y[1:, 1:-1], wetness[1:, 1:-1]))
    flux_cols = face_flux(*walled(height[1:-1, :-1], flow_y[1:-1, :-1], flow_x[1:-1, :-1], wetness[1:-1, :-1], height[1:-1, 1:], flow_y[1:-1, 1:], flow_x[1:-1, 1:], wetness[1:-1, 1:]))
    change_h = flux_rows[0][1:] - flux_rows[0][:-1] + flux_cols[0][:, 1:] - flux_cols[0][:, :-1]
    change_x = flux_rows[1][1:] - flux_rows[1][:-1] + flux_cols[2][:, 1:] - flux_cols[2][:, :-1]
    change_y = flux_rows[2][1:] - flux_rows[2][:-1] + flux_cols[1][:, 1:] - flux_cols[1][:, :-1]
    inside_wet = wetness[1:-1, 1:-1]
    previous = fields[:, 1:-1, 1:-1]
    return jnp.stack((jnp.where(inside_wet, previous[0] - TIME_RATIO * change_h, previous[0]), jnp.where(inside_wet, previous[1] - TIME_RATIO * change_x, previous[1]), jnp.where(inside_wet, previous[2] - TIME_RATIO * change_y, previous[2])))

def add_inflow(height, amounts, dam_rows, dam_cols, row_start, col_start):
    local_rows = dam_rows - row_start
    local_cols = dam_cols - col_start
    inside = (local_rows >= 0) & (local_rows < height.shape[0]) & (local_cols >= 0) & (local_cols < height.shape[1])
    return height.at[jnp.clip(local_rows, 0, height.shape[0] - 1), jnp.clip(local_cols, 0, height.shape[1] - 1)].add(jnp.where(inside, INFLOW_GAIN * amounts, 0.0))

def forward_step(fields, wetness, amounts, dam_rows, dam_cols, row_start, col_start):
    advanced = advance(fields, wetness)
    height = add_inflow(advanced[0], amounts, dam_rows, dam_cols, row_start + 1, col_start + 1)
    return jnp.concatenate((height[None], advanced[1:]), axis=0)

def cell_rates(damage_class, damage_rates, wet_mask):
    class_rate = jnp.zeros(damage_class.shape, jnp.float32)
    for class_index in range(damage_rates.shape[0]):
        class_rate = class_rate + jnp.where(damage_class == class_index, damage_rates[class_index], 0.0)
    return jnp.where(wet_mask > 0, class_rate, 0.0)

def reference(water_depth, momentum_x, momentum_y, wet_mask, damage_class, damage_rates, dam_cell, releases):
    total_rows, total_cols = water_depth.shape
    dam_rows = (dam_cell // total_cols).astype(jnp.int32)
    dam_cols = (dam_cell % total_cols).astype(jnp.int32)
    margin = 2 * STEPS
    fields = jnp.stack((water_depth, momentum_x, momentum_y))
    padded = jnp.pad(fields, ((0, 0), (margin, margin), (margin, margin)))
    wet_padded = jnp.pad(wet_mask, margin) > 0
    weight = cell_rates(damage_class, damage_rates, wet_mask)
    weight_padded = jnp.pad(weight, STEPS)
    rows_block = total_rows // N_GX
    width = total_cols + 2 * margin
    zero_index = jnp.zeros((), jnp.int32)

    def one_block(block_index):
        row_start = (block_index * rows_block).astype(jnp.int32)
        block_fields = lax.dynamic_slice(padded, (zero_index, row_start, zero_index), (3, rows_block + 2 * margin, width))
        wet_block = lax.dynamic_slice(wet_padded, (row_start, zero_index), (rows_block + 2 * margin, width))
        weights = lax.dynamic_slice(weight_padded, (row_start, zero_index), (rows_block + 2 * STEPS, total_cols + 2 * STEPS))
        owned_dams = (dam_rows >= row_start) & (dam_rows < row_start + rows_block)

        def advance_block(start_fields, own_releases):
            amounts = jnp.where(owned_dams[:, None], own_releases, releases)
            current = start_fields
            for step_index in range(STEPS):
                wet_now = wet_block[step_index:wet_block.shape[0] - step_index, step_index:width - step_index]
                current = forward_step(current, wet_now, amounts[:, step_index], dam_rows, dam_cols, row_start - margin + step_index, step_index - margin)
            return current
        ending, pullback = jax.vjp(advance_block, block_fields, releases)
        final_adjoint = jnp.stack((weights * ending[0], jnp.zeros_like(weights), jnp.zeros_like(weights)))
        field_grad, release_part = pullback(final_adjoint)
        return (ending[0, STEPS:-STEPS, STEPS:-STEPS], field_grad[0, margin:-margin, margin:-margin], release_part)
    depths, adjoints, release_parts = lax.map(one_block, jnp.arange(N_GX, dtype=jnp.int32))
    return (depths.reshape(total_rows, total_cols), adjoints.reshape(total_rows, total_cols), lax.optimization_barrier(jnp.sum(release_parts, axis=0)))
```

```python
import functools

import jax
import jax.numpy as jnp
from jax import lax
from jax.experimental import pallas as pl
from jax.experimental.pallas import tpu as pltpu
from jax.sharding import PartitionSpec as P

GRAVITY = 9.81
TIME_RATIO = 0.05
INFLOW_GAIN = 0.25
HALO = 4
LANES = 128
TOP = 8
OWN = TOP + HALO
G_STATIC, G_FIRST, G_LAST, G_BACK_LAST, G_BACK_FIRST = 2, 1, 2, 1, 1
MESH = pl.DeviceIdType.MESH


def speeds(u_l, c_l, u_r, c_r):
    low_l, low_r = u_l - c_l, u_r - c_r
    high_l, high_r = u_l + c_l, u_r + c_r
    return low_l, low_r, high_l, high_r, jnp.minimum(low_l, low_r), jnp.maximum(high_l, high_r)


def sweep(body, first, last, group):
    whole = (last - first) // group

    def run(i, carry):
        base = pl.multiple_of(i * (8 * group), 8)
        for j in range(group):
            body(base + 8 * (first + j))
        return carry

    lax.fori_loop(0, whole, run, 0)
    for chunk in range(first + whole * group, last):
        body(8 * chunk)


def picked_by(values, hot, dims):
    out = None
    for _ in range(3):
        part = values.astype(jnp.bfloat16)
        values = values - part.astype(jnp.float32)
        term = lax.dot_general(part, hot, (dims, ((), ())), preferred_element_type=jnp.float32)
        out = term if out is None else out + term
    return out


def halved_on_tie(value, picks, ties):
    return jnp.where(picks, value, jnp.where(ties, 0.5 * value, 0.0))


def speed_grads(u_l, c_l, u_r, c_r, inverse, slope_of):
    low_l, low_r, high_l, high_r, low, high = speeds(u_l, c_l, u_r, c_r)
    slow, fast = jnp.minimum(low, 0.0), jnp.maximum(high, 0.0)
    alpha = fast * inverse
    beta = -slow * inverse
    gamma = slow * alpha
    d_term, k_term = slope_of
    g_fast = -(inverse * beta) * (d_term - slow * k_term)
    g_slow = -(inverse * alpha) * (d_term - fast * k_term)
    g_slow = halved_on_tie(g_slow, low < 0.0, low == 0.0)
    g_fast = halved_on_tie(g_fast, high > 0.0, high == 0.0)
    slow_l = halved_on_tie(g_slow, low_l < low_r, low_l == low_r)
    slow_r = g_slow - slow_l
    fast_l = halved_on_tie(g_fast, high_l > high_r, high_l == high_r)
    fast_r = g_fast - fast_l
    return (
        alpha,
        beta,
        gamma,
        (fast_l + slow_l, fast_l - slow_l),
        (fast_r + slow_r, fast_r - slow_r),
    )


def kernel(
    n_gx,
    n_gy,
    total_cols,
    classes,
    depth_in,
    mx_in,
    my_in,
    wet_in,
    class_in,
    rates_in,
    dams_in,
    releases_in,
    depth_out,
    adjoint_out,
    grad_out,
    raw_d,
    raw_x,
    raw_y,
    raw_wet,
    raw_cls,
    fields,
    prims,
    statics,
    inverses,
    inflow,
    adj,
    shifted,
    col_hot,
    pack_cols,
    send_rows,
    recv_rows,
    send_cols,
    recv_cols,
    recv_corner,
    gpart,
    gsum,
    recv_gy,
    recv_gx,
    rates,
    dams,
    releases,
    small_sem,
    know_sem,
    in_sem,
    edge_send,
    edge_recv,
    gy_send,
    gy_recv,
    gx_send,
    gx_recv,
):
    rows, cols = depth_in.shape
    tiles = cols // LANES
    wide = tiles + 1
    span = rows + 2 * HALO
    chunks = span // 8
    ix, iy = lax.axis_index("gx"), lax.axis_index("gy")
    lane = lax.broadcasted_iota(jnp.int32, (8, LANES), 1)

    has_up, has_down = ix > 0, ix < n_gx - 1
    has_left, has_right = iy > 0, iy < n_gy - 1

    barrier = pltpu.get_barrier_semaphore()
    for step in range(1, n_gy):
        pl.semaphore_signal(
            barrier, inc=1, device_id=(ix, lax.rem(iy + step, n_gy)), device_id_type=MESH
        )
    sides = (
        (has_up, -1, 0),
        (has_down, 1, 0),
        (has_left, 0, -1),
        (has_right, 0, 1),
        (has_up & has_left, -1, -1),
        (has_up & has_right, -1, 1),
        (has_down & has_left, 1, -1),
        (has_down & has_right, 1, 1),
    )
    corners = 0
    for exists, dx, dy in sides[:2] + sides[4:]:
        corners = corners + exists.astype(jnp.int32)

        @pl.when(exists)
        def _(dx=dx, dy=dy):
            pl.semaphore_signal(barrier, inc=1, device_id=(ix + dx, iy + dy), device_id_type=MESH)

    small = [
        pltpu.make_async_copy(source, target, small_sem.at[index])
        for index, (source, target) in enumerate(
            ((rates_in, rates), (dams_in, dams), (releases_in, releases))
        )
    ]
    for copy in small[:1]:
        copy.start()
    loads = []
    for c in (0, tiles - 1, *range(1, tiles - 1)):
        for index, (source, target) in enumerate(
            ((wet_in, raw_wet), (class_in, raw_cls), (depth_in, raw_d), (mx_in, raw_x), (my_in, raw_y))
        ):
            copy = pltpu.make_async_copy(
                source.at[:, pl.ds(c * LANES, LANES)], target.at[c], in_sem.at[index, c]
            )
            copy.start()
            loads.append(copy)
    for copy in small[1:]:
        copy.start()

    for copy in loads:
        copy.wait()
    small[0].wait()

    rate = [rates[k] for k in range(classes)]

    def coded_chunk(c, start, size=8):
        at = (c, pl.ds(start, size), slice(None))
        wet = raw_wet[at] > 0
        cls = raw_cls[at]
        weight = jnp.full(cls.shape, rate[0])
        for k in range(1, classes):
            weight = jnp.where(cls == k, rate[k], weight)
        return (
            jnp.where(wet, raw_d[at], -1.0),
            raw_x[at],
            raw_y[at],
            jnp.where(wet, weight, 0.0),
        )

    for c in range(tiles):
        for side, start, pick in ((0, 0, 0), (1, rows - 8, 4)):
            four = coded_chunk(c, start)
            for k in range(4):
                send_rows[side, c, 4 * k : 4 * k + 4, :] = four[k][pick : pick + 4]

    def pack_body(i, carry):
        start = pl.multiple_of(i * 8, 8)
        left = coded_chunk(0, start)
        right = coded_chunk(tiles - 1, start)
        packed = jnp.zeros((8, LANES), jnp.float32)
        for k in range(4):
            mine = (lane >= 4 * k) & (lane < 4 * k + 4)
            packed = jnp.where(mine, pltpu.roll(left[k], 4 * k, 1) if k else left[k], packed)
            mine = (lane >= 16 + 4 * k) & (lane < 20 + 4 * k)
            packed = jnp.where(mine, pltpu.roll(right[k], 20 + 4 * k, 1), packed)
        pack_cols[pl.ds(start, 8), :] = packed
        return carry

    lax.fori_loop(0, rows // 8, pack_body, 0, unroll=2)
    turned = jnp.transpose(pack_cols[...])
    send_cols[0] = turned[0:16]
    send_cols[1] = turned[16:32]

    pl.semaphore_wait(barrier, (n_gy - 1) + corners)

    rounds = max(n_gx - 2, 0).bit_length()

    def reach(level):
        return (ix >= 2**level, -(2**level)), (ix + 2**level < n_gx, 2**level)

    def tell(level):
        for exists, offset in reach(level):

            @pl.when(exists)
            def _(offset=offset):
                pl.semaphore_signal(
                    know_sem.at[level], inc=1, device_id=(ix + offset, iy), device_id_type=MESH
                )

    def learn(level):
        pl.semaphore_wait(
            know_sem.at[level], sum(exists.astype(jnp.int32) for exists, _ in reach(level))
        )

    def edge_copy(index):
        _, dx, dy = sides[index]
        opposite = (1, 0, 3, 2, 7, 6, 5, 4)[index]
        if index < 2:
            source, target = send_rows.at[index], recv_rows.at[opposite]
        elif index < 4:
            source, target = send_cols.at[index - 2], recv_cols.at[opposite - 2]
        else:
            first = 0 if index < 6 else rows - 8
            source, target = pack_cols.at[pl.ds(first, 8), :], recv_corner.at[opposite - 4]
        return pltpu.make_async_remote_copy(
            src_ref=source,
            dst_ref=target,
            send_sem=edge_send.at[index],
            recv_sem=edge_recv.at[opposite],
            device_id=(ix + dx, iy + dy),
            device_id_type=MESH,
        )

    for index in (4, 5, 6, 7, 0, 1, 2, 3):

        @pl.when(sides[index][0])
        def _(index=index):
            edge_copy(index).start()

    if rounds > 0:
        tell(0)

    H, MX, MY = 0, 1, 2
    UX, UY, CC, QX, QY, TT, IH = range(7)
    WET, WGT, FMX, FMY, WDX, WSX, WDY, WSY = range(8)

    def put_start(c, at_rows, size, four):
        wet = four[0] > 0.0
        at = (c, pl.ds(at_rows, size), slice(None))
        fields[(0, H) + at] = jnp.where(wet, four[0], 1.0)
        fields[(0, MX) + at] = jnp.where(wet, four[1], 0.0)
        fields[(0, MY) + at] = jnp.where(wet, four[2], 0.0)
        statics[(WGT,) + at] = jnp.where(wet, four[3], 0.0)
        statics[(WET,) + at] = jnp.where(wet, 1.0, 0.0)

    def own_body(i, carry):
        start = pl.multiple_of(i * 8, 8)
        for c in range(tiles):
            put_start(c, start + OWN, 8, coded_chunk(c, start))
        return carry

    lax.fori_loop(0, rows // 8, own_body, 0)

    for copy in small[1:]:
        copy.wait()
    cell = dams[...]
    if total_cols & (total_cols - 1) == 0:
        dam_row = lax.shift_right_logical(cell, total_cols.bit_length() - 1)
    else:
        dam_row = lax.div(cell, total_cols)
    dam_col = cell - dam_row * total_cols
    dam_count = cell.shape[1]
    local_row = dam_row - ix * rows
    local_col = dam_col - iy * cols
    amounts = INFLOW_GAIN * releases[...]
    wide_row = lax.broadcasted_iota(jnp.int32, (span, dam_count), 0) - HALO
    row_hot = wide_row == local_row
    gain_rows = jnp.concatenate(
        [jnp.where(row_hot, amounts[s : s + 1], 0.0) for s in range(2)], axis=0
    )
    position = lax.broadcasted_iota(jnp.int32, (LANES, dam_count), 0)
    for c in range(wide):
        if c < tiles:
            column = position + c * LANES
        else:
            column = jnp.where(
                position < HALO,
                position + cols,
                jnp.where(position >= LANES - HALO, position - LANES, -2 * LANES),
            )
        hot = (column == local_col).astype(jnp.float32).astype(jnp.bfloat16)
        col_hot[c] = hot
        poured = picked_by(gain_rows, hot, ((1,), (1,)))
        inflow[0, c, TOP : TOP + span, :] = poured[:span]
        inflow[1, c, TOP : TOP + span, :] = poured[span:]

    for index in range(8):

        @pl.when(sides[index][0])
        def _(index=index):
            copy = edge_copy(index)
            copy.wait_send()
            opposite = (1, 0, 3, 2, 7, 6, 5, 4)[index]
            if index < 2:
                target = recv_rows.at[index]
            elif index < 4:
                target = recv_cols.at[index - 2]
            else:
                target = recv_corner.at[index - 4]
            pltpu.make_async_copy(target, target, edge_recv.at[index]).wait()

    if rounds > 0:
        learn(0)
        if rounds > 1:
            tell(1)

    for c in range(tiles):
        for side, exists, at_rows in ((0, has_up, TOP), (1, has_down, OWN + rows)):
            four = [recv_rows[side, c, 4 * k : 4 * k + 4, :] for k in range(4)]
            four[0] = jnp.where(exists, four[0], -1.0)
            put_start(c, at_rows, 4, four)

    halves = jnp.concatenate(
        [recv_cols[0], recv_cols[1], jnp.zeros((LANES - 32, rows), jnp.float32)], axis=0
    )
    pack_cols[...] = jnp.transpose(halves)

    def rim_tile(left_part, right_part, k, left_at, right_at, from_left, from_right):
        fill = -1.0 if k == 0 else 0.0
        on_right = (lane < HALO) & from_right
        on_left = (lane >= LANES - HALO) & from_left
        shift_r = (LANES - right_at - 4 * k) % LANES
        shift_l = (LANES - HALO - left_at - 4 * k) % LANES
        right_val = pltpu.roll(right_part, shift_r, 1) if shift_r else right_part
        left_val = pltpu.roll(left_part, shift_l, 1) if shift_l else left_part
        return jnp.where(on_right, right_val, jnp.where(on_left, left_val, fill))

    def rim_body(i, carry):
        start = pl.multiple_of(i * 8, 8)
        part = pack_cols[pl.ds(start, 8), :]
        four = [rim_tile(part, part, k, 0, 16, has_left, has_right) for k in range(4)]
        put_start(tiles, start + OWN, 8, four)
        return carry

    lax.fori_loop(0, rows // 8, rim_body, 0, unroll=2)
    for left_slot, right_slot, exists, at_rows, pick in (
        (0, 1, has_up, TOP, 4),
        (2, 3, has_down, OWN + rows, 0),
    ):
        four = [
            rim_tile(
                recv_corner[left_slot],
                recv_corner[right_slot],
                k,
                16,
                0,
                has_left & exists,
                has_right & exists,
            )[pick : pick + 4]
            for k in range(4)
        ]
        put_start(tiles, at_rows, 4, four)

    def next_lanes(values):
        turned_all = [pltpu.roll(value, LANES - 1, 1) for value in values]
        return [
            jnp.where(lane == LANES - 1, turned_all[(c + 1) % wide], turned_all[c])
            for c in range(wide)
        ]

    def with_next(get, k):
        values = [get(k, c) for c in range(wide)]
        return list(zip(values, next_lanes(values)))

    def derived(h, n):
        ih = 1.0 / h
        squared = GRAVITY * h
        return n * ih, squared * lax.rsqrt(squared), ih

    def from_previous(current, previous):
        return jnp.where(
            lane == 0, pltpu.roll(previous, 1, 1), pltpu.roll(current, 1, 1)
        )

    def put_prims(step, c, at, h, mx, my):
        ih = 1.0 / h
        ux, uy = mx * ih, my * ih
        squared = GRAVITY * h
        pressure = 0.5 * squared * h
        values = (
            ux,
            uy,
            squared * lax.rsqrt(squared),
            mx * ux + pressure,
            my * uy + pressure,
            mx * uy,
            ih,
        )
        for k, value in enumerate(values):
            prims[(step, k) + at] = value

    def static_body(row):
        start = row + TOP
        wets = [statics[WET, c, pl.ds(start, 8), :] for c in range(wide)]
        rights = next_lanes(wets)
        for c in range(wide):
            at = (c, pl.ds(start, 8), slice(None))
            wet = wets[c]
            above = statics[WET, c, pl.ds(start - 1, 8), :]
            below = statics[WET, c, pl.ds(start + 1, 8), :]
            right = rights[c]
            left = from_previous(wet, wets[(c - 1) % wide])
            statics[(FMX,) + at] = wet * below
            statics[(FMY,) + at] = wet * right
            statics[(WDX,) + at] = above - below
            statics[(WSX,) + at] = 2.0 - above - below
            statics[(WDY,) + at] = left - right
            statics[(WSY,) + at] = 2.0 - left - right
            put_prims(0, c, at, fields[(0, H) + at], fields[(0, MX) + at], fields[(0, MY) + at])

    sweep(static_body, 0, chunks, G_STATIC)

    def face(u_l, c_l, u_r, c_r, mask):
        low, high = speeds(u_l, c_l, u_r, c_r)[4:]
        slow, fast = jnp.minimum(low, 0.0), jnp.maximum(high, 0.0)
        inverse = mask / (fast - slow)
        alpha = fast * inverse
        return inverse, alpha, slow * inverse, slow * alpha

    def forward_body(step, row):
        start = row + TOP
        last = step == 1
        here = pl.ds(start, 8)
        after = pl.ds(start + 1, 8)
        before = pl.ds(start - 1, 8)

        def f_at(k, c, rows_at=here):
            return fields[step, k, c, rows_at, :]

        def p_at(k, c, rows_at=here):
            return prims[step, k, c, rows_at, :]

        col_h, col_n = with_next(f_at, H), with_next(f_at, MY)
        col_t = None if last else with_next(f_at, MX)

        def col_fluxes(c):
            (h_l, h_r), (n_l, n_r) = col_h[c], col_n[c]
            u_r, c_r, _ = derived(h_r, n_r)
            inverse, alpha, minus_beta, gamma = face(
                p_at(UY, c), p_at(CC, c), u_r, c_r, statics[FMY, c, here, :]
            )
            inverses[step, 1, c, here, :] = inverse
            out = [alpha * n_l - minus_beta * n_r + gamma * (h_r - h_l)]
            if not last:
                t_l, t_r = col_t[c]
                q_r = n_r * u_r + (0.5 * GRAVITY) * h_r * h_r
                out.append(alpha * p_at(QY, c) - minus_beta * q_r + gamma * (n_r - n_l))
                out.append(
                    alpha * p_at(TT, c) - minus_beta * (t_r * u_r) + gamma * (t_r - t_l)
                )
            return out

        previous = col_fluxes(wide - 1)
        for c in range(wide):
            at = (c, here, slice(None))
            h, mx, ux, cc = f_at(H, c), f_at(MX, c), p_at(UX, c), p_at(CC, c)
            h_r, n_r = f_at(H, c, after), f_at(MX, c, after)
            inverse, alpha, minus_beta, gamma = face(
                ux, cc, p_at(UX, c, after), p_at(CC, c, after), statics[FMX, c, here, :]
            )
            inverses[step, 0, c, here, :] = inverse
            row_flux = [alpha * mx - minus_beta * n_r + gamma * (h_r - h)]
            if not last:
                my, qx, tt = f_at(MY, c), p_at(QX, c), p_at(TT, c)
                row_flux.append(
                    alpha * qx - minus_beta * p_at(QX, c, after) + gamma * (n_r - mx)
                )
                row_flux.append(
                    alpha * tt
                    - minus_beta * p_at(TT, c, after)
                    + gamma * (f_at(MY, c, after) - my)
                )
            for k, value in enumerate(row_flux):
                shifted[k, c, here, :] = value
            current = col_fluxes(c) if c < wide - 1 else kept_col
            if c == 0:
                kept_col = previous
            changes = [
                value - shifted[k, c, before, :] + mine - from_previous(mine, other)
                if k == 0
                else None
                for k, (value, mine, other) in enumerate(zip(row_flux, current, previous))
            ]
            wet = statics[WET, c, here, :]
            gain = TIME_RATIO * wet
            new_h = h - gain * changes[0] + inflow[step, c, here, :]
            if last:
                fields[2, H, c, here, :] = new_h
                terminal = statics[WGT, c, here, :] * new_h
                adj[3, c, here, :] = terminal
                adj[4, c, here, :] = gain * terminal
            else:
                uy, qy = p_at(UY, c), p_at(QY, c)
                change_x = (
                    row_flux[1]
                    - shifted[1, c, before, :]
                    + current[2]
                    - from_previous(current[2], previous[2])
                    + statics[WDX, c, here, :] * qx
                    + statics[WSX, c, here, :] * (jnp.abs(ux) + cc) * mx
                )
                change_y = (
                    row_flux[2]
                    - shifted[2, c, before, :]
                    + current[1]
                    - from_previous(current[1], previous[1])
                    + statics[WDY, c, here, :] * qy
                    + statics[WSY, c, here, :] * (jnp.abs(uy) + cc) * my
                )
                new_x = mx - gain * change_x
                new_y = my - gain * change_y
                fields[(1, H) + at] = new_h
                fields[(1, MX) + at] = new_x
                fields[(1, MY) + at] = new_y
                put_prims(1, c, at, new_h, new_x, new_y)
            previous = current

    sweep(functools.partial(forward_body, 0), 0, chunks, G_FIRST)
    if rounds > 1:
        learn(1)
        if rounds > 2:
            tell(2)
    sweep(functools.partial(forward_body, 1), 0, chunks, G_LAST)

    def depth_body(i, carry):
        start = pl.multiple_of(i * 8, 8)
        for c in range(tiles):
            own = pl.ds(start + OWN, 8)
            depth_out[pl.ds(start, 8), c * LANES : (c + 1) * LANES] = jnp.where(
                statics[WET, c, own, :] > 0.0, fields[2, H, c, own, :], raw_d[c, pl.ds(start, 8), :]
            )
        return carry

    lax.fori_loop(0, rows // 8, depth_body, 0)
    def backward_last(row):
        start = row + TOP
        here, after, before = pl.ds(start, 8), pl.ds(start + 1, 8), pl.ds(start - 1, 8)

        def f_at(k, c, rows_at=here):
            return fields[1, k, c, rows_at, :]

        def p_at(k, c, rows_at=here):
            return prims[1, k, c, rows_at, :]

        def z_at(k, c, rows_at=here):
            return adj[4, c, rows_at, :]

        def one_face(h, n, u, cc, ih, z, inverse):
            gh = z[1] - z[0]
            slopes = (gh * (n[1] - n[0]), gh * (h[1] - h[0]))
            alpha, beta, gamma, left, right = speed_grads(u[0], cc[0], u[1], cc[1], inverse, slopes)
            jump = gamma * gh
            left_u, right_u = left[0] * ih[0], right[0] * ih[1]
            return (
                0.5 * cc[0] * ih[0] * left[1] - left_u * u[0] - jump,
                alpha * gh + left_u,
            ), (
                0.5 * cc[1] * ih[1] * right[1] - right_u * u[1] + jump,
                beta * gh + right_u,
            )

        col_h, col_n, col_z = with_next(f_at, H), with_next(f_at, MY), with_next(z_at, 0)

        def col_face(c):
            u_r, c_r, ih_r = derived(col_h[c][1], col_n[c][1])
            return one_face(
                col_h[c], col_n[c], (p_at(UY, c), u_r), (p_at(CC, c), c_r), (p_at(IH, c), ih_r),
                col_z[c], inverses[1, 1, c, here, :],
            )

        edge = col_face(wide - 1)
        previous = edge
        for c in range(wide):

            def pair(get, k):
                return get(k, c), get(k, c, after)

            left, right = one_face(
                pair(f_at, H), pair(f_at, MX), pair(p_at, UX), pair(p_at, CC), pair(p_at, IH),
                pair(z_at, 0), inverses[1, 0, c, here, :],
            )
            for k in range(2):
                shifted[k, c, here, :] = right[k]
            in_x = [left[k] + shifted[k, c, before, :] for k in range(2)]
            current = col_face(c) if c < wide - 1 else edge
            in_y = [
                current[0][k] + from_previous(current[1][k], previous[1][k]) for k in range(2)
            ]
            previous = current
            adj_h = adj[3, c, here, :] + in_x[0] + in_y[0]
            gain = TIME_RATIO * statics[WET, c, here, :]
            adj[5, c, here, :] = adj_h
            adj[0, c, here, :] = gain * adj_h
            adj[1, c, here, :] = gain * in_x[1]
            adj[2, c, here, :] = gain * in_y[1]

    sweep(backward_last, 0, chunks, G_BACK_LAST)

    own_hot = lax.broadcasted_iota(jnp.int32, (rows, dam_count), 0) == local_row
    gpart[...] = jnp.zeros(gpart.shape, jnp.float32)
    for s, plane in ((0, 5), (1, 3)):
        picked = jnp.zeros((rows, dam_count), jnp.float32)
        for c in range(tiles):
            picked = picked + picked_by(
                adj[plane, c, OWN : OWN + rows, :], col_hot[c], ((1,), (0,))
            )
        gpart[s : s + 1, 0:dam_count] = INFLOW_GAIN * jnp.sum(
            jnp.where(own_hot, picked, 0.0), axis=0, keepdims=True
        )

    def gy_copy(step):
        return pltpu.make_async_remote_copy(
            src_ref=gpart,
            dst_ref=recv_gy.at[step - 1],
            send_sem=gy_send.at[step - 1],
            recv_sem=gy_recv.at[step - 1],
            device_id=(ix, lax.rem(iy + step, n_gy)),
            device_id_type=MESH,
        )

    def gx_copy(step):
        return pltpu.make_async_remote_copy(
            src_ref=gsum,
            dst_ref=recv_gx.at[step - 1],
            send_sem=gx_send.at[step - 1],
            recv_sem=gx_recv.at[step - 1],
            device_id=(lax.rem(ix + step, n_gx), iy),
            device_id_type=MESH,
        )

    for step in range(1, n_gy):
        gy_copy(step).start()

    def backward_first(row):
        start = row + OWN - 8
        out_row = max(row - 8, 0) if isinstance(row, int) else pl.multiple_of(jnp.maximum(row - 8, 0), 8)
        here, after, before = pl.ds(start, 8), pl.ds(start + 1, 8), pl.ds(start - 1, 8)

        def f_at(k, c, rows_at=here):
            return fields[0, k, c, rows_at, :]

        def p_at(k, c, rows_at=here):
            return prims[0, k, c, rows_at, :]

        def z_at(k, c, rows_at=here):
            return adj[k, c, rows_at, :]

        def one_face(h, n, t, u, cc, ih, q, v, zh, zn, zt, inverse):
            gh, gn, gt = zh[1] - zh[0], zn[1] - zn[0], zt[1] - zt[0]
            dn = n[1] - n[0]
            slopes = (
                gh * dn + gn * (q[1] - q[0]) + gt * (v[1] - v[0]),
                gh * (h[1] - h[0]) + gn * dn + gt * (t[1] - t[0]),
            )
            alpha, beta, gamma, left, right = speed_grads(u[0], cc[0], u[1], cc[1], inverse, slopes)
            jump = gamma * gh
            out = []
            for k, share, (g_u, g_c) in ((0, alpha, left), (1, beta, right)):
                g_u = g_u + share * (gn * n[k] + gt * t[k])
                rest = GRAVITY * h[k] * (share * gn) + ih[k] * (0.5 * cc[k] * g_c - g_u * u[k])
                out.append(rest - jump if k == 0 else rest + jump)
            return out

        col_h, col_n, col_t = with_next(f_at, H), with_next(f_at, MY), with_next(f_at, MX)
        col_zh, col_zn, col_zt = with_next(z_at, 0), with_next(z_at, 2), with_next(z_at, 1)

        def col_face(c):
            h_r, n_r, t_r = col_h[c][1], col_n[c][1], col_t[c][1]
            u_r, c_r, ih_r = derived(h_r, n_r)
            q_r = n_r * u_r + (0.5 * GRAVITY) * h_r * h_r
            return one_face(
                col_h[c], col_n[c], col_t[c], (p_at(UY, c), u_r), (p_at(CC, c), c_r),
                (p_at(IH, c), ih_r), (p_at(QY, c), q_r), (p_at(TT, c), t_r * u_r),
                col_zh[c], col_zn[c], col_zt[c], inverses[0, 1, c, here, :],
            )

        previous = col_face(wide - 1)
        for c in range(tiles):

            def pair(get, k):
                return get(k, c), get(k, c, after)

            left, right = one_face(
                pair(f_at, H), pair(f_at, MX), pair(f_at, MY), pair(p_at, UX), pair(p_at, CC),
                pair(p_at, IH), pair(p_at, QX), pair(p_at, TT), pair(z_at, 0), pair(z_at, 1),
                pair(z_at, 2), inverses[0, 0, c, here, :],
            )
            shifted[0, c, here, :] = right
            current = col_face(c)
            across = left + shifted[0, c, before, :] + current[0]
            across = across + from_previous(current[1], previous[1])
            previous = current
            h, mx, my = f_at(H, c), f_at(MX, c), f_at(MY, c)
            ux, uy, ih = p_at(UX, c), p_at(UY, c), p_at(IH, c)
            zx, zy = z_at(1, c), z_at(2, c)
            normal_x = zx * statics[WDX, c, here, :]
            normal_y = zy * statics[WDY, c, here, :]
            wall_x = zx * statics[WSX, c, here, :] * mx
            wall_y = zy * statics[WSY, c, here, :] * my

            adjoint_out[pl.ds(out_row, 8), c * LANES : (c + 1) * LANES] = (
                adj[5, c, here, :]
                + across
                - GRAVITY * h * (normal_x + normal_y)
                + ih
                * (
                    normal_x * mx * ux
                    + normal_y * my * uy
                    + wall_x * jnp.abs(ux)
                    + wall_y * jnp.abs(uy)
                    - 0.5 * p_at(CC, c) * (wall_x + wall_y)
                )
            )

    runs = rows // 8 + 1
    half = runs // 2 // G_BACK_FIRST * G_BACK_FIRST
    sweep(backward_first, 0, half, G_BACK_FIRST)

    for step in range(1, n_gy):
        gy_copy(step).wait()
    total = gpart[...]
    for step in range(1, n_gy):
        total = total + recv_gy[step - 1]
    gsum[...] = total
    for level in range(2, rounds):
        learn(level)
        if level + 1 < rounds:
            tell(level + 1)
    for step in range(1, n_gx):
        gx_copy(step).start()

    sweep(backward_first, half, runs, G_BACK_FIRST)
    for step in range(1, n_gx):
        gx_copy(step).wait()
    for step in range(1, n_gx):
        total = total + recv_gx[step - 1]
    grad_out[...] = total[0:2, 0:dam_count]


def on_device(
    n_gx,
    n_gy,
    water_depth,
    momentum_x,
    momentum_y,
    wet_mask,
    damage_class,
    damage_rates,
    dam_cell,
    releases,
):
    rows, cols = water_depth.shape
    tiles = cols // LANES
    wide = tiles + 1
    high = rows + 2 * HALO + 2 * TOP
    dam_count = dam_cell.shape[0]
    f32 = jnp.float32
    plane = (wide, high, LANES)
    own = (tiles, rows, LANES)
    anywhere = pl.BlockSpec(memory_space=pl.ANY)
    vmem = pl.BlockSpec(memory_space=pltpu.VMEM)
    dma = pltpu.SemaphoreType.DMA
    final_depth, adjoint, grad = pl.pallas_call(
        functools.partial(kernel, n_gx, n_gy, cols * n_gy, damage_rates.shape[0]),
        out_shape=(
            pltpu.VMEM((rows, cols), f32),
            pltpu.VMEM((rows, cols), f32),
            pltpu.VMEM(releases.shape[::-1], f32),
        ),
        in_specs=[anywhere] * 8,
        out_specs=(vmem, vmem, vmem),
        scratch_shapes=[
            pltpu.VMEM(own, f32),
            pltpu.VMEM(own, f32),
            pltpu.VMEM(own, f32),
            pltpu.VMEM(own, jnp.int32),
            pltpu.VMEM(own, jnp.int32),
            pltpu.VMEM((3, 3) + plane, f32),
            pltpu.VMEM((2, 7) + plane, f32),
            pltpu.VMEM((8,) + plane, f32),
            pltpu.VMEM((2, 2) + plane, f32),
            pltpu.VMEM((2,) + plane, f32),
            pltpu.VMEM((6,) + plane, f32),
            pltpu.VMEM((3,) + plane, f32),
            pltpu.VMEM((wide, LANES, dam_count), jnp.bfloat16),
            pltpu.VMEM((rows, LANES), f32),
            pltpu.VMEM((2, tiles, 16, LANES), f32),
            pltpu.VMEM((2, tiles, 16, LANES), f32),
            pltpu.VMEM((2, 16, rows), f32),
            pltpu.VMEM((2, 16, rows), f32),
            pltpu.VMEM((4, 8, LANES), f32),
            pltpu.VMEM((8, LANES), f32),
            pltpu.VMEM((8, LANES), f32),
            pltpu.VMEM((n_gy - 1, 8, LANES), f32),
            pltpu.VMEM((n_gx - 1, 8, LANES), f32),
            pltpu.SMEM(damage_rates.shape, f32),
            pltpu.VMEM((1, dam_count), jnp.int32),
            pltpu.VMEM(releases.shape[::-1], f32),
            dma((3,)),
            pltpu.SemaphoreType.REGULAR((max(n_gx - 2, 1).bit_length(),)),
            dma((5, tiles)),
            dma((8,)),
            dma((8,)),
            dma((n_gy - 1,)),
            dma((n_gy - 1,)),
            dma((n_gx - 1,)),
            dma((n_gx - 1,)),
        ],
        compiler_params=pltpu.CompilerParams(
            collective_id=0, has_side_effects=True, vmem_limit_bytes=56 * 1024 * 1024
        ),
        name="window",
    )(
        water_depth,
        momentum_x,
        momentum_y,
        wet_mask,
        damage_class,
        damage_rates,
        dam_cell.reshape(1, dam_count),
        releases.T,
    )
    return final_depth, adjoint, grad.T


def solution(mesh):
    n_gx, n_gy = mesh.shape["gx"], mesh.shape["gy"]
    grid = P("gx", "gy")
    return jax.shard_map(
        functools.partial(on_device, n_gx, n_gy),
        mesh=mesh,
        in_specs=(grid,) * 5 + (P(),) * 3,
        out_specs=(grid, grid, P()),
        check_vma=False,
    )
```

```python
import functools

import jax
import jax.numpy as jnp
from jax import lax
from jax.experimental import pallas as pl
from jax.experimental.pallas import tpu as pltpu
from jax.sharding import PartitionSpec as P

GRAVITY = 9.81
TIME_RATIO = 0.05
INFLOW_GAIN = 0.25
HALO = 4
LANES = 128
TOP = 8
OWN = TOP + HALO
G_STATIC, G_FIRST, G_LAST, G_BACK_LAST, G_BACK_FIRST = 2, 1, 2, 1, 1
MESH = pl.DeviceIdType.MESH


def sweep(body, first, last, group):
    whole = (last - first) // group

    def run(i, carry):
        base = pl.multiple_of(i * (8 * group), 8)
        for j in range(group):
            body(base + 8 * (first + j))
        return carry

    lax.fori_loop(0, whole, run, 0)
    for chunk in range(first + whole * group, last):
        body(8 * chunk)


def picked_by(values, hot, dims):
    out = None
    for _ in range(3):
        part = values.astype(jnp.bfloat16)
        values = values - part.astype(jnp.float32)
        term = lax.dot_general(part, hot, (dims, ((), ())), preferred_element_type=jnp.float32)
        out = term if out is None else out + term
    return out


def halved_on_tie(value, picks, ties):
    return jnp.where(picks, value, jnp.where(ties, 0.5 * value, 0.0))


def split_speed_grads(lm_l, lm_r, lp_l, lp_r, coefs, d_term, k_term):
    _, _, _, slow, fast, e_slow, e_fast = coefs
    g_slow = e_slow * (fast * k_term - d_term)
    g_fast = e_fast * (d_term - slow * k_term)
    slow_l = halved_on_tie(g_slow, lm_l < lm_r, lm_l == lm_r)
    fast_l = halved_on_tie(g_fast, lp_l > lp_r, lp_l == lp_r)
    return fast_l, slow_l, g_fast - fast_l, g_slow - slow_l


def kernel(
    n_gx,
    n_gy,
    total_cols,
    classes,
    depth_in,
    mx_in,
    my_in,
    wet_in,
    class_in,
    rates_in,
    dams_in,
    releases_in,
    depth_out,
    adjoint_out,
    grad_out,
    raw_d,
    raw_x,
    raw_y,
    raw_wet,
    raw_cls,
    first,
    second,
    statics,
    faces,
    inflow,
    adj,
    last_h,
    row_flux,
    col_flux,
    col_hot,
    pack_cols,
    send_rows,
    recv_rows,
    send_cols,
    recv_cols,
    recv_corner,
    gpart,
    gsum,
    recv_gy,
    recv_gx,
    rates,
    dams,
    releases,
    small_sem,
    know_sem,
    in_sem,
    edge_send,
    edge_recv,
    gy_send,
    gy_recv,
    gx_send,
    gx_recv,
):
    rows, cols = depth_in.shape
    tiles = cols // LANES
    wide = tiles + 1
    span = rows + 2 * HALO
    chunks = span // 8
    ix, iy = lax.axis_index("gx"), lax.axis_index("gy")
    lane = lax.broadcasted_iota(jnp.int32, (8, LANES), 1)

    has_up, has_down = ix > 0, ix < n_gx - 1
    has_left, has_right = iy > 0, iy < n_gy - 1

    barrier = pltpu.get_barrier_semaphore()
    for step in range(1, n_gy):
        pl.semaphore_signal(
            barrier, inc=1, device_id=(ix, lax.rem(iy + step, n_gy)), device_id_type=MESH
        )
    sides = (
        (has_up, -1, 0),
        (has_down, 1, 0),
        (has_left, 0, -1),
        (has_right, 0, 1),
        (has_up & has_left, -1, -1),
        (has_up & has_right, -1, 1),
        (has_down & has_left, 1, -1),
        (has_down & has_right, 1, 1),
    )
    corners = 0
    for exists, dx, dy in sides[:2] + sides[4:]:
        corners = corners + exists.astype(jnp.int32)

        @pl.when(exists)
        def _(dx=dx, dy=dy):
            pl.semaphore_signal(barrier, inc=1, device_id=(ix + dx, iy + dy), device_id_type=MESH)

    small = [
        pltpu.make_async_copy(source, target, small_sem.at[index])
        for index, (source, target) in enumerate(
            ((rates_in, rates), (dams_in, dams), (releases_in, releases))
        )
    ]
    for copy in small[:1]:
        copy.start()
    loads = []
    for c in (0, tiles - 1, *range(1, tiles - 1)):
        for index, (source, target) in enumerate(
            ((wet_in, raw_wet), (class_in, raw_cls), (depth_in, raw_d), (mx_in, raw_x), (my_in, raw_y))
        ):
            copy = pltpu.make_async_copy(
                source.at[:, pl.ds(c * LANES, LANES)], target.at[c], in_sem.at[index, c]
            )
            copy.start()
            loads.append(copy)
    for copy in small[1:]:
        copy.start()

    for copy in loads:
        copy.wait()
    small[0].wait()

    rate = [rates[k] for k in range(classes)]

    def coded_chunk(c, start, size=8):
        at = (c, pl.ds(start, size), slice(None))
        wet = raw_wet[at] > 0
        cls = raw_cls[at]
        weight = jnp.full(cls.shape, rate[0])
        for k in range(1, classes):
            weight = jnp.where(cls == k, rate[k], weight)
        return (
            jnp.where(wet, raw_d[at], -1.0),
            raw_x[at],
            raw_y[at],
            jnp.where(wet, weight, 0.0),
        )

    for c in range(tiles):
        for side, start, pick in ((0, 0, 0), (1, rows - 8, 4)):
            four = coded_chunk(c, start)
            for k in range(4):
                send_rows[side, c, 4 * k : 4 * k + 4, :] = four[k][pick : pick + 4]

    def pack_body(i, carry):
        start = pl.multiple_of(i * 8, 8)
        left = coded_chunk(0, start)
        right = coded_chunk(tiles - 1, start)
        packed = jnp.zeros((8, LANES), jnp.float32)
        for k in range(4):
            mine = (lane >= 4 * k) & (lane < 4 * k + 4)
            packed = jnp.where(mine, pltpu.roll(left[k], 4 * k, 1) if k else left[k], packed)
            mine = (lane >= 16 + 4 * k) & (lane < 20 + 4 * k)
            packed = jnp.where(mine, pltpu.roll(right[k], 20 + 4 * k, 1), packed)
        pack_cols[pl.ds(start, 8), :] = packed
        return carry

    lax.fori_loop(0, rows // 8, pack_body, 0, unroll=2)
    turned = jnp.transpose(pack_cols[...])
    send_cols[0] = turned[0:16]
    send_cols[1] = turned[16:32]

    pl.semaphore_wait(barrier, (n_gy - 1) + corners)

    rounds = max(n_gx - 2, 0).bit_length()

    def reach(level):
        return (ix >= 2**level, -(2**level)), (ix + 2**level < n_gx, 2**level)

    def tell(level):
        for exists, offset in reach(level):

            @pl.when(exists)
            def _(offset=offset):
                pl.semaphore_signal(
                    know_sem.at[level], inc=1, device_id=(ix + offset, iy), device_id_type=MESH
                )

    def learn(level):
        pl.semaphore_wait(
            know_sem.at[level], sum(exists.astype(jnp.int32) for exists, _ in reach(level))
        )

    def edge_copy(index):
        _, dx, dy = sides[index]
        opposite = (1, 0, 3, 2, 7, 6, 5, 4)[index]
        if index < 2:
            source, target = send_rows.at[index], recv_rows.at[opposite]
        elif index < 4:
            source, target = send_cols.at[index - 2], recv_cols.at[opposite - 2]
        else:
            first = 0 if index < 6 else rows - 8
            source, target = pack_cols.at[pl.ds(first, 8), :], recv_corner.at[opposite - 4]
        return pltpu.make_async_remote_copy(
            src_ref=source,
            dst_ref=target,
            send_sem=edge_send.at[index],
            recv_sem=edge_recv.at[opposite],
            device_id=(ix + dx, iy + dy),
            device_id_type=MESH,
        )

    for index in (4, 5, 6, 7, 0, 1, 2, 3):

        @pl.when(sides[index][0])
        def _(index=index):
            edge_copy(index).start()

    if rounds > 0:
        tell(0)

    H, MX, MY, LMX, LPX, LMY, LPY, PX, RX, PY, RY = range(11)
    IH = 11
    QX, QY, TT, AX, AY, UV, WX, WY, BX, BY = range(11, 21)
    NEXT = 21
    WET, WGT, FMX, FMY = range(4)
    ALPHA, BETA, GAMMA, SLOW, FAST, ESLOW, EFAST = range(7)

    def put_start(c, at_rows, size, four):
        wet = four[0] > 0.0
        at = (c, pl.ds(at_rows, size), slice(None))
        first[(H,) + at] = jnp.where(wet, four[0], 1.0)
        first[(MX,) + at] = jnp.where(wet, four[1], 0.0)
        first[(MY,) + at] = jnp.where(wet, four[2], 0.0)
        statics[(WGT,) + at] = jnp.where(wet, four[3], 0.0)
        statics[(WET,) + at] = jnp.where(wet, 1.0, 0.0)

    def own_body(i, carry):
        start = pl.multiple_of(i * 8, 8)
        for c in range(tiles):
            put_start(c, start + OWN, 8, coded_chunk(c, start))
        return carry

    lax.fori_loop(0, rows // 8, own_body, 0)

    for copy in small[1:]:
        copy.wait()
    cell = dams[...]
    if total_cols & (total_cols - 1) == 0:
        dam_row = lax.shift_right_logical(cell, total_cols.bit_length() - 1)
    else:
        dam_row = lax.div(cell, total_cols)
    dam_col = cell - dam_row * total_cols
    dam_count = cell.shape[1]
    local_row = dam_row - ix * rows
    local_col = dam_col - iy * cols
    amounts = INFLOW_GAIN * releases[...]
    wide_row = lax.broadcasted_iota(jnp.int32, (span, dam_count), 0) - HALO
    row_hot = wide_row == local_row
    gain_rows = jnp.concatenate(
        [jnp.where(row_hot, amounts[s : s + 1], 0.0) for s in range(2)], axis=0
    )
    position = lax.broadcasted_iota(jnp.int32, (LANES, dam_count), 0)
    for c in range(wide):
        if c < tiles:
            column = position + c * LANES
        else:
            column = jnp.where(
                position < HALO,
                position + cols,
                jnp.where(position >= LANES - HALO, position - LANES, -2 * LANES),
            )
        hot = (column == local_col).astype(jnp.float32).astype(jnp.bfloat16)
        col_hot[c] = hot
        poured = picked_by(gain_rows, hot, ((1,), (1,)))
        inflow[0, c, TOP : TOP + span, :] = poured[:span]
        inflow[1, c, TOP : TOP + span, :] = poured[span:]

    for index in range(8):

        @pl.when(sides[index][0])
        def _(index=index):
            copy = edge_copy(index)
            copy.wait_send()
            opposite = (1, 0, 3, 2, 7, 6, 5, 4)[index]
            if index < 2:
                target = recv_rows.at[index]
            elif index < 4:
                target = recv_cols.at[index - 2]
            else:
                target = recv_corner.at[index - 4]
            pltpu.make_async_copy(target, target, edge_recv.at[index]).wait()

    if rounds > 0:
        learn(0)
        if rounds > 1:
            tell(1)

    for c in range(tiles):
        for side, exists, at_rows in ((0, has_up, TOP), (1, has_down, OWN + rows)):
            four = [recv_rows[side, c, 4 * k : 4 * k + 4, :] for k in range(4)]
            four[0] = jnp.where(exists, four[0], -1.0)
            put_start(c, at_rows, 4, four)

    halves = jnp.concatenate(
        [recv_cols[0], recv_cols[1], jnp.zeros((LANES - 32, rows), jnp.float32)], axis=0
    )
    pack_cols[...] = jnp.transpose(halves)

    def rim_tile(left_part, right_part, k, left_at, right_at, from_left, from_right):
        fill = -1.0 if k == 0 else 0.0
        on_right = (lane < HALO) & from_right
        on_left = (lane >= LANES - HALO) & from_left
        shift_r = (LANES - right_at - 4 * k) % LANES
        shift_l = (LANES - HALO - left_at - 4 * k) % LANES
        right_val = pltpu.roll(right_part, shift_r, 1) if shift_r else right_part
        left_val = pltpu.roll(left_part, shift_l, 1) if shift_l else left_part
        return jnp.where(on_right, right_val, jnp.where(on_left, left_val, fill))

    def rim_body(i, carry):
        start = pl.multiple_of(i * 8, 8)
        part = pack_cols[pl.ds(start, 8), :]
        four = [rim_tile(part, part, k, 0, 16, has_left, has_right) for k in range(4)]
        put_start(tiles, start + OWN, 8, four)
        return carry

    lax.fori_loop(0, rows // 8, rim_body, 0, unroll=2)
    for left_slot, right_slot, exists, at_rows, pick in (
        (0, 1, has_up, TOP, 4),
        (2, 3, has_down, OWN + rows, 0),
    ):
        four = [
            rim_tile(
                recv_corner[left_slot],
                recv_corner[right_slot],
                k,
                16,
                0,
                has_left & exists,
                has_right & exists,
            )[pick : pick + 4]
            for k in range(4)
        ]
        put_start(tiles, at_rows, 4, four)

    def next_lanes(values):
        turned_all = [pltpu.roll(value, LANES - 1, 1) for value in values]
        return [
            jnp.where(lane == LANES - 1, turned_all[(c + 1) % wide], turned_all[c])
            for c in range(wide)
        ]

    def last_lanes(values):
        turned_all = [pltpu.roll(value, 1, 1) for value in values]
        return [
            jnp.where(lane == 0, turned_all[(c - 1) % wide], turned_all[c]) for c in range(wide)
        ]

    def put_next(target, offset, here, columns):
        for k, values in columns.items():
            for c, value in enumerate(next_lanes(values)):
                target[offset + k, c, here, :] = value

    FIRST_NEXT = (H, MX, MY, LMY, LPY, QY, TT, AY, UV, PY, RY)
    SECOND_NEXT = (H, MY, LMY, LPY, PY, RY, IH)

    def base_prims(target, c, here, h, mx, my, ih):
        ux, uy = mx * ih, my * ih
        squared = GRAVITY * h
        cc = squared * lax.rsqrt(squared)
        half = 0.5 * cc
        out = {H: h, MX: mx, MY: my, LMX: ux - cc, LPX: ux + cc, LMY: uy - cc, LPY: uy + cc}
        half_i, ux_i, uy_i = half * ih, ux * ih, uy * ih
        out |= {PX: half_i - ux_i, RX: half_i + ux_i, PY: half_i - uy_i, RY: half_i + uy_i}
        return out, ux, uy, squared, cc, half

    def static_body(row):
        start = row + TOP
        here = pl.ds(start, 8)
        wets = [statics[WET, c, here, :] for c in range(wide)]
        rights, lefts = next_lanes(wets), last_lanes(wets)
        kept = {k: [] for k in FIRST_NEXT}
        for c in range(wide):
            wet = wets[c]
            above = statics[WET, c, pl.ds(start - 1, 8), :]
            below = statics[WET, c, pl.ds(start + 1, 8), :]
            scale = TIME_RATIO * wet
            statics[FMX, c, here, :] = scale * below
            statics[FMY, c, here, :] = scale * rights[c]
            h, mx, my = (first[k, c, here, :] for k in (H, MX, MY))
            ih = 1.0 / h
            out, ux, uy, squared, cc, half = base_prims(first, c, here, h, mx, my, ih)
            pressure = 0.5 * squared * h
            out[QX], out[QY], out[TT] = mx * ux + pressure, my * uy + pressure, mx * uy
            out[AX], out[AY], out[UV] = squared - ux * ux, squared - uy * uy, ux * uy
            for lower, upper, u, n, q, a, wall, back in (
                (above, below, ux, mx, QX, AX, WX, BX),
                (lefts[c], rights[c], uy, my, QY, AY, WY, BY),
            ):
                single = scale * (lower - upper)
                both = scale * (2.0 - (lower + upper))
                size = jnp.abs(u)
                out[wall] = single * out[q] + both * ((size + cc) * n)
                out[back] = single * out[a] + both * (u * (half - size))
            for k, value in out.items():
                if k not in (H, MX, MY):
                    first[k, c, here, :] = value
            for k in FIRST_NEXT:
                kept[k].append(out[k])
        put_next(first, 0, here, {NEXT + j: kept[k] for j, k in enumerate(FIRST_NEXT)})

    sweep(static_body, 0, chunks, G_STATIC)

    def reader(source, keys):
        def at(k, c, rows_at):
            return source[k, c, rows_at, :]

        def right(k, c, rows_at):
            return source[NEXT_OF[id(keys)] + keys.index(k), c, rows_at, :]

        return at, right

    SECOND_AT = 12
    NEXT_OF = {id(FIRST_NEXT): NEXT, id(SECOND_NEXT): SECOND_AT}
    f_at, f_right = reader(first, FIRST_NEXT)
    s_at, s_right = reader(second, SECOND_NEXT)

    def face(step, dim, c, here, lm_l, lm_r, lp_l, lp_r):
        low, high = jnp.minimum(lm_l, lm_r), jnp.maximum(lp_l, lp_r)
        slow, fast = jnp.minimum(low, 0.0), jnp.maximum(high, 0.0)
        inverse = 1.0 / (fast - slow)
        masked = statics[FMX + dim, c, here, :] * inverse
        alpha, beta = fast * masked, slow * masked
        gamma = slow * alpha
        e_slow = halved_on_tie(alpha * inverse, low < 0.0, low == 0.0)
        e_fast = halved_on_tie(beta * inverse, high > 0.0, high == 0.0)
        for k, value in enumerate((alpha, beta, gamma, slow, fast, e_slow, e_fast)):
            faces[step, dim, k, c, here, :] = value
        return alpha, beta, gamma

    def coefs_of(step, dim, c, here):
        return [faces[step, dim, k, c, here, :] for k in range(7)]

    def crossing(coefs, flux_l, flux_r, held_l, held_r):
        alpha, beta, gamma = coefs
        return alpha * flux_l - beta * flux_r + gamma * (held_r - held_l)

    def forward_first(row):
        start = row + TOP
        here, after, before = pl.ds(start, 8), pl.ds(start + 1, 8), pl.ds(start - 1, 8)
        cols = []
        for c in range(wide):
            coefs = face(
                0, 1, c, here, f_at(LMY, c, here), f_right(LMY, c, here),
                f_at(LPY, c, here), f_right(LPY, c, here),
            )
            cols.append([
                crossing(
                    coefs, f_at(flux, c, here), f_right(flux, c, here),
                    f_at(held, c, here), f_right(held, c, here),
                )
                for flux, held in ((MY, H), (TT, MX), (QY, MY))
            ])
        entering = [last_lanes([cols[c][k] for c in range(wide)]) for k in range(3)]
        kept = {k: [] for k in SECOND_NEXT}
        for c in range(wide):
            coefs = face(
                0, 0, c, here, f_at(LMX, c, here), f_at(LMX, c, after),
                f_at(LPX, c, here), f_at(LPX, c, after),
            )
            new = []
            for k, (flux, held) in enumerate(((MX, H), (QX, MX), (TT, MY))):
                value = crossing(
                    coefs, f_at(flux, c, here), f_at(flux, c, after),
                    f_at(held, c, here), f_at(held, c, after),
                )
                row_flux[k, c, here, :] = value
                change = value - row_flux[k, c, before, :] + (cols[c][k] - entering[k][c])
                if k > 0:
                    change = change + f_at((None, WX, WY)[k], c, here)
                new.append(f_at((H, MX, MY)[k], c, here) - change)
            h = new[0] + inflow[0, c, here, :]
            ih = 1.0 / h
            out = base_prims(second, c, here, h, new[1], new[2], ih)[0]
            out[IH] = ih
            for k, value in out.items():
                second[k, c, here, :] = value
            for k in SECOND_NEXT:
                kept[k].append(out[k])
        put_next(second, 0, here, {SECOND_AT + j: kept[k] for j, k in enumerate(SECOND_NEXT)})

    TERM, ADJ, ZX, ZY, TERM_R, ADJ_R, ZX_R, ZY_R = range(8)

    def forward_last(row):
        start = row + TOP
        here, after, before = pl.ds(start, 8), pl.ds(start + 1, 8), pl.ds(start - 1, 8)
        cols = []
        for c in range(wide):
            coefs = face(
                1, 1, c, here, s_at(LMY, c, here), s_right(LMY, c, here),
                s_at(LPY, c, here), s_right(LPY, c, here),
            )
            cols.append(
                crossing(
                    coefs, s_at(MY, c, here), s_right(MY, c, here),
                    s_at(H, c, here), s_right(H, c, here),
                )
            )
        entering = last_lanes(cols)
        terms = []
        for c in range(wide):
            coefs = face(
                1, 0, c, here, s_at(LMX, c, here), s_at(LMX, c, after),
                s_at(LPX, c, here), s_at(LPX, c, after),
            )
            value = crossing(
                coefs, s_at(MX, c, here), s_at(MX, c, after),
                s_at(H, c, here), s_at(H, c, after),
            )
            row_flux[0, c, here, :] = value
            change = value - row_flux[0, c, before, :] + (cols[c] - entering[c])
            h = s_at(H, c, here) - change + inflow[1, c, here, :]
            last_h[c, here, :] = h
            term = statics[WGT, c, here, :] * h
            adj[TERM, c, here, :] = term
            terms.append(term)
        put_next(adj, 0, here, {TERM_R: terms})

    sweep(forward_first, 0, chunks, G_FIRST)
    if rounds > 1:
        learn(1)
        if rounds > 2:
            tell(2)
    sweep(forward_last, 0, chunks, G_LAST)

    def depth_body(i, carry):
        start = pl.multiple_of(i * 8, 8)
        for c in range(tiles):
            own = pl.ds(start + OWN, 8)
            depth_out[pl.ds(start, 8), c * LANES : (c + 1) * LANES] = jnp.where(
                statics[WET, c, own, :] > 0.0, last_h[c, own, :], raw_d[c, pl.ds(start, 8), :]
            )
        return carry

    lax.fori_loop(0, rows // 8, depth_body, 0)
    def backward_last(row):
        start = row + TOP
        here, after, before = pl.ds(start, 8), pl.ds(start + 1, 8), pl.ds(start - 1, 8)

        def one_face(coefs, lm, lp, h, n, z, p, r, ih):
            alpha, beta, gamma = coefs[:3]
            gh = z[1] - z[0]
            fast_l, slow_l, fast_r, slow_r = split_speed_grads(
                *lm, *lp, coefs, gh * (n[1] - n[0]), gh * (h[1] - h[0])
            )
            jump = gamma * gh
            return (
                fast_l * p[0] - slow_l * r[0] - jump,
                alpha * gh + (fast_l + slow_l) * ih[0],
            ), (
                fast_r * p[1] - slow_r * r[1] + jump,
                (fast_r + slow_r) * ih[1] - beta * gh,
            )

        lefts, rights = [], []
        for c in range(wide):

            def pair(k):
                return s_at(k, c, here), s_right(k, c, here)

            left, right = one_face(
                coefs_of(1, 1, c, here), pair(LMY), pair(LPY), pair(H), pair(MY),
                (adj[TERM, c, here, :], adj[TERM_R, c, here, :]), pair(PY), pair(RY),
                pair(IH),
            )
            lefts.append(left)
            rights.append(right)
        entering = [last_lanes([rights[c][k] for c in range(wide)]) for k in range(2)]
        outs = []
        for c in range(wide):

            def pair(k):
                return s_at(k, c, here), s_at(k, c, after)

            left, right = one_face(
                coefs_of(1, 0, c, here), pair(LMX), pair(LPX), pair(H), pair(MX),
                (adj[TERM, c, here, :], adj[TERM, c, after, :]), pair(PX), pair(RX), pair(IH),
            )
            in_x = []
            for k in range(2):
                row_flux[k, c, here, :] = right[k]
                in_x.append(left[k] + row_flux[k, c, before, :])
            in_y = [lefts[c][k] + entering[k][c] for k in range(2)]
            out = (adj[TERM, c, here, :] + (in_x[0] + in_y[0]), in_x[1], in_y[1])
            for k, value in zip((ADJ, ZX, ZY), out):
                adj[k, c, here, :] = value
            outs.append(out)
        put_next(
            adj, 0, here,
            {k: [outs[c][j] for c in range(wide)] for j, k in enumerate((ADJ_R, ZX_R, ZY_R))},
        )

    sweep(backward_last, 0, chunks, G_BACK_LAST)

    own_hot = lax.broadcasted_iota(jnp.int32, (rows, dam_count), 0) == local_row
    gpart[...] = jnp.zeros(gpart.shape, jnp.float32)
    for s, plane in ((0, ADJ), (1, TERM)):
        picked = jnp.zeros((rows, dam_count), jnp.float32)
        for c in range(tiles):
            picked = picked + picked_by(
                adj[plane, c, OWN : OWN + rows, :], col_hot[c], ((1,), (0,))
            )
        gpart[s : s + 1, 0:dam_count] = INFLOW_GAIN * jnp.sum(
            jnp.where(own_hot, picked, 0.0), axis=0, keepdims=True
        )

    def gy_copy(step):
        return pltpu.make_async_remote_copy(
            src_ref=gpart,
            dst_ref=recv_gy.at[step - 1],
            send_sem=gy_send.at[step - 1],
            recv_sem=gy_recv.at[step - 1],
            device_id=(ix, lax.rem(iy + step, n_gy)),
            device_id_type=MESH,
        )

    def gx_copy(step):
        return pltpu.make_async_remote_copy(
            src_ref=gsum,
            dst_ref=recv_gx.at[step - 1],
            send_sem=gx_send.at[step - 1],
            recv_sem=gx_recv.at[step - 1],
            device_id=(lax.rem(ix + step, n_gx), iy),
            device_id_type=MESH,
        )

    for step in range(1, n_gy):
        gy_copy(step).start()

    def first_face(coefs, lm, lp, h, n, t, q, v, zh, zn, zt, a, uv, p, r):
        alpha, beta, gamma = coefs[:3]
        gh, gn, gt = zh[1] - zh[0], zn[1] - zn[0], zt[1] - zt[0]
        dn = n[1] - n[0]
        fast_l, slow_l, fast_r, slow_r = split_speed_grads(
            *lm, *lp, coefs,
            gh * dn + gn * (q[1] - q[0]) + gt * (v[1] - v[0]),
            gh * (h[1] - h[0]) + gn * dn + gt * (t[1] - t[0]),
        )
        jump = gamma * gh
        return (
            alpha * (gn * a[0] - gt * uv[0]) + (fast_l * p[0] - slow_l * r[0]) - jump,
            (fast_r * p[1] - slow_r * r[1]) - beta * (gn * a[1] - gt * uv[1]) + jump,
        )

    def first_row_face(c, start):
        here, after = pl.ds(start, 8), pl.ds(start + 1, 8)

        def pair(k):
            return f_at(k, c, here), f_at(k, c, after)

        def z_pair(k):
            return adj[k, c, here, :], adj[k, c, after, :]

        return first_face(
            coefs_of(0, 0, c, here), pair(LMX), pair(LPX), pair(H), pair(MX), pair(MY), pair(QX),
            pair(TT), z_pair(ADJ), z_pair(ZX), z_pair(ZY), pair(AX), pair(UV), pair(PX), pair(RX),
        )

    for c in range(tiles):
        row_flux[0, c, pl.ds(OWN - 8, 8), :] = first_row_face(c, OWN - 8)[1]

    def backward_first(row):
        start = row + OWN
        here, before = pl.ds(start, 8), pl.ds(start - 1, 8)

        def col_face(c):
            def pair(k):
                return f_at(k, c, here), f_right(k, c, here)

            def z_pair(k):
                return adj[k, c, here, :], adj[k + TERM_R - TERM, c, here, :]

            return first_face(
                coefs_of(0, 1, c, here), pair(LMY), pair(LPY), pair(H), pair(MY), pair(MX),
                pair(QY), pair(TT), z_pair(ADJ), z_pair(ZY), z_pair(ZX), pair(AY), pair(UV),
                pair(PY), pair(RY),
            )

        turned = pltpu.roll(col_face(wide - 1)[1], 1, 1)
        for c in range(tiles):
            left, right = first_row_face(c, start)
            row_flux[0, c, here, :] = right
            left_y, right_y = col_face(c)
            turned, last = pltpu.roll(right_y, 1, 1), turned
            entering = jnp.where(lane == 0, last, turned)
            across = left + row_flux[0, c, before, :] + (left_y + entering)
            walls = adj[ZX, c, here, :] * f_at(BX, c, here) + adj[ZY, c, here, :] * f_at(BY, c, here)
            adjoint_out[pl.ds(row, 8), c * LANES : (c + 1) * LANES] = (
                adj[ADJ, c, here, :] + across - walls
            )

    half = rows // 16 // G_BACK_FIRST * G_BACK_FIRST
    sweep(backward_first, 0, half, G_BACK_FIRST)

    for step in range(1, n_gy):
        gy_copy(step).wait()
    total = gpart[...]
    for step in range(1, n_gy):
        total = total + recv_gy[step - 1]
    gsum[...] = total
    for level in range(2, rounds):
        learn(level)
        if level + 1 < rounds:
            tell(level + 1)
    for step in range(1, n_gx):
        gx_copy(step).start()

    sweep(backward_first, half, rows // 8, G_BACK_FIRST)
    for step in range(1, n_gx):
        gx_copy(step).wait()
    for step in range(1, n_gx):
        total = total + recv_gx[step - 1]
    grad_out[...] = total[0:2, 0:dam_count]


def on_device(
    n_gx,
    n_gy,
    water_depth,
    momentum_x,
    momentum_y,
    wet_mask,
    damage_class,
    damage_rates,
    dam_cell,
    releases,
):
    rows, cols = water_depth.shape
    tiles = cols // LANES
    wide = tiles + 1
    high = rows + 2 * HALO + 2 * TOP
    dam_count = dam_cell.shape[0]
    f32 = jnp.float32
    plane = (wide, high, LANES)
    own = (tiles, rows, LANES)
    anywhere = pl.BlockSpec(memory_space=pl.ANY)
    vmem = pl.BlockSpec(memory_space=pltpu.VMEM)
    dma = pltpu.SemaphoreType.DMA
    final_depth, adjoint, grad = pl.pallas_call(
        functools.partial(kernel, n_gx, n_gy, cols * n_gy, damage_rates.shape[0]),
        out_shape=(
            pltpu.VMEM((rows, cols), f32),
            pltpu.VMEM((rows, cols), f32),
            pltpu.VMEM(releases.shape[::-1], f32),
        ),
        in_specs=[anywhere] * 8,
        out_specs=(vmem, vmem, vmem),
        scratch_shapes=[
            pltpu.VMEM(own, f32),
            pltpu.VMEM(own, f32),
            pltpu.VMEM(own, f32),
            pltpu.VMEM(own, jnp.int32),
            pltpu.VMEM(own, jnp.int32),
            pltpu.VMEM((32,) + plane, f32),
            pltpu.VMEM((19,) + plane, f32),
            pltpu.VMEM((4,) + plane, f32),
            pltpu.VMEM((2, 2, 7) + plane, f32),
            pltpu.VMEM((2,) + plane, f32),
            pltpu.VMEM((8,) + plane, f32),
            pltpu.VMEM(plane, f32),
            pltpu.VMEM((3,) + plane, f32),
            pltpu.VMEM((3,) + plane, f32),
            pltpu.VMEM((wide, LANES, dam_count), jnp.bfloat16),
            pltpu.VMEM((rows, LANES), f32),
            pltpu.VMEM((2, tiles, 16, LANES), f32),
            pltpu.VMEM((2, tiles, 16, LANES), f32),
            pltpu.VMEM((2, 16, rows), f32),
            pltpu.VMEM((2, 16, rows), f32),
            pltpu.VMEM((4, 8, LANES), f32),
            pltpu.VMEM((8, LANES), f32),
            pltpu.VMEM((8, LANES), f32),
            pltpu.VMEM((n_gy - 1, 8, LANES), f32),
            pltpu.VMEM((n_gx - 1, 8, LANES), f32),
            pltpu.SMEM(damage_rates.shape, f32),
            pltpu.VMEM((1, dam_count), jnp.int32),
            pltpu.VMEM(releases.shape[::-1], f32),
            dma((3,)),
            pltpu.SemaphoreType.REGULAR((max(n_gx - 2, 1).bit_length(),)),
            dma((5, tiles)),
            dma((8,)),
            dma((8,)),
            dma((n_gy - 1,)),
            dma((n_gy - 1,)),
            dma((n_gx - 1,)),
            dma((n_gx - 1,)),
        ],
        compiler_params=pltpu.CompilerParams(
            collective_id=0, has_side_effects=True, vmem_limit_bytes=56 * 1024 * 1024
        ),
        name="window",
    )(
        water_depth,
        momentum_x,
        momentum_y,
        wet_mask,
        damage_class,
        damage_rates,
        dam_cell.reshape(1, dam_count),
        releases.T,
    )
    return final_depth, adjoint, grad.T


def solution(mesh):
    n_gx, n_gy = mesh.shape["gx"], mesh.shape["gy"]
    grid = P("gx", "gy")
    return jax.shard_map(
        functools.partial(on_device, n_gx, n_gy),
        mesh=mesh,
        in_specs=(grid,) * 5 + (P(),) * 3,
        out_specs=(grid, grid, P()),
        check_vma=False,
    )
```

```python
import functools

import jax
import jax.numpy as jnp
from jax import lax
from jax.experimental import pallas as pl
from jax.experimental.pallas import tpu as pltpu
from jax.sharding import PartitionSpec as P

GRAVITY = 9.81
TIME_RATIO = 0.05
INFLOW_GAIN = 0.25
HALO = 4
LANES = 128
TOP = 8
OWN = TOP + HALO
G_STATIC, G_FIRST, G_LAST, G_BACK_LAST, G_BACK_FIRST = 1, 1, 1, 1, 1
MESH = pl.DeviceIdType.MESH


def sweep(body, first, last, group):
    whole = (last - first) // group

    def run(i, carry):
        base = pl.multiple_of(i * (8 * group), 8)
        for j in range(group):
            body(base + 8 * (first + j))
        return carry

    lax.fori_loop(0, whole, run, 0)
    for chunk in range(first + whole * group, last):
        body(8 * chunk)


def pipeline(stages, first, last, group=1):
    depth = len(stages)

    def step(at, index=None):
        for k in reversed(range(depth)):
            if index is None or first <= index - k < last:
                stages[k](at - 8 * k)

    for index in range(first, first + depth - 1):
        step(8 * index, index)
    begin = first + depth - 1
    whole = (last - begin) // group

    def run(i, carry):
        base = pl.multiple_of(i * (8 * group), 8)
        for j in range(group):
            step(base + 8 * (begin + j))
        return carry

    lax.fori_loop(0, whole, run, 0)
    for index in range(begin + whole * group, last + depth - 1):
        step(8 * index, index)


def three_parts(values):
    parts = []
    for _ in range(3):
        part = values.astype(jnp.bfloat16)
        values = values - part.astype(jnp.float32)
        parts.append(part)
    return parts


def halved_on_tie(value, picks, ties):
    return jnp.where(picks, value, jnp.where(ties, 0.5 * value, 0.0))


def split_speed_grads(lm_l, lm_r, lp_l, lp_r, coefs, d_term, k_term):
    _, _, _, slow, fast, e_slow, e_fast = coefs
    g_slow = e_slow * (fast * k_term - d_term)
    g_fast = e_fast * (d_term - slow * k_term)
    slow_l = halved_on_tie(g_slow, lm_l < lm_r, lm_l == lm_r)
    fast_l = halved_on_tie(g_fast, lp_l > lp_r, lp_l == lp_r)
    return fast_l, slow_l, g_fast - fast_l, g_slow - slow_l


def kernel(
    n_gx,
    n_gy,
    total_cols,
    classes,
    depth_in,
    mx_in,
    my_in,
    wet_in,
    class_in,
    rates_in,
    dams_in,
    releases_in,
    depth_out,
    adjoint_out,
    grad_out,
    raw_d,
    raw_x,
    raw_y,
    raw_wet,
    raw_cls,
    first,
    second,
    statics,
    faces,
    inflow,
    adj,
    last_h,
    row_flux,
    col_flux,
    col_hot,
    pack_cols,
    send_rows,
    recv_rows,
    send_cols,
    recv_cols,
    recv_corner,
    gpart,
    gsum,
    recv_gy,
    recv_gx,
    rates,
    dams,
    releases,
    small_sem,
    know_sem,
    in_sem,
    edge_send,
    edge_recv,
    gy_send,
    gy_recv,
    gx_send,
    gx_recv,
):
    rows, cols = depth_in.shape
    tiles = cols // LANES
    wide = tiles + 1
    span = rows + 2 * HALO
    chunks = span // 8
    ix, iy = lax.axis_index("gx"), lax.axis_index("gy")
    lane = lax.broadcasted_iota(jnp.int32, (8, LANES), 1)

    has_up, has_down = ix > 0, ix < n_gx - 1
    has_left, has_right = iy > 0, iy < n_gy - 1

    barrier = pltpu.get_barrier_semaphore()
    for step in range(1, n_gy):
        pl.semaphore_signal(
            barrier, inc=1, device_id=(ix, lax.rem(iy + step, n_gy)), device_id_type=MESH
        )
    sides = (
        (has_up, -1, 0),
        (has_down, 1, 0),
        (has_left, 0, -1),
        (has_right, 0, 1),
        (has_up & has_left, -1, -1),
        (has_up & has_right, -1, 1),
        (has_down & has_left, 1, -1),
        (has_down & has_right, 1, 1),
    )
    corners = 0
    for exists, dx, dy in sides[:2] + sides[4:]:
        corners = corners + exists.astype(jnp.int32)

        @pl.when(exists)
        def _(dx=dx, dy=dy):
            pl.semaphore_signal(barrier, inc=1, device_id=(ix + dx, iy + dy), device_id_type=MESH)

    small = [
        pltpu.make_async_copy(source, target, small_sem.at[index])
        for index, (source, target) in enumerate(
            ((rates_in, rates), (dams_in, dams), (releases_in, releases))
        )
    ]
    for copy in small[:1]:
        copy.start()
    loads = []
    for c in (0, tiles - 1, *range(1, tiles - 1)):
        for index, (source, target) in enumerate(
            ((wet_in, raw_wet), (class_in, raw_cls), (depth_in, raw_d), (mx_in, raw_x), (my_in, raw_y))
        ):
            copy = pltpu.make_async_copy(
                source.at[:, pl.ds(c * LANES, LANES)], target.at[c], in_sem.at[index, c]
            )
            copy.start()
            loads.append(copy)
    for copy in small[1:]:
        copy.start()

    for copy in loads:
        copy.wait()
    small[0].wait()

    rate = [rates[k] for k in range(classes)]

    def coded_chunk(c, start, size=8):
        at = (c, pl.ds(start, size), slice(None))
        wet = raw_wet[at] > 0
        cls = raw_cls[at]
        weight = jnp.full(cls.shape, rate[0])
        for k in range(1, classes):
            weight = jnp.where(cls == k, rate[k], weight)
        return (
            jnp.where(wet, raw_d[at], -1.0),
            raw_x[at],
            raw_y[at],
            jnp.where(wet, weight, 0.0),
        )

    for c in range(tiles):
        for side, start, pick in ((0, 0, 0), (1, rows - 8, 4)):
            four = coded_chunk(c, start)
            for k in range(4):
                send_rows[side, c, 4 * k : 4 * k + 4, :] = four[k][pick : pick + 4]

    def pack_body(i, carry):
        start = pl.multiple_of(i * 8, 8)
        left = coded_chunk(0, start)
        right = coded_chunk(tiles - 1, start)
        packed = jnp.zeros((8, LANES), jnp.float32)
        for k in range(4):
            mine = (lane >= 4 * k) & (lane < 4 * k + 4)
            packed = jnp.where(mine, pltpu.roll(left[k], 4 * k, 1) if k else left[k], packed)
            mine = (lane >= 16 + 4 * k) & (lane < 20 + 4 * k)
            packed = jnp.where(mine, pltpu.roll(right[k], 20 + 4 * k, 1), packed)
        pack_cols[pl.ds(start, 8), :] = packed
        return carry

    lax.fori_loop(0, rows // 8, pack_body, 0, unroll=2)
    turned = jnp.transpose(pack_cols[...])
    send_cols[0] = turned[0:16]
    send_cols[1] = turned[16:32]

    pl.semaphore_wait(barrier, (n_gy - 1) + corners)

    rounds = max(n_gx - 2, 0).bit_length()

    def reach(level):
        return (ix >= 2**level, -(2**level)), (ix + 2**level < n_gx, 2**level)

    def tell(level):
        for exists, offset in reach(level):

            @pl.when(exists)
            def _(offset=offset):
                pl.semaphore_signal(
                    know_sem.at[level], inc=1, device_id=(ix + offset, iy), device_id_type=MESH
                )

    def learn(level):
        pl.semaphore_wait(
            know_sem.at[level], sum(exists.astype(jnp.int32) for exists, _ in reach(level))
        )

    def edge_copy(index):
        _, dx, dy = sides[index]
        opposite = (1, 0, 3, 2, 7, 6, 5, 4)[index]
        if index < 2:
            source, target = send_rows.at[index], recv_rows.at[opposite]
        elif index < 4:
            source, target = send_cols.at[index - 2], recv_cols.at[opposite - 2]
        else:
            first = 0 if index < 6 else rows - 8
            source, target = pack_cols.at[pl.ds(first, 8), :], recv_corner.at[opposite - 4]
        return pltpu.make_async_remote_copy(
            src_ref=source,
            dst_ref=target,
            send_sem=edge_send.at[index],
            recv_sem=edge_recv.at[opposite],
            device_id=(ix + dx, iy + dy),
            device_id_type=MESH,
        )

    for index in (4, 5, 6, 7, 0, 1, 2, 3):

        @pl.when(sides[index][0])
        def _(index=index):
            edge_copy(index).start()

    if rounds > 0:
        tell(0)

    H, MX, MY, LMX, LPX, LMY, LPY, PX, RX, PY, RY = range(11)
    IH = 11
    QX, QY, TT, AX, AY, UV, WX, WY, BX, BY = range(11, 21)
    NEXT = 21
    WET, WGT, FMX, FMY = range(4)
    ALPHA, BETA, GAMMA, SLOW, FAST, ESLOW, EFAST = range(7)

    def put_start(c, at_rows, size, four):
        wet = four[0] > 0.0
        at = (c, pl.ds(at_rows, size), slice(None))
        first[(H,) + at] = jnp.where(wet, four[0], 1.0)
        first[(MX,) + at] = jnp.where(wet, four[1], 0.0)
        first[(MY,) + at] = jnp.where(wet, four[2], 0.0)
        statics[(WGT,) + at] = jnp.where(wet, four[3], 0.0)
        statics[(WET,) + at] = jnp.where(wet, 1.0, 0.0)

    def own_body(i, carry):
        start = pl.multiple_of(i * 8, 8)
        for c in range(tiles):
            put_start(c, start + OWN, 8, coded_chunk(c, start))
        return carry

    lax.fori_loop(0, rows // 8, own_body, 0)

    for copy in small[1:]:
        copy.wait()
    cell = dams[...]
    if total_cols & (total_cols - 1) == 0:
        dam_row = lax.shift_right_logical(cell, total_cols.bit_length() - 1)
    else:
        dam_row = lax.div(cell, total_cols)
    dam_col = cell - dam_row * total_cols
    dam_count = cell.shape[1]
    local_row = dam_row - ix * rows
    local_col = dam_col - iy * cols
    amounts = INFLOW_GAIN * releases[...]
    thrice = lambda values: jnp.concatenate([values] * 3, axis=1)
    amounts = jnp.concatenate(
        [part.astype(jnp.float32) for part in three_parts(amounts)], axis=1
    )
    wide_row = lax.broadcasted_iota(jnp.int32, (span, 3 * dam_count), 0) - HALO
    row_hot = wide_row == thrice(local_row)
    gain_rows = jnp.concatenate(
        [jnp.where(row_hot, amounts[s : s + 1], 0.0) for s in range(2)], axis=0
    ).astype(jnp.bfloat16)
    position = lax.broadcasted_iota(jnp.int32, (LANES, 3 * dam_count), 0)
    col_thrice = thrice(local_col)
    hots = []
    for c in range(wide):
        if c < tiles:
            column = position + c * LANES
        else:
            column = jnp.where(
                position < HALO,
                position + cols,
                jnp.where(position >= LANES - HALO, position - LANES, -2 * LANES),
            )
        hot = (column == col_thrice).astype(jnp.float32).astype(jnp.bfloat16)
        if c < tiles:
            col_hot[c * LANES : (c + 1) * LANES, :] = hot[:, :dam_count]
        hots.append(hot)
    poured = lax.dot_general(
        gain_rows, jnp.concatenate(hots, axis=0), (((1,), (1,)), ((), ())),
        preferred_element_type=jnp.float32,
    )
    for s in range(2):
        for c in range(wide):
            inflow[s, c, TOP : TOP + span, :] = poured[
                s * span : (s + 1) * span, c * LANES : (c + 1) * LANES
            ]

    for index in range(8):

        @pl.when(sides[index][0])
        def _(index=index):
            copy = edge_copy(index)
            copy.wait_send()
            opposite = (1, 0, 3, 2, 7, 6, 5, 4)[index]
            if index < 2:
                target = recv_rows.at[index]
            elif index < 4:
                target = recv_cols.at[index - 2]
            else:
                target = recv_corner.at[index - 4]
            pltpu.make_async_copy(target, target, edge_recv.at[index]).wait()

    if rounds > 0:
        learn(0)
        if rounds > 1:
            tell(1)

    for c in range(tiles):
        for side, exists, at_rows in ((0, has_up, TOP), (1, has_down, OWN + rows)):
            four = [recv_rows[side, c, 4 * k : 4 * k + 4, :] for k in range(4)]
            four[0] = jnp.where(exists, four[0], -1.0)
            put_start(c, at_rows, 4, four)

    halves = jnp.concatenate(
        [recv_cols[0], recv_cols[1], jnp.zeros((LANES - 32, rows), jnp.float32)], axis=0
    )
    pack_cols[...] = jnp.transpose(halves)

    def rim_tile(left_part, right_part, k, left_at, right_at, from_left, from_right):
        fill = -1.0 if k == 0 else 0.0
        on_right = (lane < HALO) & from_right
        on_left = (lane >= LANES - HALO) & from_left
        shift_r = (LANES - right_at - 4 * k) % LANES
        shift_l = (LANES - HALO - left_at - 4 * k) % LANES
        right_val = pltpu.roll(right_part, shift_r, 1) if shift_r else right_part
        left_val = pltpu.roll(left_part, shift_l, 1) if shift_l else left_part
        return jnp.where(on_right, right_val, jnp.where(on_left, left_val, fill))

    def rim_body(i, carry):
        start = pl.multiple_of(i * 8, 8)
        part = pack_cols[pl.ds(start, 8), :]
        four = [rim_tile(part, part, k, 0, 16, has_left, has_right) for k in range(4)]
        put_start(tiles, start + OWN, 8, four)
        return carry

    lax.fori_loop(0, rows // 8, rim_body, 0, unroll=2)
    for left_slot, right_slot, exists, at_rows, pick in (
        (0, 1, has_up, TOP, 4),
        (2, 3, has_down, OWN + rows, 0),
    ):
        four = [
            rim_tile(
                recv_corner[left_slot],
                recv_corner[right_slot],
                k,
                16,
                0,
                has_left & exists,
                has_right & exists,
            )[pick : pick + 4]
            for k in range(4)
        ]
        put_start(tiles, at_rows, 4, four)

    def next_lanes(values):
        turned_all = [pltpu.roll(value, LANES - 1, 1) for value in values]
        return [
            jnp.where(lane == LANES - 1, turned_all[(c + 1) % wide], turned_all[c])
            for c in range(wide)
        ]

    def last_lanes(values):
        turned_all = [pltpu.roll(value, 1, 1) for value in values]
        return [
            jnp.where(lane == 0, turned_all[(c - 1) % wide], turned_all[c]) for c in range(wide)
        ]

    def put_next(target, offset, here, columns):
        for k, values in columns.items():
            for c, value in enumerate(next_lanes(values)):
                target[offset + k, c, here, :] = value

    FIRST_NEXT = (H, MX, MY, LMY, LPY, QY, TT, AY, UV, PY, RY)
    SECOND_NEXT = (H, MY, LMY, LPY, PY, RY, IH)
    SECOND_AT = 12

    def base_prims(h, mx, my, ih):
        ux, uy = mx * ih, my * ih
        squared = GRAVITY * h
        cc = squared * lax.rsqrt(squared)
        half = 0.5 * cc
        out = {H: h, MX: mx, MY: my, LMX: ux - cc, LPX: ux + cc, LMY: uy - cc, LPY: uy + cc}
        half_i, ux_i, uy_i = half * ih, ux * ih, uy * ih
        out |= {PX: half_i - ux_i, RX: half_i + ux_i, PY: half_i - uy_i, RY: half_i + uy_i}
        return out, ux, uy, squared, cc, half

    def static_shift(row):
        here = pl.ds(row + TOP, 8)
        wets = [statics[WET, c, here, :] for c in range(wide)]
        for c, (right, left) in enumerate(zip(next_lanes(wets), last_lanes(wets))):
            col_flux[0, c, here, :] = right
            col_flux[1, c, here, :] = left
        put_next(
            first, NEXT, here,
            {j: [first[k, c, here, :] for c in range(wide)] for j, k in enumerate((H, MX, MY))},
        )

    def static_body(row):
        start = row + TOP
        here = pl.ds(start, 8)
        for c in range(wide):
            wet = statics[WET, c, here, :]
            above = statics[WET, c, pl.ds(start - 1, 8), :]
            below = statics[WET, c, pl.ds(start + 1, 8), :]
            right, left = col_flux[0, c, here, :], col_flux[1, c, here, :]
            scale = TIME_RATIO * wet
            statics[FMX, c, here, :] = scale * below
            statics[FMY, c, here, :] = scale * right
            h, mx, my = (first[k, c, here, :] for k in (H, MX, MY))
            out, ux, uy, squared, cc, half = base_prims(h, mx, my, 1.0 / h)
            pressure = 0.5 * squared * h
            out[QX], out[QY], out[TT] = mx * ux + pressure, my * uy + pressure, mx * uy
            out[AX], out[AY], out[UV] = squared - ux * ux, squared - uy * uy, ux * uy
            for lower, upper, u, n, q, a, wall, back in (
                (above, below, ux, mx, QX, AX, WX, BX),
                (left, right, uy, my, QY, AY, WY, BY),
            ):
                single = scale * (lower - upper)
                both = scale * (2.0 - (lower + upper))
                size = jnp.abs(u)
                out[wall] = single * out[q] + both * ((size + cc) * n)
                out[back] = single * out[a] + both * (u * (half - size))
            for k, value in out.items():
                if k not in (H, MX, MY):
                    first[k, c, here, :] = value
            h, mx, my = (first[NEXT + k, c, here, :] for k in range(3))
            out, ux, uy, squared, cc, half = base_prims(h, mx, my, 1.0 / h)
            out[QY], out[TT] = my * uy + 0.5 * squared * h, mx * uy
            out[AY], out[UV] = squared - uy * uy, ux * uy
            for j, k in enumerate(FIRST_NEXT):
                if j >= 3:
                    first[NEXT + j, c, here, :] = out[k]

    pipeline((static_shift, static_body), 0, chunks, G_STATIC)

    def reader(source, keys, offset):
        def at(k, c, rows_at):
            return source[k, c, rows_at, :]

        def right(k, c, rows_at):
            return source[offset + keys.index(k), c, rows_at, :]

        return at, right

    f_at, f_right = reader(first, FIRST_NEXT, NEXT)
    s_at, s_right = reader(second, SECOND_NEXT, SECOND_AT)

    def face(step, dim, c, here, lm_l, lm_r, lp_l, lp_r):
        low, high = jnp.minimum(lm_l, lm_r), jnp.maximum(lp_l, lp_r)
        slow, fast = jnp.minimum(low, 0.0), jnp.maximum(high, 0.0)
        inverse = 1.0 / (fast - slow)
        masked = statics[FMX + dim, c, here, :] * inverse
        alpha, beta = fast * masked, slow * masked
        gamma = slow * alpha
        e_slow = halved_on_tie(alpha * inverse, low < 0.0, low == 0.0)
        e_fast = halved_on_tie(beta * inverse, high > 0.0, high == 0.0)
        for k, value in enumerate((alpha, beta, gamma, slow, fast, e_slow, e_fast)):
            faces[step, dim, k, c, here, :] = value
        return alpha, beta, gamma

    def coefs_of(step, dim, c, here):
        return [faces[step, dim, k, c, here, :] for k in range(7)]

    def crossing(coefs, flux_l, flux_r, held_l, held_r):
        alpha, beta, gamma = coefs
        return alpha * flux_l - beta * flux_r + gamma * (held_r - held_l)

    def net_of(k, here):
        values = [col_flux[k, c, here, :] for c in range(wide)]
        return [mine - entering for mine, entering in zip(values, last_lanes(values))]

    def first_cols(row):
        here = pl.ds(row + TOP, 8)
        for c in range(wide):
            coefs = face(
                0, 1, c, here, f_at(LMY, c, here), f_right(LMY, c, here),
                f_at(LPY, c, here), f_right(LPY, c, here),
            )
            for k, (flux, held) in enumerate(((MY, H), (TT, MX), (QY, MY))):
                col_flux[k, c, here, :] = crossing(
                    coefs, f_at(flux, c, here), f_right(flux, c, here),
                    f_at(held, c, here), f_right(held, c, here),
                )

    def first_cells(row):
        start = row + TOP
        here, after, before = pl.ds(start, 8), pl.ds(start + 1, 8), pl.ds(start - 1, 8)
        net = [net_of(k, here) for k in range(3)]
        for c in range(wide):
            coefs = face(
                0, 0, c, here, f_at(LMX, c, here), f_at(LMX, c, after),
                f_at(LPX, c, here), f_at(LPX, c, after),
            )
            new = []
            for k, (flux, held) in enumerate(((MX, H), (QX, MX), (TT, MY))):
                value = crossing(
                    coefs, f_at(flux, c, here), f_at(flux, c, after),
                    f_at(held, c, here), f_at(held, c, after),
                )
                row_flux[k, c, here, :] = value
                change = value - row_flux[k, c, before, :] + net[k][c]
                if k > 0:
                    change = change + f_at((None, WX, WY)[k], c, here)
                new.append(f_at((H, MX, MY)[k], c, here) - change)
            h = new[0] + inflow[0, c, here, :]
            ih = 1.0 / h
            out = base_prims(h, new[1], new[2], ih)[0]
            out[IH] = ih
            for k, value in out.items():
                second[k, c, here, :] = value

    def first_shift(row):
        here = pl.ds(row + TOP, 8)
        heights = next_lanes([second[H, c, here, :] for c in range(wide)])
        flows = next_lanes([second[MY, c, here, :] for c in range(wide)])
        for c, (h, n) in enumerate(zip(heights, flows)):
            ih = 1.0 / h
            out = base_prims(h, n, n, ih)[0]
            out[IH] = ih
            for j, k in enumerate(SECOND_NEXT):
                second[SECOND_AT + j, c, here, :] = out[k]

    TERM, ADJ, ZX, ZY, TERM_R, ADJ_R, ZX_R, ZY_R = range(8)

    def last_cols(row):
        here = pl.ds(row + TOP, 8)
        for c in range(wide):
            coefs = face(
                1, 1, c, here, s_at(LMY, c, here), s_right(LMY, c, here),
                s_at(LPY, c, here), s_right(LPY, c, here),
            )
            col_flux[0, c, here, :] = crossing(
                coefs, s_at(MY, c, here), s_right(MY, c, here),
                s_at(H, c, here), s_right(H, c, here),
            )

    def last_cells(row):
        start = row + TOP
        here, after, before = pl.ds(start, 8), pl.ds(start + 1, 8), pl.ds(start - 1, 8)
        net = net_of(0, here)
        for c in range(wide):
            coefs = face(
                1, 0, c, here, s_at(LMX, c, here), s_at(LMX, c, after),
                s_at(LPX, c, here), s_at(LPX, c, after),
            )
            value = crossing(
                coefs, s_at(MX, c, here), s_at(MX, c, after),
                s_at(H, c, here), s_at(H, c, after),
            )
            row_flux[0, c, here, :] = value
            change = value - row_flux[0, c, before, :] + net[c]
            h = s_at(H, c, here) - change + inflow[1, c, here, :]
            last_h[c, here, :] = h
            adj[TERM, c, here, :] = statics[WGT, c, here, :] * h

    def adj_shift(*planes):
        def shift(row):
            here = pl.ds(row + TOP, 8)
            for k in planes:
                put_next(adj, TERM_R + k, here, {0: [adj[k, c, here, :] for c in range(wide)]})

        return shift

    pipeline((first_cols, first_cells, first_shift), 0, chunks, G_FIRST)
    if rounds > 1:
        learn(1)
        if rounds > 2:
            tell(2)
    pipeline((last_cols, last_cells, adj_shift(TERM)), 0, chunks, G_LAST)

    def depth_body(i, carry):
        start = pl.multiple_of(i * 8, 8)
        for c in range(tiles):
            own = pl.ds(start + OWN, 8)
            depth_out[pl.ds(start, 8), c * LANES : (c + 1) * LANES] = jnp.where(
                statics[WET, c, own, :] > 0.0, last_h[c, own, :], raw_d[c, pl.ds(start, 8), :]
            )
        return carry

    lax.fori_loop(0, rows // 8, depth_body, 0)
    def last_face(coefs, lm, lp, h, n, z, p, r, ih):
        alpha, beta, gamma = coefs[:3]
        gh = z[1] - z[0]
        fast_l, slow_l, fast_r, slow_r = split_speed_grads(
            *lm, *lp, coefs, gh * (n[1] - n[0]), gh * (h[1] - h[0])
        )
        jump = gamma * gh
        return (
            fast_l * p[0] - slow_l * r[0] - jump,
            alpha * gh + (fast_l + slow_l) * ih[0],
        ), (
            fast_r * p[1] - slow_r * r[1] + jump,
            (fast_r + slow_r) * ih[1] - beta * gh,
        )

    def back_cols(row):
        here = pl.ds(row + TOP, 8)
        for c in range(wide):

            def pair(k):
                return s_at(k, c, here), s_right(k, c, here)

            left, right = last_face(
                coefs_of(1, 1, c, here), pair(LMY), pair(LPY), pair(H), pair(MY),
                (adj[TERM, c, here, :], adj[TERM_R, c, here, :]), pair(PY), pair(RY), pair(IH),
            )
            for k in range(2):
                col_flux[k, c, here, :] = left[k]
                col_flux[2 + k, c, here, :] = right[k]

    def back_cells(row):
        start = row + TOP
        here, after, before = pl.ds(start, 8), pl.ds(start + 1, 8), pl.ds(start - 1, 8)
        entering = [
            last_lanes([col_flux[2 + k, c, here, :] for c in range(wide)]) for k in range(2)
        ]
        for c in range(wide):

            def pair(k):
                return s_at(k, c, here), s_at(k, c, after)

            left, right = last_face(
                coefs_of(1, 0, c, here), pair(LMX), pair(LPX), pair(H), pair(MX),
                (adj[TERM, c, here, :], adj[TERM, c, after, :]), pair(PX), pair(RX), pair(IH),
            )
            in_x = []
            for k in range(2):
                row_flux[k, c, here, :] = right[k]
                in_x.append(left[k] + row_flux[k, c, before, :])
            in_y = [col_flux[k, c, here, :] + entering[k][c] for k in range(2)]
            adj[ADJ, c, here, :] = adj[TERM, c, here, :] + (in_x[0] + in_y[0])
            adj[ZX, c, here, :] = in_x[1]
            adj[ZY, c, here, :] = in_y[1]

    pipeline((back_cols, back_cells, adj_shift(ADJ, ZX, ZY)), 0, chunks, G_BACK_LAST)

    own_hot = lax.broadcasted_iota(jnp.int32, (rows, dam_count), 0) == local_row
    gpart[...] = jnp.zeros(gpart.shape, jnp.float32)
    stacked = []
    for plane in (ADJ, TERM):
        parts = [three_parts(adj[plane, c, OWN : OWN + rows, :]) for c in range(tiles)]
        stacked.append(
            jnp.concatenate([parts[c][k] for k in range(3) for c in range(tiles)], axis=1)
        )
    picked = lax.dot_general(
        jnp.concatenate(stacked, axis=0), jnp.concatenate([col_hot[...]] * 3, axis=0),
        (((1,), (0,)), ((), ())), preferred_element_type=jnp.float32,
    )
    for s in range(2):
        gpart[s : s + 1, 0:dam_count] = INFLOW_GAIN * jnp.sum(
            jnp.where(own_hot, picked[s * rows : (s + 1) * rows], 0.0), axis=0, keepdims=True
        )

    def gy_copy(step):
        return pltpu.make_async_remote_copy(
            src_ref=gpart,
            dst_ref=recv_gy.at[step - 1],
            send_sem=gy_send.at[step - 1],
            recv_sem=gy_recv.at[step - 1],
            device_id=(ix, lax.rem(iy + step, n_gy)),
            device_id_type=MESH,
        )

    def gx_copy(step):
        return pltpu.make_async_remote_copy(
            src_ref=gsum,
            dst_ref=recv_gx.at[step - 1],
            send_sem=gx_send.at[step - 1],
            recv_sem=gx_recv.at[step - 1],
            device_id=(lax.rem(ix + step, n_gx), iy),
            device_id_type=MESH,
        )

    for step in range(1, n_gy):
        gy_copy(step).start()

    def first_face(coefs, lm, lp, h, n, t, q, v, zh, zn, zt, a, uv, p, r):
        alpha, beta, gamma = coefs[:3]
        gh, gn, gt = zh[1] - zh[0], zn[1] - zn[0], zt[1] - zt[0]
        dn = n[1] - n[0]
        fast_l, slow_l, fast_r, slow_r = split_speed_grads(
            *lm, *lp, coefs,
            gh * dn + gn * (q[1] - q[0]) + gt * (v[1] - v[0]),
            gh * (h[1] - h[0]) + gn * dn + gt * (t[1] - t[0]),
        )
        jump = gamma * gh
        return (
            alpha * (gn * a[0] - gt * uv[0]) + (fast_l * p[0] - slow_l * r[0]) - jump,
            (fast_r * p[1] - slow_r * r[1]) - beta * (gn * a[1] - gt * uv[1]) + jump,
        )

    def first_row_face(c, start):
        here, after = pl.ds(start, 8), pl.ds(start + 1, 8)

        def pair(k):
            return f_at(k, c, here), f_at(k, c, after)

        def z_pair(k):
            return adj[k, c, here, :], adj[k, c, after, :]

        return first_face(
            coefs_of(0, 0, c, here), pair(LMX), pair(LPX), pair(H), pair(MX), pair(MY), pair(QX),
            pair(TT), z_pair(ADJ), z_pair(ZX), z_pair(ZY), pair(AX), pair(UV), pair(PX), pair(RX),
        )

    for c in range(tiles):
        row_flux[0, c, pl.ds(OWN - 8, 8), :] = first_row_face(c, OWN - 8)[1]

    def backward_first(row):
        start = row + OWN
        here, before = pl.ds(start, 8), pl.ds(start - 1, 8)

        def col_face(c):
            def pair(k):
                return f_at(k, c, here), f_right(k, c, here)

            def z_pair(k):
                return adj[k, c, here, :], adj[k + TERM_R - TERM, c, here, :]

            return first_face(
                coefs_of(0, 1, c, here), pair(LMY), pair(LPY), pair(H), pair(MY), pair(MX),
                pair(QY), pair(TT), z_pair(ADJ), z_pair(ZY), z_pair(ZX), pair(AY), pair(UV),
                pair(PY), pair(RY),
            )

        turned = pltpu.roll(col_face(wide - 1)[1], 1, 1)
        for c in range(tiles):
            left, right = first_row_face(c, start)
            row_flux[0, c, here, :] = right
            left_y, right_y = col_face(c)
            turned, last = pltpu.roll(right_y, 1, 1), turned
            entering = jnp.where(lane == 0, last, turned)
            across = left + row_flux[0, c, before, :] + (left_y + entering)
            walls = adj[ZX, c, here, :] * f_at(BX, c, here) + adj[ZY, c, here, :] * f_at(BY, c, here)
            adjoint_out[pl.ds(row, 8), c * LANES : (c + 1) * LANES] = (
                adj[ADJ, c, here, :] + across - walls
            )

    half = rows // 16 // G_BACK_FIRST * G_BACK_FIRST
    sweep(backward_first, 0, half, G_BACK_FIRST)

    for step in range(1, n_gy):
        gy_copy(step).wait()
    total = gpart[...]
    for step in range(1, n_gy):
        total = total + recv_gy[step - 1]
    gsum[...] = total
    for level in range(2, rounds):
        learn(level)
        if level + 1 < rounds:
            tell(level + 1)
    for step in range(1, n_gx):
        gx_copy(step).start()

    sweep(backward_first, half, rows // 8, G_BACK_FIRST)
    for step in range(1, n_gx):
        gx_copy(step).wait()
    for step in range(1, n_gx):
        total = total + recv_gx[step - 1]
    grad_out[...] = total[0:2, 0:dam_count]


def on_device(
    n_gx,
    n_gy,
    water_depth,
    momentum_x,
    momentum_y,
    wet_mask,
    damage_class,
    damage_rates,
    dam_cell,
    releases,
):
    rows, cols = water_depth.shape
    tiles = cols // LANES
    wide = tiles + 1
    high = rows + 2 * HALO + 2 * TOP
    dam_count = dam_cell.shape[0]
    f32 = jnp.float32
    plane = (wide, high, LANES)
    own = (tiles, rows, LANES)
    anywhere = pl.BlockSpec(memory_space=pl.ANY)
    vmem = pl.BlockSpec(memory_space=pltpu.VMEM)
    dma = pltpu.SemaphoreType.DMA
    final_depth, adjoint, grad = pl.pallas_call(
        functools.partial(kernel, n_gx, n_gy, cols * n_gy, damage_rates.shape[0]),
        out_shape=(
            pltpu.VMEM((rows, cols), f32),
            pltpu.VMEM((rows, cols), f32),
            pltpu.VMEM(releases.shape[::-1], f32),
        ),
        in_specs=[anywhere] * 8,
        out_specs=(vmem, vmem, vmem),
        scratch_shapes=[
            pltpu.VMEM(own, f32),
            pltpu.VMEM(own, f32),
            pltpu.VMEM(own, f32),
            pltpu.VMEM(own, jnp.int32),
            pltpu.VMEM(own, jnp.int32),
            pltpu.VMEM((32,) + plane, f32),
            pltpu.VMEM((19,) + plane, f32),
            pltpu.VMEM((4,) + plane, f32),
            pltpu.VMEM((2, 2, 7) + plane, f32),
            pltpu.VMEM((2,) + plane, f32),
            pltpu.VMEM((8,) + plane, f32),
            pltpu.VMEM(plane, f32),
            pltpu.VMEM((3,) + plane, f32),
            pltpu.VMEM((4,) + plane, f32),
            pltpu.VMEM((cols, dam_count), jnp.bfloat16),
            pltpu.VMEM((rows, LANES), f32),
            pltpu.VMEM((2, tiles, 16, LANES), f32),
            pltpu.VMEM((2, tiles, 16, LANES), f32),
            pltpu.VMEM((2, 16, rows), f32),
            pltpu.VMEM((2, 16, rows), f32),
            pltpu.VMEM((4, 8, LANES), f32),
            pltpu.VMEM((8, LANES), f32),
            pltpu.VMEM((8, LANES), f32),
            pltpu.VMEM((n_gy - 1, 8, LANES), f32),
            pltpu.VMEM((n_gx - 1, 8, LANES), f32),
            pltpu.SMEM(damage_rates.shape, f32),
            pltpu.VMEM((1, dam_count), jnp.int32),
            pltpu.VMEM(releases.shape[::-1], f32),
            dma((3,)),
            pltpu.SemaphoreType.REGULAR((max(n_gx - 2, 1).bit_length(),)),
            dma((5, tiles)),
            dma((8,)),
            dma((8,)),
            dma((n_gy - 1,)),
            dma((n_gy - 1,)),
            dma((n_gx - 1,)),
            dma((n_gx - 1,)),
        ],
        compiler_params=pltpu.CompilerParams(
            collective_id=0, has_side_effects=True, vmem_limit_bytes=56 * 1024 * 1024
        ),
        name="window",
    )(
        water_depth,
        momentum_x,
        momentum_y,
        wet_mask,
        damage_class,
        damage_rates,
        dam_cell.reshape(1, dam_count),
        releases.T,
    )
    return final_depth, adjoint, grad.T


def solution(mesh):
    n_gx, n_gy = mesh.shape["gx"], mesh.shape["gy"]
    grid = P("gx", "gy")
    return jax.shard_map(
        functools.partial(on_device, n_gx, n_gy),
        mesh=mesh,
        in_specs=(grid,) * 5 + (P(),) * 3,
        out_specs=(grid, grid, P()),
        check_vma=False,
    )
```

```python
import functools

import jax
import jax.numpy as jnp
from jax import lax
from jax.experimental import pallas as pl
from jax.experimental.pallas import tpu as pltpu
from jax.sharding import PartitionSpec as P

GRAVITY = 9.81
TIME_RATIO = 0.05
INFLOW_GAIN = 0.25
HALO = 4
LANES = 128
TOP = 8
OWN = TOP + HALO
G_STATIC, G_FIRST, G_LAST, G_BACK_LAST, G_BACK_FIRST = 3, 3, 5, 3, 1
MESH = pl.DeviceIdType.MESH


def sweep(body, first, last, group):
    whole = (last - first) // group

    def run(i, carry):
        base = pl.multiple_of(i * (8 * group), 8)
        for j in range(group):
            body(base + 8 * (first + j))
        return carry

    lax.fori_loop(0, whole, run, 0)
    for chunk in range(first + whole * group, last):
        body(8 * chunk)


def pipeline(stages, first, last, group=1):
    depth = len(stages)

    def step(at, index=None):
        for k in reversed(range(depth)):
            if index is None or first <= index - k < last:
                stages[k](at - 8 * k)

    for index in range(first, first + depth - 1):
        step(8 * index, index)
    begin = first + depth - 1
    whole = (last - begin) // group

    def run(i, carry):
        base = pl.multiple_of(i * (8 * group), 8)
        for j in range(group):
            step(base + 8 * (begin + j))
        return carry

    lax.fori_loop(0, whole, run, 0)
    for index in range(begin + whole * group, last + depth - 1):
        step(8 * index, index)


def three_parts(values):
    parts = []
    for _ in range(3):
        part = values.astype(jnp.bfloat16)
        values = values - part.astype(jnp.float32)
        parts.append(part)
    return parts


def halved_on_tie(value, picks, ties):
    return jnp.where(picks, value, jnp.where(ties, 0.5 * value, 0.0))


def split_speed_grads(lm_l, lm_r, lp_l, lp_r, coefs, d_term, k_term):
    _, _, _, slow, fast, e_slow, e_fast = coefs
    g_slow = e_slow * (fast * k_term - d_term)
    g_fast = e_fast * (d_term - slow * k_term)
    slow_l = halved_on_tie(g_slow, lm_l < lm_r, lm_l == lm_r)
    fast_l = halved_on_tie(g_fast, lp_l > lp_r, lp_l == lp_r)
    return fast_l, slow_l, g_fast - fast_l, g_slow - slow_l


def kernel(
    n_gx,
    n_gy,
    total_cols,
    classes,
    depth_in,
    mx_in,
    my_in,
    wet_in,
    class_in,
    rates_in,
    dams_in,
    releases_in,
    depth_out,
    adjoint_out,
    grad_out,
    raw_d,
    raw_x,
    raw_y,
    raw_wet,
    raw_cls,
    first,
    second,
    statics,
    faces,
    inflow,
    adj,
    last_h,
    row_flux,
    col_flux,
    col_hot,
    pack_cols,
    send_rows,
    recv_rows,
    send_cols,
    recv_cols,
    recv_corner,
    gpart,
    recv_all,
    rates,
    dams,
    releases,
    small_sem,
    know_sem,
    in_sem,
    edge_send,
    edge_recv,
    grad_send,
    grad_recv,
):
    rows, cols = depth_in.shape
    tiles = cols // LANES
    wide = tiles + 1
    span = rows + 2 * HALO
    chunks = span // 8
    ix, iy = lax.axis_index("gx"), lax.axis_index("gy")
    lane = lax.broadcasted_iota(jnp.int32, (8, LANES), 1)

    has_up, has_down = ix > 0, ix < n_gx - 1
    has_left, has_right = iy > 0, iy < n_gy - 1

    barrier = pltpu.get_barrier_semaphore()
    for step in range(1, n_gy):
        pl.semaphore_signal(
            barrier, inc=1, device_id=(ix, lax.rem(iy + step, n_gy)), device_id_type=MESH
        )
    sides = (
        (has_up, -1, 0),
        (has_down, 1, 0),
        (has_left, 0, -1),
        (has_right, 0, 1),
        (has_up & has_left, -1, -1),
        (has_up & has_right, -1, 1),
        (has_down & has_left, 1, -1),
        (has_down & has_right, 1, 1),
    )
    corners = 0
    for exists, dx, dy in sides[:2] + sides[4:]:
        corners = corners + exists.astype(jnp.int32)

        @pl.when(exists)
        def _(dx=dx, dy=dy):
            pl.semaphore_signal(barrier, inc=1, device_id=(ix + dx, iy + dy), device_id_type=MESH)

    small = [
        pltpu.make_async_copy(source, target, small_sem.at[index])
        for index, (source, target) in enumerate(
            ((rates_in, rates), (dams_in, dams), (releases_in, releases))
        )
    ]
    for copy in small[:1]:
        copy.start()
    loads = []
    for c in (0, tiles - 1, *range(1, tiles - 1)):
        for index, (source, target) in enumerate(
            ((wet_in, raw_wet), (class_in, raw_cls), (depth_in, raw_d), (mx_in, raw_x), (my_in, raw_y))
        ):
            copy = pltpu.make_async_copy(
                source.at[:, pl.ds(c * LANES, LANES)], target.at[c], in_sem.at[index, c]
            )
            copy.start()
            loads.append(copy)
    for copy in small[1:]:
        copy.start()

    for copy in loads:
        copy.wait()
    small[0].wait()

    rate = [rates[k] for k in range(classes)]

    def coded_chunk(c, start, size=8):
        at = (c, pl.ds(start, size), slice(None))
        wet = raw_wet[at] > 0
        cls = raw_cls[at]
        weight = jnp.full(cls.shape, rate[0])
        for k in range(1, classes):
            weight = jnp.where(cls == k, rate[k], weight)
        return (
            jnp.where(wet, raw_d[at], -1.0),
            raw_x[at],
            raw_y[at],
            jnp.where(wet, weight, 0.0),
        )

    for c in range(tiles):
        for side, start, pick in ((0, 0, 0), (1, rows - 8, 4)):
            four = coded_chunk(c, start)
            for k in range(4):
                send_rows[side, c, 4 * k : 4 * k + 4, :] = four[k][pick : pick + 4]

    def pack_body(i, carry):
        start = pl.multiple_of(i * 8, 8)
        left = coded_chunk(0, start)
        right = coded_chunk(tiles - 1, start)
        packed = jnp.zeros((8, LANES), jnp.float32)
        for k in range(4):
            mine = (lane >= 4 * k) & (lane < 4 * k + 4)
            packed = jnp.where(mine, pltpu.roll(left[k], 4 * k, 1) if k else left[k], packed)
            mine = (lane >= 16 + 4 * k) & (lane < 20 + 4 * k)
            packed = jnp.where(mine, pltpu.roll(right[k], 20 + 4 * k, 1), packed)
        pack_cols[pl.ds(start, 8), :] = packed
        return carry

    lax.fori_loop(0, rows // 8, pack_body, 0, unroll=2)
    turned = jnp.transpose(pack_cols[...])
    send_cols[0] = turned[0:16]
    send_cols[1] = turned[16:32]

    pl.semaphore_wait(barrier, (n_gy - 1) + corners)

    rounds = (n_gx - 1).bit_length()

    def reach(level):
        return (ix >= 2**level, -(2**level)), (ix + 2**level < n_gx, 2**level)

    def tell(level):
        for exists, offset in reach(level):

            @pl.when(exists)
            def _(offset=offset):
                pl.semaphore_signal(
                    know_sem.at[level], inc=1, device_id=(ix + offset, iy), device_id_type=MESH
                )

    def learn(level):
        pl.semaphore_wait(
            know_sem.at[level], sum(exists.astype(jnp.int32) for exists, _ in reach(level))
        )

    def edge_copy(index):
        _, dx, dy = sides[index]
        opposite = (1, 0, 3, 2, 7, 6, 5, 4)[index]
        if index < 2:
            source, target = send_rows.at[index], recv_rows.at[opposite]
        elif index < 4:
            source, target = send_cols.at[index - 2], recv_cols.at[opposite - 2]
        else:
            first = 0 if index < 6 else rows - 8
            source, target = pack_cols.at[pl.ds(first, 8), :], recv_corner.at[opposite - 4]
        return pltpu.make_async_remote_copy(
            src_ref=source,
            dst_ref=target,
            send_sem=edge_send.at[index],
            recv_sem=edge_recv.at[opposite],
            device_id=(ix + dx, iy + dy),
            device_id_type=MESH,
        )

    for index in (4, 5, 6, 7, 0, 1, 2, 3):

        @pl.when(sides[index][0])
        def _(index=index):
            edge_copy(index).start()

    if rounds > 0:
        tell(0)

    H, MX, MY, LMX, LPX, LMY, LPY, PX, RX, PY, RY = range(11)
    IH = 11
    QX, QY, TT, AX, AY, UV, WX, WY, BX, BY = range(11, 21)
    NEXT = 21
    WET, WGT, FMX, FMY = range(4)
    ALPHA, BETA, GAMMA, SLOW, FAST, ESLOW, EFAST = range(7)

    def put_start(c, at_rows, size, four):
        wet = four[0] > 0.0
        at = (c, pl.ds(at_rows, size), slice(None))
        first[(H,) + at] = jnp.where(wet, four[0], 1.0)
        first[(MX,) + at] = jnp.where(wet, four[1], 0.0)
        first[(MY,) + at] = jnp.where(wet, four[2], 0.0)
        statics[(WGT,) + at] = jnp.where(wet, four[3], 0.0)
        statics[(WET,) + at] = jnp.where(wet, 1.0, 0.0)

    def own_body(i, carry):
        start = pl.multiple_of(i * 8, 8)
        for c in range(tiles):
            put_start(c, start + OWN, 8, coded_chunk(c, start))
        return carry

    lax.fori_loop(0, rows // 8, own_body, 0)

    for copy in small[1:]:
        copy.wait()
    cell = dams[...]
    if total_cols & (total_cols - 1) == 0:
        dam_row = lax.shift_right_logical(cell, total_cols.bit_length() - 1)
    else:
        dam_row = lax.div(cell, total_cols)
    dam_col = cell - dam_row * total_cols
    dam_count = cell.shape[1]
    local_row = dam_row - ix * rows
    local_col = dam_col - iy * cols
    amounts = INFLOW_GAIN * releases[...]
    thrice = lambda values: jnp.concatenate([values] * 3, axis=1)
    amounts = jnp.concatenate(
        [part.astype(jnp.float32) for part in three_parts(amounts)], axis=1
    )
    wide_row = lax.broadcasted_iota(jnp.int32, (span, 3 * dam_count), 0) - HALO
    row_hot = wide_row == thrice(local_row)
    gain_rows = jnp.concatenate(
        [jnp.where(row_hot, amounts[s : s + 1], 0.0) for s in range(2)], axis=0
    ).astype(jnp.bfloat16)
    position = lax.broadcasted_iota(jnp.int32, (LANES, 3 * dam_count), 0)
    col_thrice = thrice(local_col)
    hots = []
    for c in range(wide):
        if c < tiles:
            column = position + c * LANES
        else:
            column = jnp.where(
                position < HALO,
                position + cols,
                jnp.where(position >= LANES - HALO, position - LANES, -2 * LANES),
            )
        hot = (column == col_thrice).astype(jnp.float32).astype(jnp.bfloat16)
        if c < tiles:
            col_hot[c * LANES : (c + 1) * LANES, :] = hot[:, :dam_count]
        hots.append(hot)
    poured = lax.dot_general(
        gain_rows, jnp.concatenate(hots, axis=0), (((1,), (1,)), ((), ())),
        preferred_element_type=jnp.float32,
    )
    for s in range(2):
        for c in range(wide):
            inflow[s, c, TOP : TOP + span, :] = poured[
                s * span : (s + 1) * span, c * LANES : (c + 1) * LANES
            ]

    for index in range(8):

        @pl.when(sides[index][0])
        def _(index=index):
            copy = edge_copy(index)
            copy.wait_send()
            opposite = (1, 0, 3, 2, 7, 6, 5, 4)[index]
            if index < 2:
                target = recv_rows.at[index]
            elif index < 4:
                target = recv_cols.at[index - 2]
            else:
                target = recv_corner.at[index - 4]
            pltpu.make_async_copy(target, target, edge_recv.at[index]).wait()

    if rounds > 0:
        learn(0)
        if rounds > 1:
            tell(1)

    for c in range(tiles):
        for side, exists, at_rows in ((0, has_up, TOP), (1, has_down, OWN + rows)):
            four = [recv_rows[side, c, 4 * k : 4 * k + 4, :] for k in range(4)]
            four[0] = jnp.where(exists, four[0], -1.0)
            put_start(c, at_rows, 4, four)

    halves = jnp.concatenate(
        [recv_cols[0], recv_cols[1], jnp.zeros((LANES - 32, rows), jnp.float32)], axis=0
    )
    pack_cols[...] = jnp.transpose(halves)

    def rim_tile(left_part, right_part, k, left_at, right_at, from_left, from_right):
        fill = -1.0 if k == 0 else 0.0
        on_right = (lane < HALO) & from_right
        on_left = (lane >= LANES - HALO) & from_left
        shift_r = (LANES - right_at - 4 * k) % LANES
        shift_l = (LANES - HALO - left_at - 4 * k) % LANES
        right_val = pltpu.roll(right_part, shift_r, 1) if shift_r else right_part
        left_val = pltpu.roll(left_part, shift_l, 1) if shift_l else left_part
        return jnp.where(on_right, right_val, jnp.where(on_left, left_val, fill))

    def rim_body(i, carry):
        start = pl.multiple_of(i * 8, 8)
        part = pack_cols[pl.ds(start, 8), :]
        four = [rim_tile(part, part, k, 0, 16, has_left, has_right) for k in range(4)]
        put_start(tiles, start + OWN, 8, four)
        return carry

    lax.fori_loop(0, rows // 8, rim_body, 0, unroll=2)
    for left_slot, right_slot, exists, at_rows, pick in (
        (0, 1, has_up, TOP, 4),
        (2, 3, has_down, OWN + rows, 0),
    ):
        four = [
            rim_tile(
                recv_corner[left_slot],
                recv_corner[right_slot],
                k,
                16,
                0,
                has_left & exists,
                has_right & exists,
            )[pick : pick + 4]
            for k in range(4)
        ]
        put_start(tiles, at_rows, 4, four)

    def next_lanes(values):
        turned_all = [pltpu.roll(value, LANES - 1, 1) for value in values]
        return [
            jnp.where(lane == LANES - 1, turned_all[(c + 1) % wide], turned_all[c])
            for c in range(wide)
        ]

    def last_lanes(values):
        turned_all = [pltpu.roll(value, 1, 1) for value in values]
        return [
            jnp.where(lane == 0, turned_all[(c - 1) % wide], turned_all[c]) for c in range(wide)
        ]

    def put_next(target, offset, here, columns):
        for k, values in columns.items():
            for c, value in enumerate(next_lanes(values)):
                target[offset + k, c, here, :] = value

    FIRST_NEXT = (H, MX, MY, LMY, LPY, QY, TT, AY, UV, PY, RY)
    SECOND_NEXT = (H, MY, LMY, LPY, PY, RY, IH)
    SECOND_AT = 12

    def base_prims(h, mx, my, ih):
        ux, uy = mx * ih, my * ih
        squared = GRAVITY * h
        cc = squared * lax.rsqrt(squared)
        half = 0.5 * cc
        out = {H: h, MX: mx, MY: my, LMX: ux - cc, LPX: ux + cc, LMY: uy - cc, LPY: uy + cc}
        half_i, ux_i, uy_i = half * ih, ux * ih, uy * ih
        out |= {PX: half_i - ux_i, RX: half_i + ux_i, PY: half_i - uy_i, RY: half_i + uy_i}
        return out, ux, uy, squared, cc, half

    def static_shift(row):
        here = pl.ds(row + TOP, 8)
        wets = [statics[WET, c, here, :] for c in range(wide)]
        for c, (right, left) in enumerate(zip(next_lanes(wets), last_lanes(wets))):
            col_flux[0, c, here, :] = right
            col_flux[1, c, here, :] = left
        put_next(
            first, NEXT, here,
            {j: [first[k, c, here, :] for c in range(wide)] for j, k in enumerate((H, MX, MY))},
        )

    def static_body(row):
        start = row + TOP
        here = pl.ds(start, 8)
        for c in range(wide):
            wet = statics[WET, c, here, :]
            above = statics[WET, c, pl.ds(start - 1, 8), :]
            below = statics[WET, c, pl.ds(start + 1, 8), :]
            right, left = col_flux[0, c, here, :], col_flux[1, c, here, :]
            scale = TIME_RATIO * wet
            statics[FMX, c, here, :] = scale * below
            statics[FMY, c, here, :] = scale * right
            h, mx, my = (first[k, c, here, :] for k in (H, MX, MY))
            out, ux, uy, squared, cc, half = base_prims(h, mx, my, 1.0 / h)
            pressure = 0.5 * squared * h
            out[QX], out[QY], out[TT] = mx * ux + pressure, my * uy + pressure, mx * uy
            out[AX], out[AY], out[UV] = squared - ux * ux, squared - uy * uy, ux * uy
            for lower, upper, u, n, q, a, wall, back in (
                (above, below, ux, mx, QX, AX, WX, BX),
                (left, right, uy, my, QY, AY, WY, BY),
            ):
                single = scale * (lower - upper)
                both = scale * (2.0 - (lower + upper))
                size = jnp.abs(u)
                out[wall] = single * out[q] + both * ((size + cc) * n)
                out[back] = single * out[a] + both * (u * (half - size))
            for k, value in out.items():
                if k not in (H, MX, MY):
                    first[k, c, here, :] = value
            h, mx, my = (first[NEXT + k, c, here, :] for k in range(3))
            out, ux, uy, squared, cc, half = base_prims(h, mx, my, 1.0 / h)
            out[QY], out[TT] = my * uy + 0.5 * squared * h, mx * uy
            out[AY], out[UV] = squared - uy * uy, ux * uy
            for j, k in enumerate(FIRST_NEXT):
                if j >= 3:
                    first[NEXT + j, c, here, :] = out[k]

    pipeline((static_shift, static_body), 0, chunks, G_STATIC)

    def reader(source, keys, offset):
        def at(k, c, rows_at):
            return source[k, c, rows_at, :]

        def right(k, c, rows_at):
            return source[offset + keys.index(k), c, rows_at, :]

        return at, right

    f_at, f_right = reader(first, FIRST_NEXT, NEXT)
    s_at, s_right = reader(second, SECOND_NEXT, SECOND_AT)

    def face(step, dim, c, here, lm_l, lm_r, lp_l, lp_r):
        low, high = jnp.minimum(lm_l, lm_r), jnp.maximum(lp_l, lp_r)
        slow, fast = jnp.minimum(low, 0.0), jnp.maximum(high, 0.0)
        inverse = 1.0 / (fast - slow)
        masked = statics[FMX + dim, c, here, :] * inverse
        alpha, beta = fast * masked, slow * masked
        gamma = slow * alpha
        e_slow = halved_on_tie(alpha * inverse, low < 0.0, low == 0.0)
        e_fast = halved_on_tie(beta * inverse, high > 0.0, high == 0.0)
        for k, value in enumerate((alpha, beta, gamma, slow, fast, e_slow, e_fast)):
            faces[step, dim, k, c, here, :] = value
        return alpha, beta, gamma

    def coefs_of(step, dim, c, here):
        return [faces[step, dim, k, c, here, :] for k in range(7)]

    def crossing(coefs, flux_l, flux_r, held_l, held_r):
        alpha, beta, gamma = coefs
        return alpha * flux_l - beta * flux_r + gamma * (held_r - held_l)

    def net_of(k, here):
        values = [col_flux[k, c, here, :] for c in range(wide)]
        return [mine - entering for mine, entering in zip(values, last_lanes(values))]

    def first_cols(row):
        here = pl.ds(row + TOP, 8)
        for c in range(wide):
            coefs = face(
                0, 1, c, here, f_at(LMY, c, here), f_right(LMY, c, here),
                f_at(LPY, c, here), f_right(LPY, c, here),
            )
            for k, (flux, held) in enumerate(((MY, H), (TT, MX), (QY, MY))):
                col_flux[k, c, here, :] = crossing(
                    coefs, f_at(flux, c, here), f_right(flux, c, here),
                    f_at(held, c, here), f_right(held, c, here),
                )

    def first_cells(row):
        start = row + TOP
        here, after, before = pl.ds(start, 8), pl.ds(start + 1, 8), pl.ds(start - 1, 8)
        net = [net_of(k, here) for k in range(3)]
        for c in range(wide):
            coefs = face(
                0, 0, c, here, f_at(LMX, c, here), f_at(LMX, c, after),
                f_at(LPX, c, here), f_at(LPX, c, after),
            )
            new = []
            for k, (flux, held) in enumerate(((MX, H), (QX, MX), (TT, MY))):
                value = crossing(
                    coefs, f_at(flux, c, here), f_at(flux, c, after),
                    f_at(held, c, here), f_at(held, c, after),
                )
                row_flux[k, c, here, :] = value
                change = value - row_flux[k, c, before, :] + net[k][c]
                if k > 0:
                    change = change + f_at((None, WX, WY)[k], c, here)
                new.append(f_at((H, MX, MY)[k], c, here) - change)
            h = new[0] + inflow[0, c, here, :]
            ih = 1.0 / h
            out = base_prims(h, new[1], new[2], ih)[0]
            out[IH] = ih
            for k, value in out.items():
                second[k, c, here, :] = value

    def first_shift(row):
        here = pl.ds(row + TOP, 8)
        heights = next_lanes([second[H, c, here, :] for c in range(wide)])
        flows = next_lanes([second[MY, c, here, :] for c in range(wide)])
        for c, (h, n) in enumerate(zip(heights, flows)):
            ih = 1.0 / h
            out = base_prims(h, n, n, ih)[0]
            out[IH] = ih
            for j, k in enumerate(SECOND_NEXT):
                second[SECOND_AT + j, c, here, :] = out[k]

    TERM, ADJ, ZX, ZY, TERM_R, ADJ_R, ZX_R, ZY_R = range(8)

    def last_cols(row):
        here = pl.ds(row + TOP, 8)
        for c in range(wide):
            coefs = face(
                1, 1, c, here, s_at(LMY, c, here), s_right(LMY, c, here),
                s_at(LPY, c, here), s_right(LPY, c, here),
            )
            col_flux[0, c, here, :] = crossing(
                coefs, s_at(MY, c, here), s_right(MY, c, here),
                s_at(H, c, here), s_right(H, c, here),
            )

    def last_cells(row):
        start = row + TOP
        here, after, before = pl.ds(start, 8), pl.ds(start + 1, 8), pl.ds(start - 1, 8)
        net = net_of(0, here)
        for c in range(wide):
            coefs = face(
                1, 0, c, here, s_at(LMX, c, here), s_at(LMX, c, after),
                s_at(LPX, c, here), s_at(LPX, c, after),
            )
            value = crossing(
                coefs, s_at(MX, c, here), s_at(MX, c, after),
                s_at(H, c, here), s_at(H, c, after),
            )
            row_flux[0, c, here, :] = value
            change = value - row_flux[0, c, before, :] + net[c]
            h = s_at(H, c, here) - change + inflow[1, c, here, :]
            last_h[c, here, :] = h
            adj[TERM, c, here, :] = statics[WGT, c, here, :] * h

    def adj_shift(*planes):
        def shift(row):
            here = pl.ds(row + TOP, 8)
            for k in planes:
                put_next(adj, TERM_R + k, here, {0: [adj[k, c, here, :] for c in range(wide)]})

        return shift

    pipeline((first_cols, first_cells, first_shift), 0, chunks, G_FIRST)
    if rounds > 1:
        learn(1)
        if rounds > 2:
            tell(2)
    pipeline((last_cols, last_cells, adj_shift(TERM)), 0, chunks, G_LAST)

    def depth_body(i, carry):
        start = pl.multiple_of(i * 8, 8)
        for c in range(tiles):
            own = pl.ds(start + OWN, 8)
            depth_out[pl.ds(start, 8), c * LANES : (c + 1) * LANES] = jnp.where(
                statics[WET, c, own, :] > 0.0, last_h[c, own, :], raw_d[c, pl.ds(start, 8), :]
            )
        return carry

    lax.fori_loop(0, rows // 8, depth_body, 0)
    def last_face(coefs, lm, lp, h, n, z, p, r, ih):
        alpha, beta, gamma = coefs[:3]
        gh = z[1] - z[0]
        fast_l, slow_l, fast_r, slow_r = split_speed_grads(
            *lm, *lp, coefs, gh * (n[1] - n[0]), gh * (h[1] - h[0])
        )
        jump = gamma * gh
        return (
            fast_l * p[0] - slow_l * r[0] - jump,
            alpha * gh + (fast_l + slow_l) * ih[0],
        ), (
            fast_r * p[1] - slow_r * r[1] + jump,
            (fast_r + slow_r) * ih[1] - beta * gh,
        )

    def back_cols(row):
        here = pl.ds(row + TOP, 8)
        for c in range(wide):

            def pair(k):
                return s_at(k, c, here), s_right(k, c, here)

            left, right = last_face(
                coefs_of(1, 1, c, here), pair(LMY), pair(LPY), pair(H), pair(MY),
                (adj[TERM, c, here, :], adj[TERM_R, c, here, :]), pair(PY), pair(RY), pair(IH),
            )
            for k in range(2):
                col_flux[k, c, here, :] = left[k]
                col_flux[2 + k, c, here, :] = right[k]

    def back_cells(row):
        start = row + TOP
        here, after, before = pl.ds(start, 8), pl.ds(start + 1, 8), pl.ds(start - 1, 8)
        entering = [
            last_lanes([col_flux[2 + k, c, here, :] for c in range(wide)]) for k in range(2)
        ]
        for c in range(wide):

            def pair(k):
                return s_at(k, c, here), s_at(k, c, after)

            left, right = last_face(
                coefs_of(1, 0, c, here), pair(LMX), pair(LPX), pair(H), pair(MX),
                (adj[TERM, c, here, :], adj[TERM, c, after, :]), pair(PX), pair(RX), pair(IH),
            )
            in_x = []
            for k in range(2):
                row_flux[k, c, here, :] = right[k]
                in_x.append(left[k] + row_flux[k, c, before, :])
            in_y = [col_flux[k, c, here, :] + entering[k][c] for k in range(2)]
            adj[ADJ, c, here, :] = adj[TERM, c, here, :] + (in_x[0] + in_y[0])
            adj[ZX, c, here, :] = in_x[1]
            adj[ZY, c, here, :] = in_y[1]

    pipeline((back_cols, back_cells, adj_shift(ADJ, ZX, ZY)), 0, chunks, G_BACK_LAST)

    own_hot = lax.broadcasted_iota(jnp.int32, (rows, dam_count), 0) == local_row
    stacked = []
    for plane in (ADJ, TERM):
        parts = [three_parts(adj[plane, c, OWN : OWN + rows, :]) for c in range(tiles)]
        stacked.append(
            jnp.concatenate([parts[c][k] for k in range(3) for c in range(tiles)], axis=1)
        )
    picked = lax.dot_general(
        jnp.concatenate(stacked, axis=0), jnp.concatenate([col_hot[...]] * 3, axis=0),
        (((1,), (0,)), ((), ())), preferred_element_type=jnp.float32,
    )
    gpart[...] = jnp.concatenate(
        [
            INFLOW_GAIN * jnp.sum(
                jnp.where(own_hot, picked[s * rows : (s + 1) * rows], 0.0), axis=0, keepdims=True
            )
            for s in range(2)
        ],
        axis=1,
    )

    for level in range(2, rounds):
        learn(level)
        if level + 1 < rounds:
            tell(level + 1)

    count = n_gx * n_gy

    def send_grads(k, carry):
        to = lax.rem(ix * n_gy + iy + 1 + k, count)
        pltpu.make_async_remote_copy(
            src_ref=gpart,
            dst_ref=recv_all.at[k],
            send_sem=grad_send.at[0],
            recv_sem=grad_recv.at[0],
            device_id=(lax.div(to, n_gy), lax.rem(to, n_gy)),
            device_id_type=MESH,
        ).start()
        return carry

    lax.fori_loop(0, count - 1, send_grads, 0)

    def first_face(coefs, lm, lp, h, n, t, q, v, zh, zn, zt, a, uv, p, r):
        alpha, beta, gamma = coefs[:3]
        gh, gn, gt = zh[1] - zh[0], zn[1] - zn[0], zt[1] - zt[0]
        dn = n[1] - n[0]
        fast_l, slow_l, fast_r, slow_r = split_speed_grads(
            *lm, *lp, coefs,
            gh * dn + gn * (q[1] - q[0]) + gt * (v[1] - v[0]),
            gh * (h[1] - h[0]) + gn * dn + gt * (t[1] - t[0]),
        )
        jump = gamma * gh
        return (
            alpha * (gn * a[0] - gt * uv[0]) + (fast_l * p[0] - slow_l * r[0]) - jump,
            (fast_r * p[1] - slow_r * r[1]) - beta * (gn * a[1] - gt * uv[1]) + jump,
        )

    def first_row_face(c, start):
        here, after = pl.ds(start, 8), pl.ds(start + 1, 8)

        def pair(k):
            return f_at(k, c, here), f_at(k, c, after)

        def z_pair(k):
            return adj[k, c, here, :], adj[k, c, after, :]

        return first_face(
            coefs_of(0, 0, c, here), pair(LMX), pair(LPX), pair(H), pair(MX), pair(MY), pair(QX),
            pair(TT), z_pair(ADJ), z_pair(ZX), z_pair(ZY), pair(AX), pair(UV), pair(PX), pair(RX),
        )

    for c in range(tiles):
        row_flux[0, c, pl.ds(OWN - 8, 8), :] = first_row_face(c, OWN - 8)[1]

    def backward_first(row):
        start = row + OWN
        here, before = pl.ds(start, 8), pl.ds(start - 1, 8)

        def col_face(c):
            def pair(k):
                return f_at(k, c, here), f_right(k, c, here)

            def z_pair(k):
                return adj[k, c, here, :], adj[k + TERM_R - TERM, c, here, :]

            return first_face(
                coefs_of(0, 1, c, here), pair(LMY), pair(LPY), pair(H), pair(MY), pair(MX),
                pair(QY), pair(TT), z_pair(ADJ), z_pair(ZY), z_pair(ZX), pair(AY), pair(UV),
                pair(PY), pair(RY),
            )

        turned = pltpu.roll(col_face(wide - 1)[1], 1, 1)
        for c in range(tiles):
            left, right = first_row_face(c, start)
            row_flux[0, c, here, :] = right
            left_y, right_y = col_face(c)
            turned, last = pltpu.roll(right_y, 1, 1), turned
            entering = jnp.where(lane == 0, last, turned)
            across = left + row_flux[0, c, before, :] + (left_y + entering)
            walls = adj[ZX, c, here, :] * f_at(BX, c, here) + adj[ZY, c, here, :] * f_at(BY, c, here)
            adjoint_out[pl.ds(row, 8), c * LANES : (c + 1) * LANES] = (
                adj[ADJ, c, here, :] + across - walls
            )

    sweep(backward_first, 0, rows // 8, G_BACK_FIRST)

    for sem in (grad_send, grad_recv):
        pltpu.make_async_copy(recv_all, recv_all, sem.at[0]).wait()
    total = gpart[...] + jnp.sum(recv_all[...], axis=0)
    for s in range(2):
        grad_out[s : s + 1, :] = total[:, s * dam_count : (s + 1) * dam_count]


def on_device(
    n_gx,
    n_gy,
    water_depth,
    momentum_x,
    momentum_y,
    wet_mask,
    damage_class,
    damage_rates,
    dam_cell,
    releases,
):
    rows, cols = water_depth.shape
    tiles = cols // LANES
    wide = tiles + 1
    high = rows + 2 * HALO + 2 * TOP
    dam_count = dam_cell.shape[0]
    f32 = jnp.float32
    plane = (wide, high, LANES)
    own = (tiles, rows, LANES)
    anywhere = pl.BlockSpec(memory_space=pl.ANY)
    vmem = pl.BlockSpec(memory_space=pltpu.VMEM)
    dma = pltpu.SemaphoreType.DMA
    final_depth, adjoint, grad = pl.pallas_call(
        functools.partial(kernel, n_gx, n_gy, cols * n_gy, damage_rates.shape[0]),
        out_shape=(
            pltpu.VMEM((rows, cols), f32),
            pltpu.VMEM((rows, cols), f32),
            pltpu.VMEM(releases.shape[::-1], f32),
        ),
        in_specs=[anywhere] * 8,
        out_specs=(vmem, vmem, vmem),
        scratch_shapes=[
            pltpu.VMEM(own, f32),
            pltpu.VMEM(own, f32),
            pltpu.VMEM(own, f32),
            pltpu.VMEM(own, jnp.int32),
            pltpu.VMEM(own, jnp.int32),
            pltpu.VMEM((32,) + plane, f32),
            pltpu.VMEM((19,) + plane, f32),
            pltpu.VMEM((4,) + plane, f32),
            pltpu.VMEM((2, 2, 7) + plane, f32),
            pltpu.VMEM((2,) + plane, f32),
            pltpu.VMEM((8,) + plane, f32),
            pltpu.VMEM(plane, f32),
            pltpu.VMEM((3,) + plane, f32),
            pltpu.VMEM((4,) + plane, f32),
            pltpu.VMEM((cols, dam_count), jnp.bfloat16),
            pltpu.VMEM((rows, LANES), f32),
            pltpu.VMEM((2, tiles, 16, LANES), f32),
            pltpu.VMEM((2, tiles, 16, LANES), f32),
            pltpu.VMEM((2, 16, rows), f32),
            pltpu.VMEM((2, 16, rows), f32),
            pltpu.VMEM((4, 8, LANES), f32),
            pltpu.VMEM((1, 2 * dam_count), f32),
            pltpu.VMEM((n_gx * n_gy - 1, 1, 2 * dam_count), f32),
            pltpu.SMEM(damage_rates.shape, f32),
            pltpu.VMEM((1, dam_count), jnp.int32),
            pltpu.VMEM(releases.shape[::-1], f32),
            dma((3,)),
            pltpu.SemaphoreType.REGULAR((max((n_gx - 1).bit_length(), 1),)),
            dma((5, tiles)),
            dma((8,)),
            dma((8,)),
            dma((1,)),
            dma((1,)),
        ],
        compiler_params=pltpu.CompilerParams(
            collective_id=0, has_side_effects=True, vmem_limit_bytes=56 * 1024 * 1024
        ),
        name="window",
    )(
        water_depth,
        momentum_x,
        momentum_y,
        wet_mask,
        damage_class,
        damage_rates,
        dam_cell.reshape(1, dam_count),
        releases.T,
    )
    return final_depth, adjoint, grad.T


def solution(mesh):
    n_gx, n_gy = mesh.shape["gx"], mesh.shape["gy"]
    grid = P("gx", "gy")
    return jax.shard_map(
        functools.partial(on_device, n_gx, n_gy),
        mesh=mesh,
        in_specs=(grid,) * 5 + (P(),) * 3,
        out_specs=(grid, grid, P()),
        check_vma=False,
    )
```

```python
import functools

import jax
import jax.numpy as jnp
from jax import lax
from jax.experimental import pallas as pl
from jax.experimental.pallas import tpu as pltpu
from jax.sharding import PartitionSpec as P

GRAVITY = 9.81
TIME_RATIO = 0.05
INFLOW_GAIN = 0.25
HALO = 4
LANES = 128
TOP = 8
OWN = TOP + HALO
G_STATIC, G_FIRST, G_LAST, G_BACK_LAST, G_BACK_FIRST = 3, 3, 5, 3, 1
MESH = pl.DeviceIdType.MESH


def sweep(body, first, last, group):
    whole = (last - first) // group

    def run(i, carry):
        base = pl.multiple_of(i * (8 * group), 8)
        for j in range(group):
            body(base + 8 * (first + j))
        return carry

    lax.fori_loop(0, whole, run, 0)
    for chunk in range(first + whole * group, last):
        body(8 * chunk)


def pipeline(stages, first, last, group=1):
    depth = len(stages)

    def step(at, index=None):
        for k in reversed(range(depth)):
            if index is None or first <= index - k < last:
                stages[k](at - 8 * k)

    for index in range(first, first + depth - 1):
        step(8 * index, index)
    begin = first + depth - 1
    whole = (last - begin) // group

    def run(i, carry):
        base = pl.multiple_of(i * (8 * group), 8)
        for j in range(group):
            step(base + 8 * (begin + j))
        return carry

    lax.fori_loop(0, whole, run, 0)
    for index in range(begin + whole * group, last + depth - 1):
        step(8 * index, index)


def three_parts(values):
    parts = []
    for _ in range(3):
        part = values.astype(jnp.bfloat16)
        values = values - part.astype(jnp.float32)
        parts.append(part)
    return parts


def halved_on_tie(value, picks, ties):
    return jnp.where(picks, value, jnp.where(ties, 0.5 * value, 0.0))


def split_speed_grads(lm_l, lm_r, lp_l, lp_r, coefs, d_term, k_term):
    _, _, _, slow, fast, e_slow, e_fast = coefs
    g_slow = e_slow * (fast * k_term - d_term)
    g_fast = e_fast * (d_term - slow * k_term)
    slow_l = halved_on_tie(g_slow, lm_l < lm_r, lm_l == lm_r)
    fast_l = halved_on_tie(g_fast, lp_l > lp_r, lp_l == lp_r)
    return fast_l, slow_l, g_fast - fast_l, g_slow - slow_l


def kernel(
    n_gx,
    n_gy,
    total_cols,
    classes,
    depth_in,
    mx_in,
    my_in,
    wet_in,
    class_in,
    rates_in,
    dams_in,
    releases_in,
    depth_out,
    adjoint_out,
    grad_out,
    raw_d,
    raw_x,
    raw_y,
    raw_wet,
    raw_cls,
    first,
    second,
    statics,
    faces,
    inflow,
    adj,
    last_h,
    row_flux,
    col_flux,
    col_hot,
    pack_cols,
    send_rows,
    recv_rows,
    send_cols,
    recv_cols,
    recv_corner,
    gpart,
    recv_all,
    rates,
    dams,
    releases,
    small_sem,
    know_sem,
    in_sem,
    edge_send,
    edge_recv,
    grad_send,
    grad_recv,
):
    rows, cols = depth_in.shape
    tiles = cols // LANES
    wide = tiles + 1
    span = rows + 2 * HALO
    chunks = span // 8
    ix, iy = lax.axis_index("gx"), lax.axis_index("gy")
    lane = lax.broadcasted_iota(jnp.int32, (8, LANES), 1)

    has_up, has_down = ix > 0, ix < n_gx - 1
    has_left, has_right = iy > 0, iy < n_gy - 1

    barrier = pltpu.get_barrier_semaphore()
    for step in range(1, n_gy):
        pl.semaphore_signal(
            barrier, inc=1, device_id=(ix, lax.rem(iy + step, n_gy)), device_id_type=MESH
        )
    sides = (
        (has_up, -1, 0),
        (has_down, 1, 0),
        (has_left, 0, -1),
        (has_right, 0, 1),
        (has_up & has_left, -1, -1),
        (has_up & has_right, -1, 1),
        (has_down & has_left, 1, -1),
        (has_down & has_right, 1, 1),
    )
    corners = 0
    for exists, dx, dy in sides[:2] + sides[4:]:
        corners = corners + exists.astype(jnp.int32)

        @pl.when(exists)
        def _(dx=dx, dy=dy):
            pl.semaphore_signal(barrier, inc=1, device_id=(ix + dx, iy + dy), device_id_type=MESH)

    small = [
        pltpu.make_async_copy(source, target, small_sem.at[index])
        for index, (source, target) in enumerate(
            ((rates_in, rates), (dams_in, dams), (releases_in, releases))
        )
    ]
    for copy in small[:1]:
        copy.start()
    loads = []
    for c in (0, tiles - 1, *range(1, tiles - 1)):
        for index, (source, target) in enumerate(
            ((wet_in, raw_wet), (class_in, raw_cls), (depth_in, raw_d), (mx_in, raw_x), (my_in, raw_y))
        ):
            copy = pltpu.make_async_copy(
                source.at[:, pl.ds(c * LANES, LANES)], target.at[c], in_sem.at[index, c]
            )
            copy.start()
            loads.append(copy)
    for copy in small[1:]:
        copy.start()

    for copy in loads:
        copy.wait()
    small[0].wait()

    rate = [rates[k] for k in range(classes)]

    def coded_chunk(c, start, size=8):
        at = (c, pl.ds(start, size), slice(None))
        wet = raw_wet[at] > 0
        cls = raw_cls[at]
        weight = jnp.full(cls.shape, rate[0])
        for k in range(1, classes):
            weight = jnp.where(cls == k, rate[k], weight)
        return (
            jnp.where(wet, raw_d[at], -1.0),
            raw_x[at],
            raw_y[at],
            jnp.where(wet, weight, 0.0),
        )

    for c in range(tiles):
        for side, start, pick in ((0, 0, 0), (1, rows - 8, 4)):
            four = coded_chunk(c, start)
            for k in range(4):
                send_rows[side, c, 4 * k : 4 * k + 4, :] = four[k][pick : pick + 4]

    def pack_body(i, carry):
        start = pl.multiple_of(i * 8, 8)
        left = coded_chunk(0, start)
        right = coded_chunk(tiles - 1, start)
        packed = jnp.zeros((8, LANES), jnp.float32)
        for k in range(4):
            mine = (lane >= 4 * k) & (lane < 4 * k + 4)
            packed = jnp.where(mine, pltpu.roll(left[k], 4 * k, 1) if k else left[k], packed)
            mine = (lane >= 16 + 4 * k) & (lane < 20 + 4 * k)
            packed = jnp.where(mine, pltpu.roll(right[k], 20 + 4 * k, 1), packed)
        pack_cols[pl.ds(start, 8), :] = packed
        return carry

    lax.fori_loop(0, rows // 8, pack_body, 0, unroll=2)
    turned = jnp.transpose(pack_cols[...])
    send_cols[0] = turned[0:16]
    send_cols[1] = turned[16:32]

    pl.semaphore_wait(barrier, (n_gy - 1) + corners)

    rounds = (n_gx - 1).bit_length()

    def reach(level):
        return (ix >= 2**level, -(2**level)), (ix + 2**level < n_gx, 2**level)

    def tell(level):
        for exists, offset in reach(level):

            @pl.when(exists)
            def _(offset=offset):
                pl.semaphore_signal(
                    know_sem.at[level], inc=1, device_id=(ix + offset, iy), device_id_type=MESH
                )

    def learn(level):
        pl.semaphore_wait(
            know_sem.at[level], sum(exists.astype(jnp.int32) for exists, _ in reach(level))
        )

    def edge_copy(index):
        _, dx, dy = sides[index]
        opposite = (1, 0, 3, 2, 7, 6, 5, 4)[index]
        if index < 2:
            source, target = send_rows.at[index], recv_rows.at[opposite]
        elif index < 4:
            source, target = send_cols.at[index - 2], recv_cols.at[opposite - 2]
        else:
            first = 0 if index < 6 else rows - 8
            source, target = pack_cols.at[pl.ds(first, 8), :], recv_corner.at[opposite - 4]
        return pltpu.make_async_remote_copy(
            src_ref=source,
            dst_ref=target,
            send_sem=edge_send.at[index],
            recv_sem=edge_recv.at[opposite],
            device_id=(ix + dx, iy + dy),
            device_id_type=MESH,
        )

    for index in (4, 5, 6, 7, 0, 1, 2, 3):

        @pl.when(sides[index][0])
        def _(index=index):
            edge_copy(index).start()

    if rounds > 0:
        tell(0)

    H, MX, MY, LMX, LPX, LMY, LPY, PX, RX, PY, RY = range(11)
    IH = 11
    QX, QY, TT, AX, AY, UV, WX, WY, BX, BY = range(11, 21)
    NEXT = 21
    WET, WGT, FMX, FMY = range(4)
    ALPHA, BETA, GAMMA, SLOW, FAST, ESLOW, EFAST = range(7)

    def put_start(c, at_rows, size, four):
        wet = four[0] > 0.0
        at = (c, pl.ds(at_rows, size), slice(None))
        first[(H,) + at] = jnp.where(wet, four[0], 1.0)
        first[(MX,) + at] = jnp.where(wet, four[1], 0.0)
        first[(MY,) + at] = jnp.where(wet, four[2], 0.0)
        statics[(WGT,) + at] = jnp.where(wet, four[3], 0.0)
        statics[(WET,) + at] = jnp.where(wet, 1.0, 0.0)

    def own_body(i, carry):
        start = pl.multiple_of(i * 8, 8)
        for c in range(tiles):
            put_start(c, start + OWN, 8, coded_chunk(c, start))
        return carry

    lax.fori_loop(0, rows // 8, own_body, 0)

    for copy in small[1:]:
        copy.wait()
    cell = dams[...]
    if total_cols & (total_cols - 1) == 0:
        dam_row = lax.shift_right_logical(cell, total_cols.bit_length() - 1)
    else:
        dam_row = lax.div(cell, total_cols)
    dam_col = cell - dam_row * total_cols
    dam_count = cell.shape[1]
    local_row = dam_row - ix * rows
    local_col = dam_col - iy * cols
    amounts = INFLOW_GAIN * releases[...]
    thrice = lambda values: jnp.concatenate([values] * 3, axis=1)
    amounts = jnp.concatenate(
        [part.astype(jnp.float32) for part in three_parts(amounts)], axis=1
    )
    wide_row = lax.broadcasted_iota(jnp.int32, (span, 3 * dam_count), 0) - HALO
    row_hot = wide_row == thrice(local_row)
    gain_rows = jnp.concatenate(
        [jnp.where(row_hot, amounts[s : s + 1], 0.0) for s in range(2)], axis=0
    ).astype(jnp.bfloat16)
    position = lax.broadcasted_iota(jnp.int32, (LANES, 3 * dam_count), 0)
    col_thrice = thrice(local_col)
    hots = []
    for c in range(wide):
        if c < tiles:
            column = position + c * LANES
        else:
            column = jnp.where(
                position < HALO,
                position + cols,
                jnp.where(position >= LANES - HALO, position - LANES, -2 * LANES),
            )
        hot = (column == col_thrice).astype(jnp.float32).astype(jnp.bfloat16)
        if c < tiles:
            col_hot[c * LANES : (c + 1) * LANES, :] = hot[:, :dam_count]
        hots.append(hot)
    poured = lax.dot_general(
        gain_rows, jnp.concatenate(hots, axis=0), (((1,), (1,)), ((), ())),
        preferred_element_type=jnp.float32,
    )
    for s in range(2):
        for c in range(wide):
            inflow[s, c, TOP : TOP + span, :] = poured[
                s * span : (s + 1) * span, c * LANES : (c + 1) * LANES
            ]

    for index in range(8):

        @pl.when(sides[index][0])
        def _(index=index):
            copy = edge_copy(index)
            copy.wait_send()
            opposite = (1, 0, 3, 2, 7, 6, 5, 4)[index]
            if index < 2:
                target = recv_rows.at[index]
            elif index < 4:
                target = recv_cols.at[index - 2]
            else:
                target = recv_corner.at[index - 4]
            pltpu.make_async_copy(target, target, edge_recv.at[index]).wait()

    if rounds > 0:
        learn(0)
        if rounds > 1:
            tell(1)

    for c in range(tiles):
        for side, exists, at_rows in ((0, has_up, TOP), (1, has_down, OWN + rows)):
            four = [recv_rows[side, c, 4 * k : 4 * k + 4, :] for k in range(4)]
            four[0] = jnp.where(exists, four[0], -1.0)
            put_start(c, at_rows, 4, four)

    halves = jnp.concatenate(
        [recv_cols[0], recv_cols[1], jnp.zeros((LANES - 32, rows), jnp.float32)], axis=0
    )
    pack_cols[...] = jnp.transpose(halves)

    def rim_tile(left_part, right_part, k, left_at, right_at, from_left, from_right):
        fill = -1.0 if k == 0 else 0.0
        on_right = (lane < HALO) & from_right
        on_left = (lane >= LANES - HALO) & from_left
        shift_r = (LANES - right_at - 4 * k) % LANES
        shift_l = (LANES - HALO - left_at - 4 * k) % LANES
        right_val = pltpu.roll(right_part, shift_r, 1) if shift_r else right_part
        left_val = pltpu.roll(left_part, shift_l, 1) if shift_l else left_part
        return jnp.where(on_right, right_val, jnp.where(on_left, left_val, fill))

    def rim_body(i, carry):
        start = pl.multiple_of(i * 8, 8)
        part = pack_cols[pl.ds(start, 8), :]
        four = [rim_tile(part, part, k, 0, 16, has_left, has_right) for k in range(4)]
        put_start(tiles, start + OWN, 8, four)
        return carry

    lax.fori_loop(0, rows // 8, rim_body, 0, unroll=2)
    for left_slot, right_slot, exists, at_rows, pick in (
        (0, 1, has_up, TOP, 4),
        (2, 3, has_down, OWN + rows, 0),
    ):
        four = [
            rim_tile(
                recv_corner[left_slot],
                recv_corner[right_slot],
                k,
                16,
                0,
                has_left & exists,
                has_right & exists,
            )[pick : pick + 4]
            for k in range(4)
        ]
        put_start(tiles, at_rows, 4, four)

    def next_lanes(values):
        turned_all = [pltpu.roll(value, LANES - 1, 1) for value in values]
        return [
            jnp.where(lane == LANES - 1, turned_all[(c + 1) % wide], turned_all[c])
            for c in range(wide)
        ]

    def last_lanes(values):
        turned_all = [pltpu.roll(value, 1, 1) for value in values]
        return [
            jnp.where(lane == 0, turned_all[(c - 1) % wide], turned_all[c]) for c in range(wide)
        ]

    def put_next(target, offset, here, columns):
        for k, values in columns.items():
            for c, value in enumerate(next_lanes(values)):
                target[offset + k, c, here, :] = value

    FIRST_NEXT = (H, MX, MY, LMY, LPY, QY, TT, AY, UV, PY, RY)
    SECOND_NEXT = (H, MY, LMY, LPY, PY, RY, IH)
    SECOND_AT = 12

    def base_prims(h, mx, my, ih):
        ux, uy = mx * ih, my * ih
        squared = GRAVITY * h
        cc = squared * lax.rsqrt(squared)
        half = 0.5 * cc
        out = {H: h, MX: mx, MY: my, LMX: ux - cc, LPX: ux + cc, LMY: uy - cc, LPY: uy + cc}
        half_i, ux_i, uy_i = half * ih, ux * ih, uy * ih
        out |= {PX: half_i - ux_i, RX: half_i + ux_i, PY: half_i - uy_i, RY: half_i + uy_i}
        return out, ux, uy, squared, cc, half

    def static_shift(row):
        here = pl.ds(row + TOP, 8)
        wets = [statics[WET, c, here, :] for c in range(wide)]
        for c, (right, left) in enumerate(zip(next_lanes(wets), last_lanes(wets))):
            col_flux[0, c, here, :] = right
            col_flux[1, c, here, :] = left
        put_next(
            first, NEXT, here,
            {j: [first[k, c, here, :] for c in range(wide)] for j, k in enumerate((H, MX, MY))},
        )

    def static_body(row):
        start = row + TOP
        here = pl.ds(start, 8)
        for c in range(wide):
            wet = statics[WET, c, here, :]
            above = statics[WET, c, pl.ds(start - 1, 8), :]
            below = statics[WET, c, pl.ds(start + 1, 8), :]
            right, left = col_flux[0, c, here, :], col_flux[1, c, here, :]
            scale = TIME_RATIO * wet
            statics[FMX, c, here, :] = scale * below
            statics[FMY, c, here, :] = scale * right
            h, mx, my = (first[k, c, here, :] for k in (H, MX, MY))
            out, ux, uy, squared, cc, half = base_prims(h, mx, my, 1.0 / h)
            pressure = 0.5 * squared * h
            out[QX], out[QY], out[TT] = mx * ux + pressure, my * uy + pressure, mx * uy
            out[AX], out[AY], out[UV] = squared - ux * ux, squared - uy * uy, ux * uy
            for lower, upper, u, n, q, a, wall, back in (
                (above, below, ux, mx, QX, AX, WX, BX),
                (left, right, uy, my, QY, AY, WY, BY),
            ):
                single = scale * (lower - upper)
                both = scale * (2.0 - (lower + upper))
                size = jnp.abs(u)
                out[wall] = single * out[q] + both * ((size + cc) * n)
                out[back] = single * out[a] + both * (u * (half - size))
            for k, value in out.items():
                if k not in (H, MX, MY):
                    first[k, c, here, :] = value
            h, mx, my = (first[NEXT + k, c, here, :] for k in range(3))
            out, ux, uy, squared, cc, half = base_prims(h, mx, my, 1.0 / h)
            out[QY], out[TT] = my * uy + 0.5 * squared * h, mx * uy
            out[AY], out[UV] = squared - uy * uy, ux * uy
            for j, k in enumerate(FIRST_NEXT):
                if j >= 3:
                    first[NEXT + j, c, here, :] = out[k]

    pipeline((static_shift, static_body), 0, chunks, G_STATIC)

    def reader(source, keys, offset):
        def at(k, c, rows_at):
            return source[k, c, rows_at, :]

        def right(k, c, rows_at):
            return source[offset + keys.index(k), c, rows_at, :]

        return at, right

    f_at, f_right = reader(first, FIRST_NEXT, NEXT)
    s_at, s_right = reader(second, SECOND_NEXT, SECOND_AT)

    def face(step, dim, c, here, lm_l, lm_r, lp_l, lp_r):
        low, high = jnp.minimum(lm_l, lm_r), jnp.maximum(lp_l, lp_r)
        slow, fast = jnp.minimum(low, 0.0), jnp.maximum(high, 0.0)
        inverse = 1.0 / (fast - slow)
        masked = statics[FMX + dim, c, here, :] * inverse
        alpha, beta = fast * masked, slow * masked
        gamma = slow * alpha
        e_slow = halved_on_tie(alpha * inverse, low < 0.0, low == 0.0)
        e_fast = halved_on_tie(beta * inverse, high > 0.0, high == 0.0)
        for k, value in enumerate((alpha, beta, gamma, slow, fast, e_slow, e_fast)):
            faces[step, dim, k, c, here, :] = value
        return alpha, beta, gamma

    def coefs_of(step, dim, c, here):
        return [faces[step, dim, k, c, here, :] for k in range(7)]

    def crossing(coefs, flux_l, flux_r, held_l, held_r):
        alpha, beta, gamma = coefs
        return alpha * flux_l - beta * flux_r + gamma * (held_r - held_l)

    def net_of(k, here):
        values = [col_flux[k, c, here, :] for c in range(wide)]
        return [mine - entering for mine, entering in zip(values, last_lanes(values))]

    def first_cols(row):
        here = pl.ds(row + TOP, 8)
        for c in range(wide):
            coefs = face(
                0, 1, c, here, f_at(LMY, c, here), f_right(LMY, c, here),
                f_at(LPY, c, here), f_right(LPY, c, here),
            )
            for k, (flux, held) in enumerate(((MY, H), (TT, MX), (QY, MY))):
                col_flux[k, c, here, :] = crossing(
                    coefs, f_at(flux, c, here), f_right(flux, c, here),
                    f_at(held, c, here), f_right(held, c, here),
                )

    def first_cells(row):
        start = row + TOP
        here, after, before = pl.ds(start, 8), pl.ds(start + 1, 8), pl.ds(start - 1, 8)
        net = [net_of(k, here) for k in range(3)]
        for c in range(wide):
            coefs = face(
                0, 0, c, here, f_at(LMX, c, here), f_at(LMX, c, after),
                f_at(LPX, c, here), f_at(LPX, c, after),
            )
            new = []
            for k, (flux, held) in enumerate(((MX, H), (QX, MX), (TT, MY))):
                value = crossing(
                    coefs, f_at(flux, c, here), f_at(flux, c, after),
                    f_at(held, c, here), f_at(held, c, after),
                )
                row_flux[k, c, here, :] = value
                change = value - row_flux[k, c, before, :] + net[k][c]
                if k > 0:
                    change = change + f_at((None, WX, WY)[k], c, here)
                new.append(f_at((H, MX, MY)[k], c, here) - change)
            h = new[0] + inflow[0, c, here, :]
            ih = 1.0 / h
            out = base_prims(h, new[1], new[2], ih)[0]
            out[IH] = ih
            for k, value in out.items():
                second[k, c, here, :] = value

    def first_shift(row):
        here = pl.ds(row + TOP, 8)
        heights = next_lanes([second[H, c, here, :] for c in range(wide)])
        flows = next_lanes([second[MY, c, here, :] for c in range(wide)])
        for c, (h, n) in enumerate(zip(heights, flows)):
            ih = 1.0 / h
            out = base_prims(h, n, n, ih)[0]
            out[IH] = ih
            for j, k in enumerate(SECOND_NEXT):
                second[SECOND_AT + j, c, here, :] = out[k]

    TERM, ADJ, ZX, ZY, TERM_R, ADJ_R, ZX_R, ZY_R = range(8)

    def last_cols(row):
        here = pl.ds(row + TOP, 8)
        for c in range(wide):
            coefs = face(
                1, 1, c, here, s_at(LMY, c, here), s_right(LMY, c, here),
                s_at(LPY, c, here), s_right(LPY, c, here),
            )
            col_flux[0, c, here, :] = crossing(
                coefs, s_at(MY, c, here), s_right(MY, c, here),
                s_at(H, c, here), s_right(H, c, here),
            )

    def last_cells(row):
        start = row + TOP
        here, after, before = pl.ds(start, 8), pl.ds(start + 1, 8), pl.ds(start - 1, 8)
        net = net_of(0, here)
        for c in range(wide):
            coefs = face(
                1, 0, c, here, s_at(LMX, c, here), s_at(LMX, c, after),
                s_at(LPX, c, here), s_at(LPX, c, after),
            )
            value = crossing(
                coefs, s_at(MX, c, here), s_at(MX, c, after),
                s_at(H, c, here), s_at(H, c, after),
            )
            row_flux[0, c, here, :] = value
            change = value - row_flux[0, c, before, :] + net[c]
            h = s_at(H, c, here) - change + inflow[1, c, here, :]
            last_h[c, here, :] = h
            adj[TERM, c, here, :] = statics[WGT, c, here, :] * h

    def adj_shift(*planes):
        def shift(row):
            here = pl.ds(row + TOP, 8)
            for k in planes:
                put_next(adj, TERM_R + k, here, {0: [adj[k, c, here, :] for c in range(wide)]})

        return shift

    pipeline((first_cols, first_cells, first_shift), 0, chunks, G_FIRST)
    if rounds > 1:
        learn(1)
        if rounds > 2:
            tell(2)
    pipeline((last_cols, last_cells, adj_shift(TERM)), 0, chunks, G_LAST)

    def depth_body(i, carry):
        start = pl.multiple_of(i * 8, 8)
        for c in range(tiles):
            own = pl.ds(start + OWN, 8)
            depth_out[pl.ds(start, 8), c * LANES : (c + 1) * LANES] = jnp.where(
                statics[WET, c, own, :] > 0.0, last_h[c, own, :], raw_d[c, pl.ds(start, 8), :]
            )
        return carry

    lax.fori_loop(0, rows // 8, depth_body, 0)
    def last_face(coefs, lm, lp, h, n, z, p, r, ih):
        alpha, beta, gamma = coefs[:3]
        gh = z[1] - z[0]
        fast_l, slow_l, fast_r, slow_r = split_speed_grads(
            *lm, *lp, coefs, gh * (n[1] - n[0]), gh * (h[1] - h[0])
        )
        jump = gamma * gh
        return (
            fast_l * p[0] - slow_l * r[0] - jump,
            alpha * gh + (fast_l + slow_l) * ih[0],
        ), (
            fast_r * p[1] - slow_r * r[1] + jump,
            (fast_r + slow_r) * ih[1] - beta * gh,
        )

    def back_cols(row):
        here = pl.ds(row + TOP, 8)
        for c in range(wide):

            def pair(k):
                return s_at(k, c, here), s_right(k, c, here)

            left, right = last_face(
                coefs_of(1, 1, c, here), pair(LMY), pair(LPY), pair(H), pair(MY),
                (adj[TERM, c, here, :], adj[TERM_R, c, here, :]), pair(PY), pair(RY), pair(IH),
            )
            for k in range(2):
                col_flux[k, c, here, :] = left[k]
                col_flux[2 + k, c, here, :] = right[k]

    def back_cells(row):
        start = row + TOP
        here, after, before = pl.ds(start, 8), pl.ds(start + 1, 8), pl.ds(start - 1, 8)
        entering = [
            last_lanes([col_flux[2 + k, c, here, :] for c in range(wide)]) for k in range(2)
        ]
        for c in range(wide):

            def pair(k):
                return s_at(k, c, here), s_at(k, c, after)

            left, right = last_face(
                coefs_of(1, 0, c, here), pair(LMX), pair(LPX), pair(H), pair(MX),
                (adj[TERM, c, here, :], adj[TERM, c, after, :]), pair(PX), pair(RX), pair(IH),
            )
            in_x = []
            for k in range(2):
                row_flux[k, c, here, :] = right[k]
                in_x.append(left[k] + row_flux[k, c, before, :])
            in_y = [col_flux[k, c, here, :] + entering[k][c] for k in range(2)]
            adj[ADJ, c, here, :] = adj[TERM, c, here, :] + (in_x[0] + in_y[0])
            adj[ZX, c, here, :] = in_x[1]
            adj[ZY, c, here, :] = in_y[1]

    pipeline((back_cols, back_cells, adj_shift(ADJ, ZX, ZY)), 0, chunks, G_BACK_LAST)

    own_hot = lax.broadcasted_iota(jnp.int32, (rows, dam_count), 0) == local_row
    stacked = []
    for plane in (ADJ, TERM):
        parts = [three_parts(adj[plane, c, OWN : OWN + rows, :]) for c in range(tiles)]
        stacked.append(
            jnp.concatenate([parts[c][k] for k in range(3) for c in range(tiles)], axis=1)
        )
    picked = lax.dot_general(
        jnp.concatenate(stacked, axis=0), jnp.concatenate([col_hot[...]] * 3, axis=0),
        (((1,), (0,)), ((), ())), preferred_element_type=jnp.float32,
    )
    gpart[...] = jnp.concatenate(
        [
            INFLOW_GAIN * jnp.sum(
                jnp.where(own_hot, picked[s * rows : (s + 1) * rows], 0.0), axis=0, keepdims=True
            )
            for s in range(2)
        ],
        axis=1,
    )

    for level in range(2, rounds):
        learn(level)
        if level + 1 < rounds:
            tell(level + 1)

    count = n_gx * n_gy

    def send_grads(k, carry):
        to = lax.rem(ix * n_gy + iy + 1 + k, count)
        pltpu.make_async_remote_copy(
            src_ref=gpart,
            dst_ref=recv_all.at[k],
            send_sem=grad_send.at[0],
            recv_sem=grad_recv.at[0],
            device_id=(lax.div(to, n_gy), lax.rem(to, n_gy)),
            device_id_type=MESH,
        ).start()
        return carry

    lax.fori_loop(0, count - 1, send_grads, 0)

    def first_face(coefs, lm, lp, h, n, t, q, v, zh, zn, zt, a, uv, p, r):
        alpha, beta, gamma = coefs[:3]
        gh, gn, gt = zh[1] - zh[0], zn[1] - zn[0], zt[1] - zt[0]
        dn = n[1] - n[0]
        fast_l, slow_l, fast_r, slow_r = split_speed_grads(
            *lm, *lp, coefs,
            gh * dn + gn * (q[1] - q[0]) + gt * (v[1] - v[0]),
            gh * (h[1] - h[0]) + gn * dn + gt * (t[1] - t[0]),
        )
        jump = gamma * gh
        return (
            alpha * (gn * a[0] - gt * uv[0]) + (fast_l * p[0] - slow_l * r[0]) - jump,
            (fast_r * p[1] - slow_r * r[1]) - beta * (gn * a[1] - gt * uv[1]) + jump,
        )

    def first_row_face(c, start):
        here, after = pl.ds(start, 8), pl.ds(start + 1, 8)

        def pair(k):
            return f_at(k, c, here), f_at(k, c, after)

        def z_pair(k):
            return adj[k, c, here, :], adj[k, c, after, :]

        return first_face(
            coefs_of(0, 0, c, here), pair(LMX), pair(LPX), pair(H), pair(MX), pair(MY), pair(QX),
            pair(TT), z_pair(ADJ), z_pair(ZX), z_pair(ZY), pair(AX), pair(UV), pair(PX), pair(RX),
        )

    for c in range(tiles):
        row_flux[0, c, pl.ds(OWN - 8, 8), :] = first_row_face(c, OWN - 8)[1]

    def backward_first(row):
        start = row + OWN
        here, before = pl.ds(start, 8), pl.ds(start - 1, 8)

        def col_face(c):
            def pair(k):
                return f_at(k, c, here), f_right(k, c, here)

            def z_pair(k):
                return adj[k, c, here, :], adj[k + TERM_R - TERM, c, here, :]

            return first_face(
                coefs_of(0, 1, c, here), pair(LMY), pair(LPY), pair(H), pair(MY), pair(MX),
                pair(QY), pair(TT), z_pair(ADJ), z_pair(ZY), z_pair(ZX), pair(AY), pair(UV),
                pair(PY), pair(RY),
            )

        turned = pltpu.roll(col_face(wide - 1)[1], 1, 1)
        for c in range(tiles):
            left, right = first_row_face(c, start)
            row_flux[0, c, here, :] = right
            left_y, right_y = col_face(c)
            turned, last = pltpu.roll(right_y, 1, 1), turned
            entering = jnp.where(lane == 0, last, turned)
            across = left + row_flux[0, c, before, :] + (left_y + entering)
            walls = adj[ZX, c, here, :] * f_at(BX, c, here) + adj[ZY, c, here, :] * f_at(BY, c, here)
            adjoint_out[pl.ds(row, 8), c * LANES : (c + 1) * LANES] = (
                adj[ADJ, c, here, :] + across - walls
            )

    sweep(backward_first, 0, rows // 8, G_BACK_FIRST)

    for sem in (grad_send, grad_recv):
        pltpu.make_async_copy(recv_all, recv_all, sem.at[0]).wait()
    total = gpart[...] + jnp.sum(recv_all[...], axis=0)
    for s in range(2):
        grad_out[s : s + 1, :] = total[:, s * dam_count : (s + 1) * dam_count]


def place(*refs):
    sources, targets, sem = refs[:3], refs[3:6], refs[6]
    copies = [
        pltpu.make_async_copy(source, target, sem.at[k])
        for k, (source, target) in enumerate(zip(sources, targets))
    ]
    for copy in copies:
        copy.start()
    for copy in copies:
        copy.wait()


def on_device(
    n_gx,
    n_gy,
    water_depth,
    momentum_x,
    momentum_y,
    wet_mask,
    damage_class,
    damage_rates,
    dam_cell,
    releases,
):
    rows, cols = water_depth.shape
    tiles = cols // LANES
    wide = tiles + 1
    high = rows + 2 * HALO + 2 * TOP
    dam_count = dam_cell.shape[0]
    f32 = jnp.float32
    plane = (wide, high, LANES)
    own = (tiles, rows, LANES)
    anywhere = pl.BlockSpec(memory_space=pl.ANY)
    vmem = pl.BlockSpec(memory_space=pltpu.VMEM)
    dma = pltpu.SemaphoreType.DMA
    results = pl.pallas_call(
        functools.partial(kernel, n_gx, n_gy, cols * n_gy, damage_rates.shape[0]),
        out_shape=(
            pltpu.VMEM((rows, cols), f32),
            pltpu.VMEM((rows, cols), f32),
            pltpu.VMEM(releases.shape[::-1], f32),
        ),
        in_specs=[anywhere] * 8,
        out_specs=(vmem, vmem, vmem),
        scratch_shapes=[
            pltpu.VMEM(own, f32),
            pltpu.VMEM(own, f32),
            pltpu.VMEM(own, f32),
            pltpu.VMEM(own, jnp.int32),
            pltpu.VMEM(own, jnp.int32),
            pltpu.VMEM((32,) + plane, f32),
            pltpu.VMEM((19,) + plane, f32),
            pltpu.VMEM((4,) + plane, f32),
            pltpu.VMEM((2, 2, 7) + plane, f32),
            pltpu.VMEM((2,) + plane, f32),
            pltpu.VMEM((8,) + plane, f32),
            pltpu.VMEM(plane, f32),
            pltpu.VMEM((3,) + plane, f32),
            pltpu.VMEM((4,) + plane, f32),
            pltpu.VMEM((cols, dam_count), jnp.bfloat16),
            pltpu.VMEM((rows, LANES), f32),
            pltpu.VMEM((2, tiles, 16, LANES), f32),
            pltpu.VMEM((2, tiles, 16, LANES), f32),
            pltpu.VMEM((2, 16, rows), f32),
            pltpu.VMEM((2, 16, rows), f32),
            pltpu.VMEM((4, 8, LANES), f32),
            pltpu.VMEM((1, 2 * dam_count), f32),
            pltpu.VMEM((n_gx * n_gy - 1, 1, 2 * dam_count), f32),
            pltpu.SMEM(damage_rates.shape, f32),
            pltpu.VMEM((1, dam_count), jnp.int32),
            pltpu.VMEM(releases.shape[::-1], f32),
            dma((3,)),
            pltpu.SemaphoreType.REGULAR((max((n_gx - 1).bit_length(), 1),)),
            dma((5, tiles)),
            dma((8,)),
            dma((8,)),
            dma((1,)),
            dma((1,)),
        ],
        compiler_params=pltpu.CompilerParams(
            collective_id=0, has_side_effects=True, vmem_limit_bytes=56 * 1024 * 1024
        ),
        name="window",
    )(
        water_depth,
        momentum_x,
        momentum_y,
        wet_mask,
        damage_class,
        damage_rates,
        dam_cell.reshape(1, dam_count),
        releases.T,
    )
    final_depth, adjoint, grad = pl.pallas_call(
        place,
        out_shape=tuple(jax.ShapeDtypeStruct(value.shape, f32) for value in results),
        in_specs=[vmem] * 3,
        out_specs=(anywhere,) * 3,
        scratch_shapes=[dma((3,))],
        name="place",
    )(*(pltpu.with_memory_space_constraint(value, pltpu.VMEM) for value in results))
    return final_depth, adjoint, grad.T


def solution(mesh):
    n_gx, n_gy = mesh.shape["gx"], mesh.shape["gy"]
    grid = P("gx", "gy")
    return jax.shard_map(
        functools.partial(on_device, n_gx, n_gy),
        mesh=mesh,
        in_specs=(grid,) * 5 + (P(),) * 3,
        out_specs=(grid, grid, P()),
        check_vma=False,
    )
```

```python
import functools

import jax
import jax.numpy as jnp
from jax import lax
from jax.experimental import pallas as pl
from jax.experimental.pallas import tpu as pltpu
from jax.sharding import PartitionSpec as P

GRAVITY = 9.81
TIME_RATIO = 0.05
INFLOW_GAIN = 0.25
HALO = 4
LANES = 128
TOP = 8
OWN = TOP + HALO
G_STATIC, G_FACES, G_OUTER, G_FIRST, G_LAST, G_BACK_LAST, G_BACK_FIRST = 2, 2, 2, 3, 5, 3, 1
MESH = pl.DeviceIdType.MESH


def sweep(body, first, last, group):
    whole = (last - first) // group

    def run(i, carry):
        base = pl.multiple_of(i * (8 * group), 8)
        for j in range(group):
            body(base + 8 * (first + j))
        return carry

    lax.fori_loop(0, whole, run, 0)
    for chunk in range(first + whole * group, last):
        body(8 * chunk)


def pipeline(stages, first, last, group=1, begin=None, end=None):
    depth = len(stages)
    begin = first + depth - 1 if begin is None else begin
    end = last if end is None else end

    def step(at, index=None):
        for k in reversed(range(depth)):
            if index is None:
                stages[k](at - 8 * k, None)
            elif first <= index - k < last:
                stages[k](at - 8 * k, index - k)

    for index in range(first, begin):
        step(8 * index, index)
    whole = (end - begin) // group

    def run(i, carry):
        base = pl.multiple_of(i * (8 * group), 8)
        for j in range(group):
            step(base + 8 * (begin + j))
        return carry

    lax.fori_loop(0, whole, run, 0)
    for index in range(begin + whole * group, last + depth - 1):
        step(8 * index, index)


def three_parts(values):
    parts = []
    for _ in range(3):
        part = values.astype(jnp.bfloat16)
        values = values - part.astype(jnp.float32)
        parts.append(part)
    return parts


def halved_on_tie(value, picks, ties):
    return jnp.where(picks, value, jnp.where(ties, 0.5 * value, 0.0))


def split_speed_grads(lm_l, lm_r, lp_l, lp_r, coefs, d_term, k_term):
    _, _, _, slow, fast, e_slow, e_fast = coefs
    g_slow = e_slow * (fast * k_term - d_term)
    g_fast = e_fast * (d_term - slow * k_term)
    slow_l = halved_on_tie(g_slow, lm_l < lm_r, lm_l == lm_r)
    fast_l = halved_on_tie(g_fast, lp_l > lp_r, lp_l == lp_r)
    return fast_l, slow_l, g_fast - fast_l, g_slow - slow_l


def kernel(
    n_gx,
    n_gy,
    total_cols,
    classes,
    depth_in,
    mx_in,
    my_in,
    wet_in,
    class_in,
    rates_in,
    dams_in,
    releases_in,
    depth_out,
    adjoint_out,
    grad_out,
    raw_d,
    raw_x,
    raw_y,
    raw_wet,
    raw_cls,
    first,
    second,
    statics,
    faces,
    inflow,
    adj,
    last_h,
    row_flux,
    col_flux,
    col_hot,
    pack_cols,
    send_rows,
    recv_rows,
    send_cols,
    recv_cols,
    recv_corner,
    gpart,
    recv_all,
    rates,
    dams,
    releases,
    small_sem,
    know_sem,
    in_sem,
    edge_send,
    edge_recv,
    grad_send,
    grad_recv,
):
    rows, cols = depth_in.shape
    tiles = cols // LANES
    wide = tiles + 1
    span = rows + 2 * HALO
    chunks = span // 8
    ix, iy = lax.axis_index("gx"), lax.axis_index("gy")
    lane = lax.broadcasted_iota(jnp.int32, (8, LANES), 1)

    has_up, has_down = ix > 0, ix < n_gx - 1
    has_left, has_right = iy > 0, iy < n_gy - 1

    barrier = pltpu.get_barrier_semaphore()
    for step in range(1, n_gy):
        pl.semaphore_signal(
            barrier, inc=1, device_id=(ix, lax.rem(iy + step, n_gy)), device_id_type=MESH
        )
    sides = (
        (has_up, -1, 0),
        (has_down, 1, 0),
        (has_left, 0, -1),
        (has_right, 0, 1),
        (has_up & has_left, -1, -1),
        (has_up & has_right, -1, 1),
        (has_down & has_left, 1, -1),
        (has_down & has_right, 1, 1),
    )
    corners = 0
    for exists, dx, dy in sides[:2] + sides[4:]:
        corners = corners + exists.astype(jnp.int32)

        @pl.when(exists)
        def _(dx=dx, dy=dy):
            pl.semaphore_signal(barrier, inc=1, device_id=(ix + dx, iy + dy), device_id_type=MESH)

    small = [
        pltpu.make_async_copy(source, target, small_sem.at[index])
        for index, (source, target) in enumerate(
            ((rates_in, rates), (dams_in, dams), (releases_in, releases))
        )
    ]
    for copy in small[:1]:
        copy.start()
    loads = []
    for c in (0, tiles - 1, *range(1, tiles - 1)):
        for index, (source, target) in enumerate(
            ((wet_in, raw_wet), (class_in, raw_cls), (depth_in, raw_d), (mx_in, raw_x), (my_in, raw_y))
        ):
            copy = pltpu.make_async_copy(
                source.at[:, pl.ds(c * LANES, LANES)], target.at[c], in_sem.at[index, c]
            )
            copy.start()
            loads.append(copy)
    for copy in small[1:]:
        copy.start()

    for copy in loads:
        copy.wait()
    small[0].wait()

    rate = [rates[k] for k in range(classes)]

    def coded_chunk(c, start, size=8):
        at = (c, pl.ds(start, size), slice(None))
        wet = raw_wet[at] > 0
        cls = raw_cls[at]
        weight = jnp.full(cls.shape, rate[0])
        for k in range(1, classes):
            weight = jnp.where(cls == k, rate[k], weight)
        return (
            jnp.where(wet, raw_d[at], -1.0),
            raw_x[at],
            raw_y[at],
            jnp.where(wet, weight, 0.0),
        )

    for c in range(tiles):
        for side, start, pick in ((0, 0, 0), (1, rows - 8, 4)):
            four = coded_chunk(c, start)
            for k in range(4):
                send_rows[side, c, 4 * k : 4 * k + 4, :] = four[k][pick : pick + 4]

    def pack_body(i, carry):
        start = pl.multiple_of(i * 8, 8)
        left = coded_chunk(0, start)
        right = coded_chunk(tiles - 1, start)
        packed = jnp.zeros((8, LANES), jnp.float32)
        for k in range(4):
            mine = (lane >= 4 * k) & (lane < 4 * k + 4)
            packed = jnp.where(mine, pltpu.roll(left[k], 4 * k, 1) if k else left[k], packed)
            mine = (lane >= 16 + 4 * k) & (lane < 20 + 4 * k)
            packed = jnp.where(mine, pltpu.roll(right[k], 20 + 4 * k, 1), packed)
        pack_cols[pl.ds(start, 8), :] = packed
        return carry

    lax.fori_loop(0, rows // 8, pack_body, 0, unroll=2)
    turned = jnp.transpose(pack_cols[...])
    send_cols[0] = turned[0:16]
    send_cols[1] = turned[16:32]

    pl.semaphore_wait(barrier, (n_gy - 1) + corners)

    rounds = (n_gx - 1).bit_length()

    def reach(level):
        return (ix >= 2**level, -(2**level)), (ix + 2**level < n_gx, 2**level)

    def tell(level):
        for exists, offset in reach(level):

            @pl.when(exists)
            def _(offset=offset):
                pl.semaphore_signal(
                    know_sem.at[level], inc=1, device_id=(ix + offset, iy), device_id_type=MESH
                )

    def learn(level):
        pl.semaphore_wait(
            know_sem.at[level], sum(exists.astype(jnp.int32) for exists, _ in reach(level))
        )

    def edge_copy(index):
        _, dx, dy = sides[index]
        opposite = (1, 0, 3, 2, 7, 6, 5, 4)[index]
        if index < 2:
            source, target = send_rows.at[index], recv_rows.at[opposite]
        elif index < 4:
            source, target = send_cols.at[index - 2], recv_cols.at[opposite - 2]
        else:
            first = 0 if index < 6 else rows - 8
            source, target = pack_cols.at[pl.ds(first, 8), :], recv_corner.at[opposite - 4]
        return pltpu.make_async_remote_copy(
            src_ref=source,
            dst_ref=target,
            send_sem=edge_send.at[index],
            recv_sem=edge_recv.at[opposite],
            device_id=(ix + dx, iy + dy),
            device_id_type=MESH,
        )

    for index in (4, 5, 6, 7, 0, 1, 2, 3):

        @pl.when(sides[index][0])
        def _(index=index):
            edge_copy(index).start()

    if rounds > 0:
        tell(0)

    H, MX, MY, LMX, LPX, LMY, LPY, PX, RX, PY, RY = range(11)
    IH = 11
    QX, QY, TT, AX, AY, UV, WX, WY, BX, BY = range(11, 21)
    NEXT = 21
    WET, WGT, FMX, FMY = range(4)
    ALPHA, BETA, GAMMA, SLOW, FAST, ESLOW, EFAST = range(7)

    def put_start(c, at_rows, size, four):
        wet = four[0] > 0.0
        at = (c, pl.ds(at_rows, size), slice(None))
        first[(H,) + at] = jnp.where(wet, four[0], 1.0)
        first[(MX,) + at] = jnp.where(wet, four[1], 0.0)
        first[(MY,) + at] = jnp.where(wet, four[2], 0.0)
        statics[(WGT,) + at] = jnp.where(wet, four[3], 0.0)
        statics[(WET,) + at] = jnp.where(wet, 1.0, 0.0)

    def own_body(i, carry):
        start = pl.multiple_of(i * 8, 8)
        for c in range(tiles):
            put_start(c, start + OWN, 8, coded_chunk(c, start))
        return carry

    lax.fori_loop(0, rows // 8, own_body, 0)

    for copy in small[1:]:
        copy.wait()
    cell = dams[...]
    if total_cols & (total_cols - 1) == 0:
        dam_row = lax.shift_right_logical(cell, total_cols.bit_length() - 1)
    else:
        dam_row = lax.div(cell, total_cols)
    dam_col = cell - dam_row * total_cols
    dam_count = cell.shape[1]
    local_row = dam_row - ix * rows
    local_col = dam_col - iy * cols
    amounts = INFLOW_GAIN * releases[...]
    thrice = lambda values: jnp.concatenate([values] * 3, axis=1)
    amounts = jnp.concatenate(
        [part.astype(jnp.float32) for part in three_parts(amounts)], axis=1
    )
    wide_row = lax.broadcasted_iota(jnp.int32, (span, 3 * dam_count), 0) - HALO
    row_hot = wide_row == thrice(local_row)
    gain_rows = jnp.concatenate(
        [jnp.where(row_hot, amounts[s : s + 1], 0.0) for s in range(2)], axis=0
    ).astype(jnp.bfloat16)
    position = lax.broadcasted_iota(jnp.int32, (LANES, 3 * dam_count), 0)
    col_thrice = thrice(local_col)
    hots = []
    for c in range(wide):
        if c < tiles:
            column = position + c * LANES
        else:
            column = jnp.where(
                position < HALO,
                position + cols,
                jnp.where(position >= LANES - HALO, position - LANES, -2 * LANES),
            )
        hot = (column == col_thrice).astype(jnp.float32).astype(jnp.bfloat16)
        if c < tiles:
            col_hot[c * LANES : (c + 1) * LANES, :] = hot[:, :dam_count]
        hots.append(hot)
    poured = lax.dot_general(
        gain_rows, jnp.concatenate(hots, axis=0), (((1,), (1,)), ((), ())),
        preferred_element_type=jnp.float32,
    )
    for s in range(2):
        for c in range(wide):
            inflow[s, c, TOP : TOP + span, :] = poured[
                s * span : (s + 1) * span, c * LANES : (c + 1) * LANES
            ]

    def turned(get, cs, shift, step):
        needed = sorted({c for c in cs} | {(c + step) % wide for c in cs})
        values = {c: pltpu.roll(get(c), shift, 1) for c in needed}
        edge = LANES - 1 if step > 0 else 0
        return {c: jnp.where(lane == edge, values[(c + step) % wide], values[c]) for c in cs}

    def next_lanes(values, cs=None):
        cs = range(wide) if cs is None else cs
        return list(turned(lambda c: values[c], cs, LANES - 1, 1).values())

    def last_lanes(values):
        return list(turned(lambda c: values[c], range(wide), 1, -1).values())

    FIRST_NEXT = (H, MX, MY, LMY, LPY, QY, TT, AY, UV, PY, RY)
    SECOND_NEXT = (H, MY, LMY, LPY, PY, RY, IH)
    SECOND_AT = 12

    def base_prims(h, mx, my, ih):
        ux, uy = mx * ih, my * ih
        squared = GRAVITY * h
        cc = squared * lax.rsqrt(squared)
        half = 0.5 * cc
        out = {H: h, MX: mx, MY: my, LMX: ux - cc, LPX: ux + cc, LMY: uy - cc, LPY: uy + cc}
        half_i, ux_i, uy_i = half * ih, ux * ih, uy * ih
        out |= {PX: half_i - ux_i, RX: half_i + ux_i, PY: half_i - uy_i, RY: half_i + uy_i}
        return out, ux, uy, squared, cc, half

    def reader(source, keys, offset):
        def at(k, c, rows_at):
            return source[k, c, rows_at, :]

        def right(k, c, rows_at):
            return source[offset + keys.index(k), c, rows_at, :]

        return at, right

    f_at, f_right = reader(first, FIRST_NEXT, NEXT)
    s_at, s_right = reader(second, SECOND_NEXT, SECOND_AT)

    def face(step, dim, c, here, lm_l, lm_r, lp_l, lp_r):
        low, high = jnp.minimum(lm_l, lm_r), jnp.maximum(lp_l, lp_r)
        slow, fast = jnp.minimum(low, 0.0), jnp.maximum(high, 0.0)
        inverse = 1.0 / (fast - slow)
        masked = statics[FMX + dim, c, here, :] * inverse
        alpha, beta = fast * masked, slow * masked
        gamma = slow * alpha
        e_slow = halved_on_tie(alpha * inverse, low < 0.0, low == 0.0)
        e_fast = halved_on_tie(beta * inverse, high > 0.0, high == 0.0)
        for k, value in enumerate((alpha, beta, gamma, slow, fast, e_slow, e_fast)):
            faces[step, dim, k, c, here, :] = value
        return alpha, beta, gamma

    def coefs_of(step, dim, c, here):
        return [faces[step, dim, k, c, here, :] for k in range(7)]

    def crossing(coefs, flux_l, flux_r, held_l, held_r):
        alpha, beta, gamma = coefs
        return alpha * flux_l - beta * flux_r + gamma * (held_r - held_l)

    def net_of(k, here):
        values = [col_flux[k, c, here, :] for c in range(wide)]
        return [mine - entering for mine, entering in zip(values, last_lanes(values))]

    RIGHT, LEFT = 0, 1
    EVERY = tuple(range(wide))

    def shift_stage(rights, lefts):
        def shift(row):
            here = pl.ds(row + TOP, 8)

            def wet_at(c):
                return statics[WET, c, here, :]

            for c, value in turned(wet_at, rights, LANES - 1, 1).items():
                adj[RIGHT, c, here, :] = value
            for c, value in turned(wet_at, lefts, 1, -1).items():
                adj[LEFT, c, here, :] = value
            for j, k in enumerate((H, MX, MY)):
                shifted = turned(lambda c, k=k: first[k, c, here, :], rights, LANES - 1, 1)
                for c, value in shifted.items():
                    first[NEXT + j, c, here, :] = value

        return shift

    def walls_of(scale, lower, upper, u, n, q, a, cc, half):
        single = scale * (lower - upper)
        both = scale * (2.0 - (lower + upper))
        size = jnp.abs(u)
        return single * q + both * ((size + cc) * n), single * a + both * (u * (half - size))

    def static_x(c, start):
        here = pl.ds(start, 8)
        scale = TIME_RATIO * statics[WET, c, here, :]
        above = statics[WET, c, pl.ds(start - 1, 8), :]
        below = statics[WET, c, pl.ds(start + 1, 8), :]
        statics[FMX, c, here, :] = scale * below
        h, mx, my = (first[k, c, here, :] for k in (H, MX, MY))
        out, ux, uy, squared, cc, half = base_prims(h, mx, my, 1.0 / h)
        pressure = 0.5 * squared * h
        out[QX], out[QY], out[TT] = mx * ux + pressure, my * uy + pressure, mx * uy
        out[AX], out[AY], out[UV] = squared - ux * ux, squared - uy * uy, ux * uy
        out[WX], out[BX] = walls_of(scale, above, below, ux, mx, out[QX], out[AX], cc, half)
        for k, value in out.items():
            if k not in (H, MX, MY):
                first[k, c, here, :] = value
        return uy, my, out[QY], out[AY], cc, half

    def static_y(c, here, parts=None):
        scale = TIME_RATIO * statics[WET, c, here, :]
        if parts is None:
            h, my = first[H, c, here, :], first[MY, c, here, :]
            squared = GRAVITY * h
            cc = squared * lax.rsqrt(squared)
            parts = my * (1.0 / h), my, first[QY, c, here, :], first[AY, c, here, :], cc, 0.5 * cc
        first[WY, c, here, :], first[BY, c, here, :] = walls_of(
            scale, adj[LEFT, c, here, :], adj[RIGHT, c, here, :], *parts
        )

    def static_next(c, here):
        scale = TIME_RATIO * statics[WET, c, here, :]
        statics[FMY, c, here, :] = scale * adj[RIGHT, c, here, :]
        h, mx, my = (first[NEXT + k, c, here, :] for k in range(3))
        out, ux, uy, squared, cc, half = base_prims(h, mx, my, 1.0 / h)
        out[QY], out[TT] = my * uy + 0.5 * squared * h, mx * uy
        out[AY], out[UV] = squared - uy * uy, ux * uy
        for j, k in enumerate(FIRST_NEXT):
            if j >= 3:
                first[NEXT + j, c, here, :] = out[k]

    def static_stage(xs, ys, nexts):
        def static(row):
            start = row + TOP
            here = pl.ds(start, 8)
            for c in range(wide):
                parts = static_x(c, start) if c in xs else None
                if c in ys:
                    static_y(c, here, parts)
                if c in nexts:
                    static_next(c, here)

        return static

    def first_faces(cols_at, rows_at):
        def faces_of(row):
            start = row + TOP
            here, after = pl.ds(start, 8), pl.ds(start + 1, 8)
            for c in cols_at:
                coefs = face(
                    0, 1, c, here, f_at(LMY, c, here), f_right(LMY, c, here),
                    f_at(LPY, c, here), f_right(LPY, c, here),
                )
                for k, (flux, held) in enumerate(((MY, H), (TT, MX), (QY, MY))):
                    col_flux[k, c, here, :] = crossing(
                        coefs, f_at(flux, c, here), f_right(flux, c, here),
                        f_at(held, c, here), f_right(held, c, here),
                    )
            for c in rows_at:
                coefs = face(
                    0, 0, c, here, f_at(LMX, c, here), f_at(LMX, c, after),
                    f_at(LPX, c, here), f_at(LPX, c, after),
                )
                for k, (flux, held) in enumerate(((MX, H), (QX, MX), (TT, MY))):
                    row_flux[k, c, here, :] = crossing(
                        coefs, f_at(flux, c, here), f_at(flux, c, after),
                        f_at(held, c, here), f_at(held, c, after),
                    )

        return faces_of

    inner, own_tiles = EVERY[: tiles - 1], EVERY[:tiles]
    shift_inner = shift_stage(inner, EVERY[1:tiles])
    static_inner = static_stage(own_tiles, EVERY[1 : tiles - 1], inner)
    faces_inner = first_faces(inner, own_tiles)

    def plain(stage):
        return lambda row, index: stage(row)

    pipeline((plain(shift_inner), plain(static_inner)), 1, chunks - 1, G_STATIC)
    pipeline((plain(faces_inner),), 1, chunks - 2, G_FACES)

    for index in range(8):

        @pl.when(sides[index][0])
        def _(index=index):
            copy = edge_copy(index)
            copy.wait_send()
            opposite = (1, 0, 3, 2, 7, 6, 5, 4)[index]
            if index < 2:
                target = recv_rows.at[index]
            elif index < 4:
                target = recv_cols.at[index - 2]
            else:
                target = recv_corner.at[index - 4]
            pltpu.make_async_copy(target, target, edge_recv.at[index]).wait()

    if rounds > 0:
        learn(0)
        if rounds > 1:
            tell(1)

    for c in range(tiles):
        for side, exists, at_rows in ((0, has_up, TOP), (1, has_down, OWN + rows)):
            four = [recv_rows[side, c, 4 * k : 4 * k + 4, :] for k in range(4)]
            four[0] = jnp.where(exists, four[0], -1.0)
            put_start(c, at_rows, 4, four)

    halves = jnp.concatenate(
        [recv_cols[0], recv_cols[1], jnp.zeros((LANES - 32, rows), jnp.float32)], axis=0
    )
    pack_cols[...] = jnp.transpose(halves)

    def rim_tile(left_part, right_part, k, left_at, right_at, from_left, from_right):
        fill = -1.0 if k == 0 else 0.0
        on_right = (lane < HALO) & from_right
        on_left = (lane >= LANES - HALO) & from_left
        shift_r = (LANES - right_at - 4 * k) % LANES
        shift_l = (LANES - HALO - left_at - 4 * k) % LANES
        right_val = pltpu.roll(right_part, shift_r, 1) if shift_r else right_part
        left_val = pltpu.roll(left_part, shift_l, 1) if shift_l else left_part
        return jnp.where(on_right, right_val, jnp.where(on_left, left_val, fill))

    def rim_body(i, carry):
        start = pl.multiple_of(i * 8, 8)
        part = pack_cols[pl.ds(start, 8), :]
        four = [rim_tile(part, part, k, 0, 16, has_left, has_right) for k in range(4)]
        put_start(tiles, start + OWN, 8, four)
        return carry

    lax.fori_loop(0, rows // 8, rim_body, 0, unroll=2)
    for left_slot, right_slot, exists, at_rows, pick in (
        (0, 1, has_up, TOP, 4),
        (2, 3, has_down, OWN + rows, 0),
    ):
        four = [
            rim_tile(
                recv_corner[left_slot],
                recv_corner[right_slot],
                k,
                16,
                0,
                has_left & exists,
                has_right & exists,
            )[pick : pick + 4]
            for k in range(4)
        ]
        put_start(tiles, at_rows, 4, four)

    shift_whole, shift_outer = shift_stage(EVERY, EVERY), shift_stage(EVERY[tiles - 1 :], (0, tiles))
    static_whole = static_stage(EVERY, EVERY, EVERY)
    static_outer = static_stage(EVERY[tiles:], (0, *EVERY[tiles - 1 :]), EVERY[tiles - 1 :])
    faces_whole, faces_outer = first_faces(EVERY, EVERY), first_faces(EVERY[tiles - 1 :], EVERY[tiles:])

    def chosen(whole_stage, outer_stage, last_inner):
        def stage(row, index):
            inside = index is None or 1 <= index <= last_inner
            (outer_stage if inside else whole_stage)(row)

        return stage

    pipeline(
        (
            chosen(shift_whole, shift_outer, chunks - 2),
            chosen(static_whole, static_outer, chunks - 2),
        ),
        0, chunks, G_OUTER, begin=2, end=chunks - 1,
    )

    def first_cells(row):
        start = row + TOP
        here, before = pl.ds(start, 8), pl.ds(start - 1, 8)
        net = [net_of(k, here) for k in range(3)]
        for c in range(wide):
            new = []
            for k in range(3):
                value = row_flux[k, c, here, :]
                change = value - row_flux[k, c, before, :] + net[k][c]
                if k > 0:
                    change = change + f_at((None, WX, WY)[k], c, here)
                new.append(f_at((H, MX, MY)[k], c, here) - change)
            h = new[0] + inflow[0, c, here, :]
            ih = 1.0 / h
            out = base_prims(h, new[1], new[2], ih)[0]
            out[IH] = ih
            for k, value in out.items():
                second[k, c, here, :] = value

    def first_shift(row):
        here = pl.ds(row + TOP, 8)
        heights = next_lanes([second[H, c, here, :] for c in range(wide)])
        flows = next_lanes([second[MY, c, here, :] for c in range(wide)])
        for c, (h, n) in enumerate(zip(heights, flows)):
            ih = 1.0 / h
            out = base_prims(h, n, n, ih)[0]
            out[IH] = ih
            for j, k in enumerate(SECOND_NEXT):
                second[SECOND_AT + j, c, here, :] = out[k]

    TERM, ADJ, ZX, ZY, TERM_R, ADJ_R, ZX_R, ZY_R = range(8)

    def last_cols(row):
        here = pl.ds(row + TOP, 8)
        for c in range(wide):
            coefs = face(
                1, 1, c, here, s_at(LMY, c, here), s_right(LMY, c, here),
                s_at(LPY, c, here), s_right(LPY, c, here),
            )
            col_flux[0, c, here, :] = crossing(
                coefs, s_at(MY, c, here), s_right(MY, c, here),
                s_at(H, c, here), s_right(H, c, here),
            )

    def last_cells(row):
        start = row + TOP
        here, after, before = pl.ds(start, 8), pl.ds(start + 1, 8), pl.ds(start - 1, 8)
        net = net_of(0, here)
        for c in range(wide):
            coefs = face(
                1, 0, c, here, s_at(LMX, c, here), s_at(LMX, c, after),
                s_at(LPX, c, here), s_at(LPX, c, after),
            )
            value = crossing(
                coefs, s_at(MX, c, here), s_at(MX, c, after),
                s_at(H, c, here), s_at(H, c, after),
            )
            row_flux[0, c, here, :] = value
            change = value - row_flux[0, c, before, :] + net[c]
            h = s_at(H, c, here) - change + inflow[1, c, here, :]
            last_h[c, here, :] = h
            adj[TERM, c, here, :] = statics[WGT, c, here, :] * h

    def adj_shift(*planes):
        def shift(row):
            here = pl.ds(row + TOP, 8)
            for k in planes:
                values = [adj[k, c, here, :] for c in range(wide)]
                for c, value in enumerate(next_lanes(values)):
                    adj[TERM_R + k, c, here, :] = value

        return shift

    pipeline(
        (chosen(faces_whole, faces_outer, chunks - 3), plain(first_cells), plain(first_shift)),
        0, chunks, G_FIRST, begin=3, end=chunks - 2,
    )
    if rounds > 1:
        learn(1)
        if rounds > 2:
            tell(2)
    pipeline((plain(last_cols), plain(last_cells), plain(adj_shift(TERM))), 0, chunks, G_LAST)

    def depth_body(i, carry):
        start = pl.multiple_of(i * 8, 8)
        for c in range(tiles):
            own = pl.ds(start + OWN, 8)
            depth_out[pl.ds(start, 8), c * LANES : (c + 1) * LANES] = jnp.where(
                statics[WET, c, own, :] > 0.0, last_h[c, own, :], raw_d[c, pl.ds(start, 8), :]
            )
        return carry

    lax.fori_loop(0, rows // 8, depth_body, 0)
    def last_face(coefs, lm, lp, h, n, z, p, r, ih):
        alpha, beta, gamma = coefs[:3]
        gh = z[1] - z[0]
        fast_l, slow_l, fast_r, slow_r = split_speed_grads(
            *lm, *lp, coefs, gh * (n[1] - n[0]), gh * (h[1] - h[0])
        )
        jump = gamma * gh
        return (
            fast_l * p[0] - slow_l * r[0] - jump,
            alpha * gh + (fast_l + slow_l) * ih[0],
        ), (
            fast_r * p[1] - slow_r * r[1] + jump,
            (fast_r + slow_r) * ih[1] - beta * gh,
        )

    def back_cols(row):
        here = pl.ds(row + TOP, 8)
        for c in range(wide):

            def pair(k):
                return s_at(k, c, here), s_right(k, c, here)

            left, right = last_face(
                coefs_of(1, 1, c, here), pair(LMY), pair(LPY), pair(H), pair(MY),
                (adj[TERM, c, here, :], adj[TERM_R, c, here, :]), pair(PY), pair(RY), pair(IH),
            )
            for k in range(2):
                col_flux[k, c, here, :] = left[k]
                col_flux[2 + k, c, here, :] = right[k]

    def back_cells(row):
        start = row + TOP
        here, after, before = pl.ds(start, 8), pl.ds(start + 1, 8), pl.ds(start - 1, 8)
        entering = [
            last_lanes([col_flux[2 + k, c, here, :] for c in range(wide)]) for k in range(2)
        ]
        for c in range(wide):

            def pair(k):
                return s_at(k, c, here), s_at(k, c, after)

            left, right = last_face(
                coefs_of(1, 0, c, here), pair(LMX), pair(LPX), pair(H), pair(MX),
                (adj[TERM, c, here, :], adj[TERM, c, after, :]), pair(PX), pair(RX), pair(IH),
            )
            in_x = []
            for k in range(2):
                row_flux[k, c, here, :] = right[k]
                in_x.append(left[k] + row_flux[k, c, before, :])
            in_y = [col_flux[k, c, here, :] + entering[k][c] for k in range(2)]
            adj[ADJ, c, here, :] = adj[TERM, c, here, :] + (in_x[0] + in_y[0])
            adj[ZX, c, here, :] = in_x[1]
            adj[ZY, c, here, :] = in_y[1]

    pipeline(
        (plain(back_cols), plain(back_cells), plain(adj_shift(ADJ, ZX, ZY))),
        0, chunks, G_BACK_LAST,
    )

    own_hot = lax.broadcasted_iota(jnp.int32, (rows, dam_count), 0) == local_row
    stacked = []
    for plane in (ADJ, TERM):
        parts = [three_parts(adj[plane, c, OWN : OWN + rows, :]) for c in range(tiles)]
        stacked.append(
            jnp.concatenate([parts[c][k] for k in range(3) for c in range(tiles)], axis=1)
        )
    picked = lax.dot_general(
        jnp.concatenate(stacked, axis=0), jnp.concatenate([col_hot[...]] * 3, axis=0),
        (((1,), (0,)), ((), ())), preferred_element_type=jnp.float32,
    )
    gpart[...] = jnp.concatenate(
        [
            INFLOW_GAIN * jnp.sum(
                jnp.where(own_hot, picked[s * rows : (s + 1) * rows], 0.0), axis=0, keepdims=True
            )
            for s in range(2)
        ],
        axis=1,
    )

    for level in range(2, rounds):
        learn(level)
        if level + 1 < rounds:
            tell(level + 1)

    count = n_gx * n_gy

    def send_grads(k, carry):
        to = lax.rem(ix * n_gy + iy + 1 + k, count)
        pltpu.make_async_remote_copy(
            src_ref=gpart,
            dst_ref=recv_all.at[k],
            send_sem=grad_send.at[0],
            recv_sem=grad_recv.at[0],
            device_id=(lax.div(to, n_gy), lax.rem(to, n_gy)),
            device_id_type=MESH,
        ).start()
        return carry

    lax.fori_loop(0, count - 1, send_grads, 0)

    def first_face(coefs, lm, lp, h, n, t, q, v, zh, zn, zt, a, uv, p, r):
        alpha, beta, gamma = coefs[:3]
        gh, gn, gt = zh[1] - zh[0], zn[1] - zn[0], zt[1] - zt[0]
        dn = n[1] - n[0]
        fast_l, slow_l, fast_r, slow_r = split_speed_grads(
            *lm, *lp, coefs,
            gh * dn + gn * (q[1] - q[0]) + gt * (v[1] - v[0]),
            gh * (h[1] - h[0]) + gn * dn + gt * (t[1] - t[0]),
        )
        jump = gamma * gh
        return (
            alpha * (gn * a[0] - gt * uv[0]) + (fast_l * p[0] - slow_l * r[0]) - jump,
            (fast_r * p[1] - slow_r * r[1]) - beta * (gn * a[1] - gt * uv[1]) + jump,
        )

    def first_row_face(c, start):
        here, after = pl.ds(start, 8), pl.ds(start + 1, 8)

        def pair(k):
            return f_at(k, c, here), f_at(k, c, after)

        def z_pair(k):
            return adj[k, c, here, :], adj[k, c, after, :]

        return first_face(
            coefs_of(0, 0, c, here), pair(LMX), pair(LPX), pair(H), pair(MX), pair(MY), pair(QX),
            pair(TT), z_pair(ADJ), z_pair(ZX), z_pair(ZY), pair(AX), pair(UV), pair(PX), pair(RX),
        )

    for c in range(tiles):
        row_flux[0, c, pl.ds(OWN - 8, 8), :] = first_row_face(c, OWN - 8)[1]

    def backward_first(row):
        start = row + OWN
        here, before = pl.ds(start, 8), pl.ds(start - 1, 8)

        def col_face(c):
            def pair(k):
                return f_at(k, c, here), f_right(k, c, here)

            def z_pair(k):
                return adj[k, c, here, :], adj[k + TERM_R - TERM, c, here, :]

            return first_face(
                coefs_of(0, 1, c, here), pair(LMY), pair(LPY), pair(H), pair(MY), pair(MX),
                pair(QY), pair(TT), z_pair(ADJ), z_pair(ZY), z_pair(ZX), pair(AY), pair(UV),
                pair(PY), pair(RY),
            )

        current = pltpu.roll(col_face(wide - 1)[1], 1, 1)
        for c in range(tiles):
            left, right = first_row_face(c, start)
            row_flux[0, c, here, :] = right
            left_y, right_y = col_face(c)
            current, last = pltpu.roll(right_y, 1, 1), current
            entering = jnp.where(lane == 0, last, current)
            across = left + row_flux[0, c, before, :] + (left_y + entering)
            walls = adj[ZX, c, here, :] * f_at(BX, c, here) + adj[ZY, c, here, :] * f_at(BY, c, here)
            adjoint_out[pl.ds(row, 8), c * LANES : (c + 1) * LANES] = (
                adj[ADJ, c, here, :] + across - walls
            )

    sweep(backward_first, 0, rows // 8, G_BACK_FIRST)

    for sem in (grad_send, grad_recv):
        pltpu.make_async_copy(recv_all, recv_all, sem.at[0]).wait()
    total = gpart[...] + jnp.sum(recv_all[...], axis=0)
    for s in range(2):
        grad_out[s : s + 1, :] = total[:, s * dam_count : (s + 1) * dam_count]


def place(*refs):
    sources, targets, sem = refs[:3], refs[3:6], refs[6]
    copies = [
        pltpu.make_async_copy(source, target, sem.at[k])
        for k, (source, target) in enumerate(zip(sources, targets))
    ]
    for copy in copies:
        copy.start()
    for copy in copies:
        copy.wait()


def on_device(
    n_gx,
    n_gy,
    water_depth,
    momentum_x,
    momentum_y,
    wet_mask,
    damage_class,
    damage_rates,
    dam_cell,
    releases,
):
    rows, cols = water_depth.shape
    tiles = cols // LANES
    wide = tiles + 1
    high = rows + 2 * HALO + 2 * TOP
    dam_count = dam_cell.shape[0]
    f32 = jnp.float32
    plane = (wide, high, LANES)
    own = (tiles, rows, LANES)
    anywhere = pl.BlockSpec(memory_space=pl.ANY)
    vmem = pl.BlockSpec(memory_space=pltpu.VMEM)
    dma = pltpu.SemaphoreType.DMA
    results = pl.pallas_call(
        functools.partial(kernel, n_gx, n_gy, cols * n_gy, damage_rates.shape[0]),
        out_shape=(
            pltpu.VMEM((rows, cols), f32),
            pltpu.VMEM((rows, cols), f32),
            pltpu.VMEM(releases.shape[::-1], f32),
        ),
        in_specs=[anywhere] * 8,
        out_specs=(vmem, vmem, vmem),
        scratch_shapes=[
            pltpu.VMEM(own, f32),
            pltpu.VMEM(own, f32),
            pltpu.VMEM(own, f32),
            pltpu.VMEM(own, jnp.int32),
            pltpu.VMEM(own, jnp.int32),
            pltpu.VMEM((32,) + plane, f32),
            pltpu.VMEM((19,) + plane, f32),
            pltpu.VMEM((4,) + plane, f32),
            pltpu.VMEM((2, 2, 7) + plane, f32),
            pltpu.VMEM((2,) + plane, f32),
            pltpu.VMEM((8,) + plane, f32),
            pltpu.VMEM(plane, f32),
            pltpu.VMEM((3,) + plane, f32),
            pltpu.VMEM((4,) + plane, f32),
            pltpu.VMEM((cols, dam_count), jnp.bfloat16),
            pltpu.VMEM((rows, LANES), f32),
            pltpu.VMEM((2, tiles, 16, LANES), f32),
            pltpu.VMEM((2, tiles, 16, LANES), f32),
            pltpu.VMEM((2, 16, rows), f32),
            pltpu.VMEM((2, 16, rows), f32),
            pltpu.VMEM((4, 8, LANES), f32),
            pltpu.VMEM((1, 2 * dam_count), f32),
            pltpu.VMEM((n_gx * n_gy - 1, 1, 2 * dam_count), f32),
            pltpu.SMEM(damage_rates.shape, f32),
            pltpu.VMEM((1, dam_count), jnp.int32),
            pltpu.VMEM(releases.shape[::-1], f32),
            dma((3,)),
            pltpu.SemaphoreType.REGULAR((max((n_gx - 1).bit_length(), 1),)),
            dma((5, tiles)),
            dma((8,)),
            dma((8,)),
            dma((1,)),
            dma((1,)),
        ],
        compiler_params=pltpu.CompilerParams(
            collective_id=0, has_side_effects=True, vmem_limit_bytes=56 * 1024 * 1024
        ),
        name="window",
    )(
        water_depth,
        momentum_x,
        momentum_y,
        wet_mask,
        damage_class,
        damage_rates,
        dam_cell.reshape(1, dam_count),
        releases.T,
    )
    final_depth, adjoint, grad = pl.pallas_call(
        place,
        out_shape=tuple(jax.ShapeDtypeStruct(value.shape, f32) for value in results),
        in_specs=[vmem] * 3,
        out_specs=(anywhere,) * 3,
        scratch_shapes=[dma((3,))],
        name="place",
    )(*(pltpu.with_memory_space_constraint(value, pltpu.VMEM) for value in results))
    return final_depth, adjoint, grad.T


def solution(mesh):
    n_gx, n_gy = mesh.shape["gx"], mesh.shape["gy"]
    grid = P("gx", "gy")
    return jax.shard_map(
        functools.partial(on_device, n_gx, n_gy),
        mesh=mesh,
        in_specs=(grid,) * 5 + (P(),) * 3,
        out_specs=(grid, grid, P()),
        check_vma=False,
    )
```

```python
import functools

import jax
import jax.numpy as jnp
from jax import lax
from jax.experimental import pallas as pl
from jax.experimental.pallas import tpu as pltpu
from jax.sharding import PartitionSpec as P

GRAVITY = 9.81
TIME_RATIO = 0.05
INFLOW_GAIN = 0.25
HALO = 4
LANES = 128
TOP = 8
OWN = TOP + HALO
G_STATIC, G_FACES, G_OUTER, G_FIRST, G_LAST, G_BACK_LAST, G_BACK_FIRST = 2, 2, 2, 3, 5, 3, 1
MESH = pl.DeviceIdType.MESH


def sweep(body, first, last, group):
    whole = (last - first) // group

    def run(i, carry):
        base = pl.multiple_of(i * (8 * group), 8)
        for j in range(group):
            body(base + 8 * (first + j))
        return carry

    lax.fori_loop(0, whole, run, 0)
    for chunk in range(first + whole * group, last):
        body(8 * chunk)


def pipeline(stages, first, last, group=1, begin=None, end=None):
    depth = len(stages)
    begin = first + depth - 1 if begin is None else begin
    end = last if end is None else end

    def step(at, index=None):
        for k in reversed(range(depth)):
            if index is None:
                stages[k](at - 8 * k, None)
            elif first <= index - k < last:
                stages[k](at - 8 * k, index - k)

    for index in range(first, begin):
        step(8 * index, index)
    whole = (end - begin) // group

    def run(i, carry):
        base = pl.multiple_of(i * (8 * group), 8)
        for j in range(group):
            step(base + 8 * (begin + j))
        return carry

    lax.fori_loop(0, whole, run, 0)
    for index in range(begin + whole * group, last + depth - 1):
        step(8 * index, index)


def three_parts(values):
    parts = []
    for _ in range(3):
        part = values.astype(jnp.bfloat16)
        values = values - part.astype(jnp.float32)
        parts.append(part)
    return parts


def halved_on_tie(value, picks, ties):
    return jnp.where(picks, value, jnp.where(ties, 0.5 * value, 0.0))


def split_speed_grads(lm_l, lm_r, lp_l, lp_r, coefs, d_term, k_term):
    _, _, _, slow, fast, e_slow, e_fast = coefs
    g_slow = e_slow * (fast * k_term - d_term)
    g_fast = e_fast * (d_term - slow * k_term)
    slow_l = halved_on_tie(g_slow, lm_l < lm_r, lm_l == lm_r)
    fast_l = halved_on_tie(g_fast, lp_l > lp_r, lp_l == lp_r)
    return fast_l, slow_l, g_fast - fast_l, g_slow - slow_l


def kernel(
    n_gx,
    n_gy,
    total_cols,
    classes,
    depth_in,
    mx_in,
    my_in,
    wet_in,
    class_in,
    rates_in,
    dams_in,
    releases_in,
    depth_out,
    adjoint_out,
    grad_out,
    raw_d,
    raw_x,
    raw_y,
    raw_wet,
    raw_cls,
    first,
    second,
    statics,
    faces,
    inflow,
    adj,
    last_h,
    row_flux,
    col_flux,
    col_hot,
    pack_cols,
    send_rows,
    recv_rows,
    send_cols,
    recv_cols,
    recv_corner,
    gpart,
    recv_all,
    rates,
    dams,
    releases,
    small_sem,
    know_sem,
    in_sem,
    edge_send,
    edge_recv,
    grad_send,
    grad_recv,
):
    rows, cols = depth_in.shape
    tiles = cols // LANES
    wide = tiles + 1
    span = rows + 2 * HALO
    chunks = span // 8
    ix, iy = lax.axis_index("gx"), lax.axis_index("gy")
    lane = lax.broadcasted_iota(jnp.int32, (8, LANES), 1)

    has_up, has_down = ix > 0, ix < n_gx - 1
    has_left, has_right = iy > 0, iy < n_gy - 1

    barrier = pltpu.get_barrier_semaphore()
    for step in range(1, n_gy):
        pl.semaphore_signal(
            barrier, inc=1, device_id=(ix, lax.rem(iy + step, n_gy)), device_id_type=MESH
        )
    sides = (
        (has_up, -1, 0),
        (has_down, 1, 0),
        (has_left, 0, -1),
        (has_right, 0, 1),
        (has_up & has_left, -1, -1),
        (has_up & has_right, -1, 1),
        (has_down & has_left, 1, -1),
        (has_down & has_right, 1, 1),
    )
    corners = 0
    for exists, dx, dy in sides[:2] + sides[4:]:
        corners = corners + exists.astype(jnp.int32)

        @pl.when(exists)
        def _(dx=dx, dy=dy):
            pl.semaphore_signal(barrier, inc=1, device_id=(ix + dx, iy + dy), device_id_type=MESH)

    small = [
        pltpu.make_async_copy(source, target, small_sem.at[index])
        for index, (source, target) in enumerate(
            ((rates_in, rates), (dams_in, dams), (releases_in, releases))
        )
    ]
    for copy in small[:1]:
        copy.start()
    loads = []
    for c in (0, tiles - 1, *range(1, tiles - 1)):
        for index, (source, target) in enumerate(
            ((wet_in, raw_wet), (class_in, raw_cls), (depth_in, raw_d), (mx_in, raw_x), (my_in, raw_y))
        ):
            copy = pltpu.make_async_copy(
                source.at[:, pl.ds(c * LANES, LANES)], target.at[c], in_sem.at[index, c]
            )
            copy.start()
            loads.append(copy)
    for copy in small[1:]:
        copy.start()

    small[0].wait()
    for copy in loads[:10]:
        copy.wait()

    rate = [rates[k] for k in range(classes)]

    def coded_chunk(c, start, size=8):
        at = (c, pl.ds(start, size), slice(None))
        wet = raw_wet[at] > 0
        cls = raw_cls[at]
        weight = jnp.full(cls.shape, rate[0])
        for k in range(1, classes):
            weight = jnp.where(cls == k, rate[k], weight)
        return (
            jnp.where(wet, raw_d[at], -1.0),
            raw_x[at],
            raw_y[at],
            jnp.where(wet, weight, 0.0),
        )

    def pack_body(i, carry):
        start = pl.multiple_of(i * 8, 8)
        left = coded_chunk(0, start)
        right = coded_chunk(tiles - 1, start)
        packed = jnp.zeros((8, LANES), jnp.float32)
        for k in range(4):
            mine = (lane >= 4 * k) & (lane < 4 * k + 4)
            packed = jnp.where(mine, pltpu.roll(left[k], 4 * k, 1) if k else left[k], packed)
            mine = (lane >= 16 + 4 * k) & (lane < 20 + 4 * k)
            packed = jnp.where(mine, pltpu.roll(right[k], 20 + 4 * k, 1), packed)
        pack_cols[pl.ds(start, 8), :] = packed
        return carry

    lax.fori_loop(0, rows // 8, pack_body, 0, unroll=4)
    for copy in loads[10:]:
        copy.wait()
    for c in range(tiles):
        for side, start, pick in ((0, 0, 0), (1, rows - 8, 4)):
            four = coded_chunk(c, start)
            for k in range(4):
                send_rows[side, c, 4 * k : 4 * k + 4, :] = four[k][pick : pick + 4]
    turned = jnp.transpose(pack_cols[...])
    send_cols[0] = turned[0:16]
    send_cols[1] = turned[16:32]

    pl.semaphore_wait(barrier, (n_gy - 1) + corners)

    rounds = (n_gx - 1).bit_length()

    def reach(level):
        return (ix >= 2**level, -(2**level)), (ix + 2**level < n_gx, 2**level)

    def tell(level):
        for exists, offset in reach(level):

            @pl.when(exists)
            def _(offset=offset):
                pl.semaphore_signal(
                    know_sem.at[level], inc=1, device_id=(ix + offset, iy), device_id_type=MESH
                )

    def learn(level):
        pl.semaphore_wait(
            know_sem.at[level], sum(exists.astype(jnp.int32) for exists, _ in reach(level))
        )

    def edge_copy(index):
        _, dx, dy = sides[index]
        opposite = (1, 0, 3, 2, 7, 6, 5, 4)[index]
        if index < 2:
            source, target = send_rows.at[index], recv_rows.at[opposite]
        elif index < 4:
            source, target = send_cols.at[index - 2], recv_cols.at[opposite - 2]
        else:
            first = 0 if index < 6 else rows - 8
            source, target = pack_cols.at[pl.ds(first, 8), :], recv_corner.at[opposite - 4]
        return pltpu.make_async_remote_copy(
            src_ref=source,
            dst_ref=target,
            send_sem=edge_send.at[index],
            recv_sem=edge_recv.at[opposite],
            device_id=(ix + dx, iy + dy),
            device_id_type=MESH,
        )

    for index in (0, 1, 4, 5, 6, 7, 2, 3):

        @pl.when(sides[index][0])
        def _(index=index):
            edge_copy(index).start()

    if rounds > 0:
        tell(0)

    H, MX, MY, LMX, LPX, LMY, LPY, PX, RX, PY, RY = range(11)
    IH = 11
    QX, QY, TT, AX, AY, UV, WX, WY, BX, BY = range(11, 21)
    NEXT = 21
    WET, WGT, FMX, FMY = range(4)
    ALPHA, BETA, GAMMA, SLOW, FAST, ESLOW, EFAST = range(7)

    def put_start(c, at_rows, size, four):
        wet = four[0] > 0.0
        at = (c, pl.ds(at_rows, size), slice(None))
        first[(H,) + at] = jnp.where(wet, four[0], 1.0)
        first[(MX,) + at] = jnp.where(wet, four[1], 0.0)
        first[(MY,) + at] = jnp.where(wet, four[2], 0.0)
        statics[(WGT,) + at] = jnp.where(wet, four[3], 0.0)
        statics[(WET,) + at] = jnp.where(wet, 1.0, 0.0)

    def own_body(i, carry):
        start = pl.multiple_of(i * 8, 8)
        for c in range(tiles):
            put_start(c, start + OWN, 8, coded_chunk(c, start))
        return carry

    lax.fori_loop(0, rows // 8, own_body, 0)

    for copy in small[1:]:
        copy.wait()
    cell = dams[...]
    if total_cols & (total_cols - 1) == 0:
        dam_row = lax.shift_right_logical(cell, total_cols.bit_length() - 1)
    else:
        dam_row = lax.div(cell, total_cols)
    dam_col = cell - dam_row * total_cols
    dam_count = cell.shape[1]
    local_row = dam_row - ix * rows
    local_col = dam_col - iy * cols
    amounts = INFLOW_GAIN * releases[...]
    thrice = lambda values: jnp.concatenate([values] * 3, axis=1)
    amounts = jnp.concatenate(
        [part.astype(jnp.float32) for part in three_parts(amounts)], axis=1
    )
    wide_row = lax.broadcasted_iota(jnp.int32, (span, 3 * dam_count), 0) - HALO
    row_hot = wide_row == thrice(local_row)
    gain_rows = jnp.concatenate(
        [jnp.where(row_hot, amounts[s : s + 1], 0.0) for s in range(2)], axis=0
    ).astype(jnp.bfloat16)
    position = lax.broadcasted_iota(jnp.int32, (LANES, 3 * dam_count), 0)
    col_thrice = thrice(local_col)
    hots = []
    for c in range(wide):
        if c < tiles:
            column = position + c * LANES
        else:
            column = jnp.where(
                position < HALO,
                position + cols,
                jnp.where(position >= LANES - HALO, position - LANES, -2 * LANES),
            )
        hot = (column == col_thrice).astype(jnp.float32).astype(jnp.bfloat16)
        if c < tiles:
            col_hot[c * LANES : (c + 1) * LANES, :] = hot[:, :dam_count]
        hots.append(hot)
    poured = lax.dot_general(
        gain_rows, jnp.concatenate(hots, axis=0), (((1,), (1,)), ((), ())),
        preferred_element_type=jnp.float32,
    )
    for s in range(2):
        for c in range(wide):
            inflow[s, c, TOP : TOP + span, :] = poured[
                s * span : (s + 1) * span, c * LANES : (c + 1) * LANES
            ]

    def turned(get, cs, shift, step):
        needed = sorted({c for c in cs} | {(c + step) % wide for c in cs})
        values = {c: pltpu.roll(get(c), shift, 1) for c in needed}
        edge = LANES - 1 if step > 0 else 0
        return {c: jnp.where(lane == edge, values[(c + step) % wide], values[c]) for c in cs}

    def next_lanes(values, cs=None):
        cs = range(wide) if cs is None else cs
        return list(turned(lambda c: values[c], cs, LANES - 1, 1).values())

    def last_lanes(values):
        return list(turned(lambda c: values[c], range(wide), 1, -1).values())

    FIRST_NEXT = (H, MX, MY, LMY, LPY, QY, TT, AY, UV, PY, RY)
    SECOND_NEXT = (H, MY, LMY, LPY, PY, RY, IH)
    SECOND_AT = 12

    def base_prims(h, mx, my, ih):
        ux, uy = mx * ih, my * ih
        squared = GRAVITY * h
        cc = squared * lax.rsqrt(squared)
        half = 0.5 * cc
        out = {H: h, MX: mx, MY: my, LMX: ux - cc, LPX: ux + cc, LMY: uy - cc, LPY: uy + cc}
        half_i, ux_i, uy_i = half * ih, ux * ih, uy * ih
        out |= {PX: half_i - ux_i, RX: half_i + ux_i, PY: half_i - uy_i, RY: half_i + uy_i}
        return out, ux, uy, squared, cc, half

    def reader(source, keys, offset):
        def at(k, c, rows_at):
            return source[k, c, rows_at, :]

        def right(k, c, rows_at):
            return source[offset + keys.index(k), c, rows_at, :]

        return at, right

    f_at, f_right = reader(first, FIRST_NEXT, NEXT)
    s_at, s_right = reader(second, SECOND_NEXT, SECOND_AT)

    def face(step, dim, c, here, lm_l, lm_r, lp_l, lp_r):
        low, high = jnp.minimum(lm_l, lm_r), jnp.maximum(lp_l, lp_r)
        slow, fast = jnp.minimum(low, 0.0), jnp.maximum(high, 0.0)
        inverse = 1.0 / (fast - slow)
        masked = statics[FMX + dim, c, here, :] * inverse
        alpha, beta = fast * masked, slow * masked
        gamma = slow * alpha
        e_slow = halved_on_tie(alpha * inverse, low < 0.0, low == 0.0)
        e_fast = halved_on_tie(beta * inverse, high > 0.0, high == 0.0)
        for k, value in enumerate((alpha, beta, gamma, slow, fast, e_slow, e_fast)):
            faces[step, dim, k, c, here, :] = value
        return alpha, beta, gamma

    def coefs_of(step, dim, c, here):
        return [faces[step, dim, k, c, here, :] for k in range(7)]

    def crossing(coefs, flux_l, flux_r, held_l, held_r):
        alpha, beta, gamma = coefs
        return alpha * flux_l - beta * flux_r + gamma * (held_r - held_l)

    def net_of(k, here):
        values = [col_flux[k, c, here, :] for c in range(wide)]
        return [mine - entering for mine, entering in zip(values, last_lanes(values))]

    RIGHT, LEFT = 0, 1
    EVERY = tuple(range(wide))

    def shift_stage(rights, lefts):
        def shift(row):
            here = pl.ds(row + TOP, 8)

            def wet_at(c):
                return statics[WET, c, here, :]

            for c, value in turned(wet_at, rights, LANES - 1, 1).items():
                adj[RIGHT, c, here, :] = value
            for c, value in turned(wet_at, lefts, 1, -1).items():
                adj[LEFT, c, here, :] = value
            for j, k in enumerate((H, MX, MY)):
                shifted = turned(lambda c, k=k: first[k, c, here, :], rights, LANES - 1, 1)
                for c, value in shifted.items():
                    first[NEXT + j, c, here, :] = value

        return shift

    def walls_of(scale, lower, upper, u, n, q, a, cc, half):
        single = scale * (lower - upper)
        both = scale * (2.0 - (lower + upper))
        size = jnp.abs(u)
        return single * q + both * ((size + cc) * n), single * a + both * (u * (half - size))

    def static_x(c, start):
        here = pl.ds(start, 8)
        scale = TIME_RATIO * statics[WET, c, here, :]
        above = statics[WET, c, pl.ds(start - 1, 8), :]
        below = statics[WET, c, pl.ds(start + 1, 8), :]
        statics[FMX, c, here, :] = scale * below
        h, mx, my = (first[k, c, here, :] for k in (H, MX, MY))
        out, ux, uy, squared, cc, half = base_prims(h, mx, my, 1.0 / h)
        pressure = 0.5 * squared * h
        out[QX], out[QY], out[TT] = mx * ux + pressure, my * uy + pressure, mx * uy
        out[AX], out[AY], out[UV] = squared - ux * ux, squared - uy * uy, ux * uy
        out[WX], out[BX] = walls_of(scale, above, below, ux, mx, out[QX], out[AX], cc, half)
        for k, value in out.items():
            if k not in (H, MX, MY):
                first[k, c, here, :] = value
        return uy, my, out[QY], out[AY], cc, half

    def static_y(c, here, parts=None):
        scale = TIME_RATIO * statics[WET, c, here, :]
        if parts is None:
            h, my = first[H, c, here, :], first[MY, c, here, :]
            squared = GRAVITY * h
            cc = squared * lax.rsqrt(squared)
            parts = my * (1.0 / h), my, first[QY, c, here, :], first[AY, c, here, :], cc, 0.5 * cc
        first[WY, c, here, :], first[BY, c, here, :] = walls_of(
            scale, adj[LEFT, c, here, :], adj[RIGHT, c, here, :], *parts
        )

    def static_next(c, here):
        scale = TIME_RATIO * statics[WET, c, here, :]
        statics[FMY, c, here, :] = scale * adj[RIGHT, c, here, :]
        h, mx, my = (first[NEXT + k, c, here, :] for k in range(3))
        out, ux, uy, squared, cc, half = base_prims(h, mx, my, 1.0 / h)
        out[QY], out[TT] = my * uy + 0.5 * squared * h, mx * uy
        out[AY], out[UV] = squared - uy * uy, ux * uy
        for j, k in enumerate(FIRST_NEXT):
            if j >= 3:
                first[NEXT + j, c, here, :] = out[k]

    def static_stage(xs, ys, nexts):
        def static(row):
            start = row + TOP
            here = pl.ds(start, 8)
            for c in range(wide):
                parts = static_x(c, start) if c in xs else None
                if c in ys:
                    static_y(c, here, parts)
                if c in nexts:
                    static_next(c, here)

        return static

    def first_faces(cols_at, rows_at):
        def faces_of(row):
            start = row + TOP
            here, after = pl.ds(start, 8), pl.ds(start + 1, 8)
            for c in cols_at:
                coefs = face(
                    0, 1, c, here, f_at(LMY, c, here), f_right(LMY, c, here),
                    f_at(LPY, c, here), f_right(LPY, c, here),
                )
                for k, (flux, held) in enumerate(((MY, H), (TT, MX), (QY, MY))):
                    col_flux[k, c, here, :] = crossing(
                        coefs, f_at(flux, c, here), f_right(flux, c, here),
                        f_at(held, c, here), f_right(held, c, here),
                    )
            for c in rows_at:
                coefs = face(
                    0, 0, c, here, f_at(LMX, c, here), f_at(LMX, c, after),
                    f_at(LPX, c, here), f_at(LPX, c, after),
                )
                for k, (flux, held) in enumerate(((MX, H), (QX, MX), (TT, MY))):
                    row_flux[k, c, here, :] = crossing(
                        coefs, f_at(flux, c, here), f_at(flux, c, after),
                        f_at(held, c, here), f_at(held, c, after),
                    )

        return faces_of

    inner, own_tiles = EVERY[: tiles - 1], EVERY[:tiles]
    shift_inner = shift_stage(inner, EVERY[1:tiles])
    static_inner = static_stage(own_tiles, EVERY[1 : tiles - 1], inner)
    faces_inner = first_faces(inner, own_tiles)

    def plain(stage):
        return lambda row, index: stage(row)

    pipeline((plain(shift_inner), plain(static_inner)), 1, chunks - 1, G_STATIC)
    pipeline((plain(faces_inner),), 1, chunks - 2, G_FACES)

    for index in range(8):

        @pl.when(sides[index][0])
        def _(index=index):
            copy = edge_copy(index)
            copy.wait_send()
            opposite = (1, 0, 3, 2, 7, 6, 5, 4)[index]
            if index < 2:
                target = recv_rows.at[index]
            elif index < 4:
                target = recv_cols.at[index - 2]
            else:
                target = recv_corner.at[index - 4]
            pltpu.make_async_copy(target, target, edge_recv.at[index]).wait()

    if rounds > 0:
        learn(0)
        if rounds > 1:
            tell(1)

    for c in range(tiles):
        for side, exists, at_rows in ((0, has_up, TOP), (1, has_down, OWN + rows)):
            four = [recv_rows[side, c, 4 * k : 4 * k + 4, :] for k in range(4)]
            four[0] = jnp.where(exists, four[0], -1.0)
            put_start(c, at_rows, 4, four)

    halves = jnp.concatenate(
        [recv_cols[0], recv_cols[1], jnp.zeros((LANES - 32, rows), jnp.float32)], axis=0
    )
    pack_cols[...] = jnp.transpose(halves)

    def rim_tile(left_part, right_part, k, left_at, right_at, from_left, from_right):
        fill = -1.0 if k == 0 else 0.0
        on_right = (lane < HALO) & from_right
        on_left = (lane >= LANES - HALO) & from_left
        shift_r = (LANES - right_at - 4 * k) % LANES
        shift_l = (LANES - HALO - left_at - 4 * k) % LANES
        right_val = pltpu.roll(right_part, shift_r, 1) if shift_r else right_part
        left_val = pltpu.roll(left_part, shift_l, 1) if shift_l else left_part
        return jnp.where(on_right, right_val, jnp.where(on_left, left_val, fill))

    def rim_body(i, carry):
        start = pl.multiple_of(i * 8, 8)
        part = pack_cols[pl.ds(start, 8), :]
        four = [rim_tile(part, part, k, 0, 16, has_left, has_right) for k in range(4)]
        put_start(tiles, start + OWN, 8, four)
        return carry

    lax.fori_loop(0, rows // 8, rim_body, 0, unroll=4)
    for left_slot, right_slot, exists, at_rows, pick in (
        (0, 1, has_up, TOP, 4),
        (2, 3, has_down, OWN + rows, 0),
    ):
        four = [
            rim_tile(
                recv_corner[left_slot],
                recv_corner[right_slot],
                k,
                16,
                0,
                has_left & exists,
                has_right & exists,
            )[pick : pick + 4]
            for k in range(4)
        ]
        put_start(tiles, at_rows, 4, four)

    shift_whole, shift_outer = shift_stage(EVERY, EVERY), shift_stage(EVERY[tiles - 1 :], (0, tiles))
    static_whole = static_stage(EVERY, EVERY, EVERY)
    static_outer = static_stage(EVERY[tiles:], (0, *EVERY[tiles - 1 :]), EVERY[tiles - 1 :])
    faces_whole, faces_outer = first_faces(EVERY, EVERY), first_faces(EVERY[tiles - 1 :], EVERY[tiles:])

    def chosen(whole_stage, outer_stage, last_inner):
        def stage(row, index):
            inside = index is None or 1 <= index <= last_inner
            (outer_stage if inside else whole_stage)(row)

        return stage

    pipeline(
        (
            chosen(shift_whole, shift_outer, chunks - 2),
            chosen(static_whole, static_outer, chunks - 2),
        ),
        0, chunks, G_OUTER, begin=2, end=chunks - 1,
    )

    def first_cells(row):
        start = row + TOP
        here, before = pl.ds(start, 8), pl.ds(start - 1, 8)
        net = [net_of(k, here) for k in range(3)]
        for c in range(wide):
            new = []
            for k in range(3):
                value = row_flux[k, c, here, :]
                change = value - row_flux[k, c, before, :] + net[k][c]
                if k > 0:
                    change = change + f_at((None, WX, WY)[k], c, here)
                new.append(f_at((H, MX, MY)[k], c, here) - change)
            h = new[0] + inflow[0, c, here, :]
            ih = 1.0 / h
            out = base_prims(h, new[1], new[2], ih)[0]
            out[IH] = ih
            for k, value in out.items():
                second[k, c, here, :] = value

    def first_shift(row):
        here = pl.ds(row + TOP, 8)
        heights = next_lanes([second[H, c, here, :] for c in range(wide)])
        flows = next_lanes([second[MY, c, here, :] for c in range(wide)])
        for c, (h, n) in enumerate(zip(heights, flows)):
            ih = 1.0 / h
            out = base_prims(h, n, n, ih)[0]
            out[IH] = ih
            for j, k in enumerate(SECOND_NEXT):
                second[SECOND_AT + j, c, here, :] = out[k]

    TERM, ADJ, ZX, ZY, TERM_R, ADJ_R, ZX_R, ZY_R = range(8)

    def last_cols(row):
        here = pl.ds(row + TOP, 8)
        for c in range(wide):
            coefs = face(
                1, 1, c, here, s_at(LMY, c, here), s_right(LMY, c, here),
                s_at(LPY, c, here), s_right(LPY, c, here),
            )
            col_flux[0, c, here, :] = crossing(
                coefs, s_at(MY, c, here), s_right(MY, c, here),
                s_at(H, c, here), s_right(H, c, here),
            )

    def last_cells(row):
        start = row + TOP
        here, after, before = pl.ds(start, 8), pl.ds(start + 1, 8), pl.ds(start - 1, 8)
        net = net_of(0, here)
        for c in range(wide):
            coefs = face(
                1, 0, c, here, s_at(LMX, c, here), s_at(LMX, c, after),
                s_at(LPX, c, here), s_at(LPX, c, after),
            )
            value = crossing(
                coefs, s_at(MX, c, here), s_at(MX, c, after),
                s_at(H, c, here), s_at(H, c, after),
            )
            row_flux[0, c, here, :] = value
            change = value - row_flux[0, c, before, :] + net[c]
            h = s_at(H, c, here) - change + inflow[1, c, here, :]
            last_h[c, here, :] = h
            adj[TERM, c, here, :] = statics[WGT, c, here, :] * h

    def adj_shift(*planes):
        def shift(row):
            here = pl.ds(row + TOP, 8)
            for k in planes:
                values = [adj[k, c, here, :] for c in range(wide)]
                for c, value in enumerate(next_lanes(values)):
                    adj[TERM_R + k, c, here, :] = value

        return shift

    pipeline(
        (chosen(faces_whole, faces_outer, chunks - 3), plain(first_cells), plain(first_shift)),
        0, chunks, G_FIRST, begin=3, end=chunks - 2,
    )
    if rounds > 1:
        learn(1)
        if rounds > 2:
            tell(2)
    pipeline((plain(last_cols), plain(last_cells), plain(adj_shift(TERM))), 0, chunks, G_LAST)

    def depth_body(i, carry):
        start = pl.multiple_of(i * 8, 8)
        for c in range(tiles):
            own = pl.ds(start + OWN, 8)
            depth_out[pl.ds(start, 8), c * LANES : (c + 1) * LANES] = jnp.where(
                statics[WET, c, own, :] > 0.0, last_h[c, own, :], raw_d[c, pl.ds(start, 8), :]
            )
        return carry

    lax.fori_loop(0, rows // 8, depth_body, 0)
    def last_face(coefs, lm, lp, h, n, z, p, r, ih):
        alpha, beta, gamma = coefs[:3]
        gh = z[1] - z[0]
        fast_l, slow_l, fast_r, slow_r = split_speed_grads(
            *lm, *lp, coefs, gh * (n[1] - n[0]), gh * (h[1] - h[0])
        )
        jump = gamma * gh
        return (
            fast_l * p[0] - slow_l * r[0] - jump,
            alpha * gh + (fast_l + slow_l) * ih[0],
        ), (
            fast_r * p[1] - slow_r * r[1] + jump,
            (fast_r + slow_r) * ih[1] - beta * gh,
        )

    def back_cols(row):
        here = pl.ds(row + TOP, 8)
        for c in range(wide):

            def pair(k):
                return s_at(k, c, here), s_right(k, c, here)

            left, right = last_face(
                coefs_of(1, 1, c, here), pair(LMY), pair(LPY), pair(H), pair(MY),
                (adj[TERM, c, here, :], adj[TERM_R, c, here, :]), pair(PY), pair(RY), pair(IH),
            )
            for k in range(2):
                col_flux[k, c, here, :] = left[k]
                col_flux[2 + k, c, here, :] = right[k]

    def back_cells(row):
        start = row + TOP
        here, after, before = pl.ds(start, 8), pl.ds(start + 1, 8), pl.ds(start - 1, 8)
        entering = [
            last_lanes([col_flux[2 + k, c, here, :] for c in range(wide)]) for k in range(2)
        ]
        for c in range(wide):

            def pair(k):
                return s_at(k, c, here), s_at(k, c, after)

            left, right = last_face(
                coefs_of(1, 0, c, here), pair(LMX), pair(LPX), pair(H), pair(MX),
                (adj[TERM, c, here, :], adj[TERM, c, after, :]), pair(PX), pair(RX), pair(IH),
            )
            in_x = []
            for k in range(2):
                row_flux[k, c, here, :] = right[k]
                in_x.append(left[k] + row_flux[k, c, before, :])
            in_y = [col_flux[k, c, here, :] + entering[k][c] for k in range(2)]
            adj[ADJ, c, here, :] = adj[TERM, c, here, :] + (in_x[0] + in_y[0])
            adj[ZX, c, here, :] = in_x[1]
            adj[ZY, c, here, :] = in_y[1]

    pipeline(
        (plain(back_cols), plain(back_cells), plain(adj_shift(ADJ, ZX, ZY))),
        0, chunks, G_BACK_LAST,
    )

    own_hot = lax.broadcasted_iota(jnp.int32, (rows, dam_count), 0) == local_row
    stacked = []
    for plane in (ADJ, TERM):
        parts = [three_parts(adj[plane, c, OWN : OWN + rows, :]) for c in range(tiles)]
        stacked.append(
            jnp.concatenate([parts[c][k] for k in range(3) for c in range(tiles)], axis=1)
        )
    picked = lax.dot_general(
        jnp.concatenate(stacked, axis=0), jnp.concatenate([col_hot[...]] * 3, axis=0),
        (((1,), (0,)), ((), ())), preferred_element_type=jnp.float32,
    )
    gpart[...] = jnp.concatenate(
        [
            INFLOW_GAIN * jnp.sum(
                jnp.where(own_hot, picked[s * rows : (s + 1) * rows], 0.0), axis=0, keepdims=True
            )
            for s in range(2)
        ],
        axis=1,
    )

    for level in range(2, rounds):
        learn(level)
        if level + 1 < rounds:
            tell(level + 1)

    count = n_gx * n_gy
    me = ix * n_gy + iy
    recv_all[me] = gpart[...]

    def send_grads(k, carry):
        to = k + (k >= me).astype(jnp.int32)
        pltpu.make_async_remote_copy(
            src_ref=gpart,
            dst_ref=recv_all.at[me],
            send_sem=grad_send.at[0],
            recv_sem=grad_recv.at[0],
            device_id=(lax.div(to, n_gy), lax.rem(to, n_gy)),
            device_id_type=MESH,
        ).start()
        return carry

    lax.fori_loop(0, count - 1, send_grads, 0)

    def first_face(coefs, lm, lp, h, n, t, q, v, zh, zn, zt, a, uv, p, r):
        alpha, beta, gamma = coefs[:3]
        gh, gn, gt = zh[1] - zh[0], zn[1] - zn[0], zt[1] - zt[0]
        dn = n[1] - n[0]
        fast_l, slow_l, fast_r, slow_r = split_speed_grads(
            *lm, *lp, coefs,
            gh * dn + gn * (q[1] - q[0]) + gt * (v[1] - v[0]),
            gh * (h[1] - h[0]) + gn * dn + gt * (t[1] - t[0]),
        )
        jump = gamma * gh
        return (
            alpha * (gn * a[0] - gt * uv[0]) + (fast_l * p[0] - slow_l * r[0]) - jump,
            (fast_r * p[1] - slow_r * r[1]) - beta * (gn * a[1] - gt * uv[1]) + jump,
        )

    def first_row_face(c, start):
        here, after = pl.ds(start, 8), pl.ds(start + 1, 8)

        def pair(k):
            return f_at(k, c, here), f_at(k, c, after)

        def z_pair(k):
            return adj[k, c, here, :], adj[k, c, after, :]

        return first_face(
            coefs_of(0, 0, c, here), pair(LMX), pair(LPX), pair(H), pair(MX), pair(MY), pair(QX),
            pair(TT), z_pair(ADJ), z_pair(ZX), z_pair(ZY), pair(AX), pair(UV), pair(PX), pair(RX),
        )

    for c in range(tiles):
        row_flux[0, c, pl.ds(OWN - 8, 8), :] = first_row_face(c, OWN - 8)[1]

    def backward_first(row):
        start = row + OWN
        here, before = pl.ds(start, 8), pl.ds(start - 1, 8)

        def col_face(c):
            def pair(k):
                return f_at(k, c, here), f_right(k, c, here)

            def z_pair(k):
                return adj[k, c, here, :], adj[k + TERM_R - TERM, c, here, :]

            return first_face(
                coefs_of(0, 1, c, here), pair(LMY), pair(LPY), pair(H), pair(MY), pair(MX),
                pair(QY), pair(TT), z_pair(ADJ), z_pair(ZY), z_pair(ZX), pair(AY), pair(UV),
                pair(PY), pair(RY),
            )

        current = pltpu.roll(col_face(wide - 1)[1], 1, 1)
        for c in range(tiles):
            left, right = first_row_face(c, start)
            row_flux[0, c, here, :] = right
            left_y, right_y = col_face(c)
            current, last = pltpu.roll(right_y, 1, 1), current
            entering = jnp.where(lane == 0, last, current)
            across = left + row_flux[0, c, before, :] + (left_y + entering)
            walls = adj[ZX, c, here, :] * f_at(BX, c, here) + adj[ZY, c, here, :] * f_at(BY, c, here)
            adjoint_out[pl.ds(row, 8), c * LANES : (c + 1) * LANES] = (
                adj[ADJ, c, here, :] + across - walls
            )

    sweep(backward_first, 0, rows // 8, G_BACK_FIRST)

    for sem in (grad_send, grad_recv):
        others = recv_all.at[pl.ds(0, count - 1)]
        pltpu.make_async_copy(others, others, sem.at[0]).wait()
    total = jnp.sum(recv_all[...], axis=0)
    for s in range(2):
        grad_out[s : s + 1, :] = total[:, s * dam_count : (s + 1) * dam_count]


def place(*refs):
    sources, targets, sem = refs[:3], refs[3:6], refs[6]
    copies = [
        pltpu.make_async_copy(source, target, sem.at[k])
        for k, (source, target) in enumerate(zip(sources, targets))
    ]
    for copy in copies:
        copy.start()
    for copy in copies:
        copy.wait()


def on_device(
    n_gx,
    n_gy,
    water_depth,
    momentum_x,
    momentum_y,
    wet_mask,
    damage_class,
    damage_rates,
    dam_cell,
    releases,
):
    rows, cols = water_depth.shape
    tiles = cols // LANES
    wide = tiles + 1
    high = rows + 2 * HALO + 2 * TOP
    dam_count = dam_cell.shape[0]
    f32 = jnp.float32
    plane = (wide, high, LANES)
    own = (tiles, rows, LANES)
    anywhere = pl.BlockSpec(memory_space=pl.ANY)
    vmem = pl.BlockSpec(memory_space=pltpu.VMEM)
    dma = pltpu.SemaphoreType.DMA
    results = pl.pallas_call(
        functools.partial(kernel, n_gx, n_gy, cols * n_gy, damage_rates.shape[0]),
        out_shape=(
            pltpu.VMEM((rows, cols), f32),
            pltpu.VMEM((rows, cols), f32),
            pltpu.VMEM(releases.shape[::-1], f32),
        ),
        in_specs=[anywhere] * 8,
        out_specs=(vmem, vmem, vmem),
        scratch_shapes=[
            pltpu.VMEM(own, f32),
            pltpu.VMEM(own, f32),
            pltpu.VMEM(own, f32),
            pltpu.VMEM(own, jnp.int32),
            pltpu.VMEM(own, jnp.int32),
            pltpu.VMEM((32,) + plane, f32),
            pltpu.VMEM((19,) + plane, f32),
            pltpu.VMEM((4,) + plane, f32),
            pltpu.VMEM((2, 2, 7) + plane, f32),
            pltpu.VMEM((2,) + plane, f32),
            pltpu.VMEM((8,) + plane, f32),
            pltpu.VMEM(plane, f32),
            pltpu.VMEM((3,) + plane, f32),
            pltpu.VMEM((4,) + plane, f32),
            pltpu.VMEM((cols, dam_count), jnp.bfloat16),
            pltpu.VMEM((rows, LANES), f32),
            pltpu.VMEM((2, tiles, 16, LANES), f32),
            pltpu.VMEM((2, tiles, 16, LANES), f32),
            pltpu.VMEM((2, 16, rows), f32),
            pltpu.VMEM((2, 16, rows), f32),
            pltpu.VMEM((4, 8, LANES), f32),
            pltpu.VMEM((1, 2 * dam_count), f32),
            pltpu.VMEM((n_gx * n_gy, 1, 2 * dam_count), f32),
            pltpu.SMEM(damage_rates.shape, f32),
            pltpu.VMEM((1, dam_count), jnp.int32),
            pltpu.VMEM(releases.shape[::-1], f32),
            dma((3,)),
            pltpu.SemaphoreType.REGULAR((max((n_gx - 1).bit_length(), 1),)),
            dma((5, tiles)),
            dma((8,)),
            dma((8,)),
            dma((1,)),
            dma((1,)),
        ],
        compiler_params=pltpu.CompilerParams(
            collective_id=0, has_side_effects=True, vmem_limit_bytes=56 * 1024 * 1024
        ),
        name="window",
    )(
        water_depth,
        momentum_x,
        momentum_y,
        wet_mask,
        damage_class,
        damage_rates,
        dam_cell.reshape(1, dam_count),
        releases.T,
    )
    final_depth, adjoint, grad = pl.pallas_call(
        place,
        out_shape=tuple(jax.ShapeDtypeStruct(value.shape, f32) for value in results),
        in_specs=[vmem] * 3,
        out_specs=(anywhere,) * 3,
        scratch_shapes=[dma((3,))],
        name="place",
    )(*(pltpu.with_memory_space_constraint(value, pltpu.VMEM) for value in results))
    return final_depth, adjoint, grad.T


def solution(mesh):
    n_gx, n_gy = mesh.shape["gx"], mesh.shape["gy"]
    grid = P("gx", "gy")
    return jax.shard_map(
        functools.partial(on_device, n_gx, n_gy),
        mesh=mesh,
        in_specs=(grid,) * 5 + (P(),) * 3,
        out_specs=(grid, grid, P()),
        check_vma=False,
    )
```

```python
import functools

import jax
import jax.numpy as jnp
from jax import lax
from jax.experimental import pallas as pl
from jax.experimental.pallas import tpu as pltpu
from jax.sharding import PartitionSpec as P

GRAVITY = 9.81
TIME_RATIO = 0.05
INFLOW_GAIN = 0.25
HALO = 4
LANES = 128
TOP = 8
OWN = TOP + HALO
G_STATIC, G_FACES, G_OUTER, G_FIRST, G_LAST, G_BACK_LAST, G_BACK_FIRST = 2, 2, 14, 6, 15, 5, 1
MESH = pl.DeviceIdType.MESH


def sweep(body, first, last, group):
    whole = (last - first) // group

    def run(i, carry):
        base = pl.multiple_of(i * (8 * group), 8)
        for j in range(group):
            body(base + 8 * (first + j))
        return carry

    lax.fori_loop(0, whole, run, 0)
    for chunk in range(first + whole * group, last):
        body(8 * chunk)


def pipeline(stages, first, last, group=1, begin=None, end=None):
    depth = len(stages)
    begin = first + depth - 1 if begin is None else begin
    end = last if end is None else end

    def step(at, index=None):
        for k in reversed(range(depth)):
            if index is None:
                stages[k](at - 8 * k, None)
            elif first <= index - k < last:
                stages[k](at - 8 * k, index - k)

    for index in range(first, begin):
        step(8 * index, index)
    whole = (end - begin) // group

    def run(i, carry):
        base = pl.multiple_of(i * (8 * group), 8)
        for j in range(group):
            step(base + 8 * (begin + j))
        return carry

    lax.fori_loop(0, whole, run, 0)
    for index in range(begin + whole * group, last + depth - 1):
        step(8 * index, index)


def three_parts(values):
    parts = []
    for _ in range(3):
        part = values.astype(jnp.bfloat16)
        values = values - part.astype(jnp.float32)
        parts.append(part)
    return parts


def halved_on_tie(value, picks, ties):
    return jnp.where(picks, value, jnp.where(ties, 0.5 * value, 0.0))


def split_speed_grads(lm_l, lm_r, lp_l, lp_r, coefs, d_term, k_term):
    _, _, _, slow, fast, e_slow, e_fast = coefs
    g_slow = e_slow * (fast * k_term - d_term)
    g_fast = e_fast * (d_term - slow * k_term)
    slow_l = halved_on_tie(g_slow, lm_l < lm_r, lm_l == lm_r)
    fast_l = halved_on_tie(g_fast, lp_l > lp_r, lp_l == lp_r)
    return fast_l, slow_l, g_fast - fast_l, g_slow - slow_l


def kernel(
    n_gx,
    n_gy,
    total_cols,
    classes,
    depth_in,
    mx_in,
    my_in,
    wet_in,
    class_in,
    rates_in,
    dams_in,
    releases_in,
    depth_out,
    adjoint_out,
    grad_out,
    raw_d,
    raw_x,
    raw_y,
    raw_wet,
    raw_cls,
    first,
    second,
    statics,
    faces,
    inflow,
    adj,
    last_h,
    row_flux,
    col_flux,
    col_hot,
    pack_cols,
    send_rows,
    recv_rows,
    send_cols,
    recv_cols,
    recv_corner,
    gpart,
    recv_all,
    rates,
    dams,
    releases,
    small_sem,
    know_sem,
    in_sem,
    edge_send,
    edge_recv,
    grad_send,
    grad_recv,
):
    rows, cols = depth_in.shape
    tiles = cols // LANES
    wide = tiles + 1
    span = rows + 2 * HALO
    chunks = span // 8
    ix, iy = lax.axis_index("gx"), lax.axis_index("gy")
    lane = lax.broadcasted_iota(jnp.int32, (8, LANES), 1)

    has_up, has_down = ix > 0, ix < n_gx - 1
    has_left, has_right = iy > 0, iy < n_gy - 1

    barrier = pltpu.get_barrier_semaphore()
    for step in range(1, n_gy):
        pl.semaphore_signal(
            barrier, inc=1, device_id=(ix, lax.rem(iy + step, n_gy)), device_id_type=MESH
        )
    sides = (
        (has_up, -1, 0),
        (has_down, 1, 0),
        (has_left, 0, -1),
        (has_right, 0, 1),
        (has_up & has_left, -1, -1),
        (has_up & has_right, -1, 1),
        (has_down & has_left, 1, -1),
        (has_down & has_right, 1, 1),
    )
    corners = 0
    for exists, dx, dy in sides[:2] + sides[4:]:
        corners = corners + exists.astype(jnp.int32)

        @pl.when(exists)
        def _(dx=dx, dy=dy):
            pl.semaphore_signal(barrier, inc=1, device_id=(ix + dx, iy + dy), device_id_type=MESH)

    small = [
        pltpu.make_async_copy(source, target, small_sem.at[index])
        for index, (source, target) in enumerate(
            ((rates_in, rates), (dams_in, dams), (releases_in, releases))
        )
    ]
    for copy in small[:1]:
        copy.start()
    loads = []
    for c in (0, tiles - 1, *range(1, tiles - 1)):
        for index, (source, target) in enumerate(
            ((wet_in, raw_wet), (class_in, raw_cls), (depth_in, raw_d), (mx_in, raw_x), (my_in, raw_y))
        ):
            copy = pltpu.make_async_copy(
                source.at[:, pl.ds(c * LANES, LANES)], target.at[c], in_sem.at[index, c]
            )
            copy.start()
            loads.append(copy)
    for copy in small[1:]:
        copy.start()

    small[0].wait()
    for copy in loads[:10]:
        copy.wait()

    rate = [rates[k] for k in range(classes)]

    def coded_chunk(c, start, size=8):
        at = (c, pl.ds(start, size), slice(None))
        wet = raw_wet[at] > 0
        cls = raw_cls[at]
        weight = jnp.full(cls.shape, rate[0])
        for k in range(1, classes):
            weight = jnp.where(cls == k, rate[k], weight)
        return (
            jnp.where(wet, raw_d[at], -1.0),
            raw_x[at],
            raw_y[at],
            jnp.where(wet, weight, 0.0),
        )

    def pack_body(i, carry):
        start = pl.multiple_of(i * 8, 8)
        left = coded_chunk(0, start)
        right = coded_chunk(tiles - 1, start)
        packed = jnp.zeros((8, LANES), jnp.float32)
        for k in range(4):
            mine = (lane >= 4 * k) & (lane < 4 * k + 4)
            packed = jnp.where(mine, pltpu.roll(left[k], 4 * k, 1) if k else left[k], packed)
            mine = (lane >= 16 + 4 * k) & (lane < 20 + 4 * k)
            packed = jnp.where(mine, pltpu.roll(right[k], 20 + 4 * k, 1), packed)
        pack_cols[pl.ds(start, 8), :] = packed
        return carry

    lax.fori_loop(0, rows // 8, pack_body, 0, unroll=4)
    for copy in loads[10:]:
        copy.wait()
    for c in range(tiles):
        for side, start, pick in ((0, 0, 0), (1, rows - 8, 4)):
            four = coded_chunk(c, start)
            for k in range(4):
                send_rows[side, c, 4 * k : 4 * k + 4, :] = four[k][pick : pick + 4]
    turned = jnp.transpose(pack_cols[...])
    send_cols[0] = turned[0:16]
    send_cols[1] = turned[16:32]

    pl.semaphore_wait(barrier, (n_gy - 1) + corners)

    rounds = (n_gx - 1).bit_length()

    def reach(level):
        return (ix >= 2**level, -(2**level)), (ix + 2**level < n_gx, 2**level)

    def tell(level):
        for exists, offset in reach(level):

            @pl.when(exists)
            def _(offset=offset):
                pl.semaphore_signal(
                    know_sem.at[level], inc=1, device_id=(ix + offset, iy), device_id_type=MESH
                )

    def learn(level):
        pl.semaphore_wait(
            know_sem.at[level], sum(exists.astype(jnp.int32) for exists, _ in reach(level))
        )

    def edge_copy(index):
        _, dx, dy = sides[index]
        opposite = (1, 0, 3, 2, 7, 6, 5, 4)[index]
        if index < 2:
            source, target = send_rows.at[index], recv_rows.at[opposite]
        elif index < 4:
            source, target = send_cols.at[index - 2], recv_cols.at[opposite - 2]
        else:
            first = 0 if index < 6 else rows - 8
            source, target = pack_cols.at[pl.ds(first, 8), :], recv_corner.at[opposite - 4]
        return pltpu.make_async_remote_copy(
            src_ref=source,
            dst_ref=target,
            send_sem=edge_send.at[index],
            recv_sem=edge_recv.at[opposite],
            device_id=(ix + dx, iy + dy),
            device_id_type=MESH,
        )

    for index in (0, 1, 4, 5, 6, 7, 2, 3):

        @pl.when(sides[index][0])
        def _(index=index):
            edge_copy(index).start()

    if rounds > 0:
        tell(0)

    H, MX, MY, LMX, LPX, LMY, LPY, PX, RX, PY, RY = range(11)
    IH = 11
    QX, QY, TT, AX, AY, UV, WX, WY, BX, BY = range(11, 21)
    NEXT = 21
    WET, WGT, FMX, FMY = range(4)
    ALPHA, BETA, GAMMA, SLOW, FAST, ESLOW, EFAST = range(7)

    def put_start(c, at_rows, size, four):
        wet = four[0] > 0.0
        at = (c, pl.ds(at_rows, size), slice(None))
        first[(H,) + at] = jnp.where(wet, four[0], 1.0)
        first[(MX,) + at] = jnp.where(wet, four[1], 0.0)
        first[(MY,) + at] = jnp.where(wet, four[2], 0.0)
        statics[(WGT,) + at] = jnp.where(wet, four[3], 0.0)
        statics[(WET,) + at] = jnp.where(wet, 1.0, 0.0)

    def own_body(i, carry):
        start = pl.multiple_of(i * 8, 8)
        for c in range(tiles):
            put_start(c, start + OWN, 8, coded_chunk(c, start))
        return carry

    lax.fori_loop(0, rows // 8, own_body, 0)

    for copy in small[1:]:
        copy.wait()
    cell = dams[...]
    if total_cols & (total_cols - 1) == 0:
        dam_row = lax.shift_right_logical(cell, total_cols.bit_length() - 1)
    else:
        dam_row = lax.div(cell, total_cols)
    dam_col = cell - dam_row * total_cols
    dam_count = cell.shape[1]
    local_row = dam_row - ix * rows
    local_col = dam_col - iy * cols
    amounts = INFLOW_GAIN * releases[...]
    thrice = lambda values: jnp.concatenate([values] * 3, axis=1)
    amounts = jnp.concatenate(
        [part.astype(jnp.float32) for part in three_parts(amounts)], axis=1
    )
    wide_row = lax.broadcasted_iota(jnp.int32, (span, 3 * dam_count), 0) - HALO
    row_hot = wide_row == thrice(local_row)
    gain_rows = jnp.concatenate(
        [jnp.where(row_hot, amounts[s : s + 1], 0.0) for s in range(2)], axis=0
    ).astype(jnp.bfloat16)
    position = lax.broadcasted_iota(jnp.int32, (LANES, 3 * dam_count), 0)
    col_thrice = thrice(local_col)
    hots = []
    for c in range(wide):
        if c < tiles:
            column = position + c * LANES
        else:
            column = jnp.where(
                position < HALO,
                position + cols,
                jnp.where(position >= LANES - HALO, position - LANES, -2 * LANES),
            )
        hot = (column == col_thrice).astype(jnp.float32).astype(jnp.bfloat16)
        if c < tiles:
            col_hot[c * LANES : (c + 1) * LANES, :] = hot[:, :dam_count]
        hots.append(hot)
    poured = lax.dot_general(
        gain_rows, jnp.concatenate(hots, axis=0), (((1,), (1,)), ((), ())),
        preferred_element_type=jnp.float32,
    )
    for s in range(2):
        for c in range(wide):
            inflow[s, c, TOP : TOP + span, :] = poured[
                s * span : (s + 1) * span, c * LANES : (c + 1) * LANES
            ]

    def turned(get, cs, shift, step):
        needed = sorted({c for c in cs} | {(c + step) % wide for c in cs})
        values = {c: pltpu.roll(get(c), shift, 1) for c in needed}
        edge = LANES - 1 if step > 0 else 0
        return {c: jnp.where(lane == edge, values[(c + step) % wide], values[c]) for c in cs}

    def next_lanes(values, cs=None):
        cs = range(wide) if cs is None else cs
        return list(turned(lambda c: values[c], cs, LANES - 1, 1).values())

    def last_lanes(values):
        return list(turned(lambda c: values[c], range(wide), 1, -1).values())

    FIRST_NEXT = (H, MX, MY, LMY, LPY, QY, TT, AY, UV, PY, RY)
    SECOND_NEXT = (H, MY, LMY, LPY, PY, RY, IH)
    SECOND_AT = 12

    def base_prims(h, mx, my, ih):
        ux, uy = mx * ih, my * ih
        squared = GRAVITY * h
        cc = squared * lax.rsqrt(squared)
        half = 0.5 * cc
        out = {H: h, MX: mx, MY: my, LMX: ux - cc, LPX: ux + cc, LMY: uy - cc, LPY: uy + cc}
        half_i, ux_i, uy_i = half * ih, ux * ih, uy * ih
        out |= {PX: half_i - ux_i, RX: half_i + ux_i, PY: half_i - uy_i, RY: half_i + uy_i}
        return out, ux, uy, squared, cc, half

    def reader(source, keys, offset):
        def at(k, c, rows_at):
            return source[k, c, rows_at, :]

        def right(k, c, rows_at):
            return source[offset + keys.index(k), c, rows_at, :]

        return at, right

    f_at, f_right = reader(first, FIRST_NEXT, NEXT)
    s_at, s_right = reader(second, SECOND_NEXT, SECOND_AT)

    def face(step, dim, c, here, lm_l, lm_r, lp_l, lp_r):
        low, high = jnp.minimum(lm_l, lm_r), jnp.maximum(lp_l, lp_r)
        slow, fast = jnp.minimum(low, 0.0), jnp.maximum(high, 0.0)
        inverse = 1.0 / (fast - slow)
        masked = statics[FMX + dim, c, here, :] * inverse
        alpha, beta = fast * masked, slow * masked
        gamma = slow * alpha
        e_slow = halved_on_tie(alpha * inverse, low < 0.0, low == 0.0)
        e_fast = halved_on_tie(beta * inverse, high > 0.0, high == 0.0)
        for k, value in enumerate((alpha, beta, gamma, slow, fast, e_slow, e_fast)):
            faces[step, dim, k, c, here, :] = value
        return alpha, beta, gamma

    def coefs_of(step, dim, c, here):
        return [faces[step, dim, k, c, here, :] for k in range(7)]

    def crossing(coefs, flux_l, flux_r, held_l, held_r):
        alpha, beta, gamma = coefs
        return alpha * flux_l - beta * flux_r + gamma * (held_r - held_l)

    def net_of(k, here):
        values = [col_flux[k, c, here, :] for c in range(wide)]
        return [mine - entering for mine, entering in zip(values, last_lanes(values))]

    RIGHT, LEFT = 0, 1
    EVERY = tuple(range(wide))

    def shift_stage(rights, lefts):
        def shift(row):
            here = pl.ds(row + TOP, 8)

            def wet_at(c):
                return statics[WET, c, here, :]

            for c, value in turned(wet_at, rights, LANES - 1, 1).items():
                adj[RIGHT, c, here, :] = value
            for c, value in turned(wet_at, lefts, 1, -1).items():
                adj[LEFT, c, here, :] = value
            for j, k in enumerate((H, MX, MY)):
                shifted = turned(lambda c, k=k: first[k, c, here, :], rights, LANES - 1, 1)
                for c, value in shifted.items():
                    first[NEXT + j, c, here, :] = value

        return shift

    def walls_of(scale, lower, upper, u, n, q, a, cc, half):
        single = scale * (lower - upper)
        both = scale * (2.0 - (lower + upper))
        size = jnp.abs(u)
        return single * q + both * ((size + cc) * n), single * a + both * (u * (half - size))

    def static_x(c, start):
        here = pl.ds(start, 8)
        scale = TIME_RATIO * statics[WET, c, here, :]
        above = statics[WET, c, pl.ds(start - 1, 8), :]
        below = statics[WET, c, pl.ds(start + 1, 8), :]
        statics[FMX, c, here, :] = scale * below
        h, mx, my = (first[k, c, here, :] for k in (H, MX, MY))
        out, ux, uy, squared, cc, half = base_prims(h, mx, my, 1.0 / h)
        pressure = 0.5 * squared * h
        out[QX], out[QY], out[TT] = mx * ux + pressure, my * uy + pressure, mx * uy
        out[AX], out[AY], out[UV] = squared - ux * ux, squared - uy * uy, ux * uy
        out[WX], out[BX] = walls_of(scale, above, below, ux, mx, out[QX], out[AX], cc, half)
        for k, value in out.items():
            if k not in (H, MX, MY):
                first[k, c, here, :] = value
        return uy, my, out[QY], out[AY], cc, half

    def static_y(c, here, parts=None):
        scale = TIME_RATIO * statics[WET, c, here, :]
        if parts is None:
            h, my = first[H, c, here, :], first[MY, c, here, :]
            squared = GRAVITY * h
            cc = squared * lax.rsqrt(squared)
            parts = my * (1.0 / h), my, first[QY, c, here, :], first[AY, c, here, :], cc, 0.5 * cc
        first[WY, c, here, :], first[BY, c, here, :] = walls_of(
            scale, adj[LEFT, c, here, :], adj[RIGHT, c, here, :], *parts
        )

    def static_next(c, here):
        scale = TIME_RATIO * statics[WET, c, here, :]
        statics[FMY, c, here, :] = scale * adj[RIGHT, c, here, :]
        h, mx, my = (first[NEXT + k, c, here, :] for k in range(3))
        out, ux, uy, squared, cc, half = base_prims(h, mx, my, 1.0 / h)
        out[QY], out[TT] = my * uy + 0.5 * squared * h, mx * uy
        out[AY], out[UV] = squared - uy * uy, ux * uy
        for j, k in enumerate(FIRST_NEXT):
            if j >= 3:
                first[NEXT + j, c, here, :] = out[k]

    def static_stage(xs, ys, nexts):
        def static(row):
            start = row + TOP
            here = pl.ds(start, 8)
            for c in range(wide):
                parts = static_x(c, start) if c in xs else None
                if c in ys:
                    static_y(c, here, parts)
                if c in nexts:
                    static_next(c, here)

        return static

    def first_faces(cols_at, rows_at):
        def faces_of(row):
            start = row + TOP
            here, after = pl.ds(start, 8), pl.ds(start + 1, 8)
            for c in cols_at:
                coefs = face(
                    0, 1, c, here, f_at(LMY, c, here), f_right(LMY, c, here),
                    f_at(LPY, c, here), f_right(LPY, c, here),
                )
                for k, (flux, held) in enumerate(((MY, H), (TT, MX), (QY, MY))):
                    col_flux[k, c, here, :] = crossing(
                        coefs, f_at(flux, c, here), f_right(flux, c, here),
                        f_at(held, c, here), f_right(held, c, here),
                    )
            for c in rows_at:
                coefs = face(
                    0, 0, c, here, f_at(LMX, c, here), f_at(LMX, c, after),
                    f_at(LPX, c, here), f_at(LPX, c, after),
                )
                for k, (flux, held) in enumerate(((MX, H), (QX, MX), (TT, MY))):
                    row_flux[k, c, here, :] = crossing(
                        coefs, f_at(flux, c, here), f_at(flux, c, after),
                        f_at(held, c, here), f_at(held, c, after),
                    )

        return faces_of

    inner, own_tiles = EVERY[: tiles - 1], EVERY[:tiles]
    shift_inner = shift_stage(inner, EVERY[1:tiles])
    static_inner = static_stage(own_tiles, EVERY[1 : tiles - 1], inner)
    faces_inner = first_faces(inner, own_tiles)

    def plain(stage):
        return lambda row, index: stage(row)

    pipeline((plain(shift_inner), plain(static_inner)), 1, chunks - 1, G_STATIC)
    pipeline((plain(faces_inner),), 1, chunks - 2, G_FACES)

    for index in range(8):

        @pl.when(sides[index][0])
        def _(index=index):
            copy = edge_copy(index)
            copy.wait_send()
            opposite = (1, 0, 3, 2, 7, 6, 5, 4)[index]
            if index < 2:
                target = recv_rows.at[index]
            elif index < 4:
                target = recv_cols.at[index - 2]
            else:
                target = recv_corner.at[index - 4]
            pltpu.make_async_copy(target, target, edge_recv.at[index]).wait()

    if rounds > 0:
        learn(0)
        if rounds > 1:
            tell(1)

    for c in range(tiles):
        for side, exists, at_rows in ((0, has_up, TOP), (1, has_down, OWN + rows)):
            four = [recv_rows[side, c, 4 * k : 4 * k + 4, :] for k in range(4)]
            four[0] = jnp.where(exists, four[0], -1.0)
            put_start(c, at_rows, 4, four)

    halves = jnp.concatenate(
        [recv_cols[0], recv_cols[1], jnp.zeros((LANES - 32, rows), jnp.float32)], axis=0
    )
    pack_cols[...] = jnp.transpose(halves)

    def rim_tile(left_part, right_part, k, left_at, right_at, from_left, from_right):
        fill = -1.0 if k == 0 else 0.0
        on_right = (lane < HALO) & from_right
        on_left = (lane >= LANES - HALO) & from_left
        shift_r = (LANES - right_at - 4 * k) % LANES
        shift_l = (LANES - HALO - left_at - 4 * k) % LANES
        right_val = pltpu.roll(right_part, shift_r, 1) if shift_r else right_part
        left_val = pltpu.roll(left_part, shift_l, 1) if shift_l else left_part
        return jnp.where(on_right, right_val, jnp.where(on_left, left_val, fill))

    def rim_body(i, carry):
        start = pl.multiple_of(i * 8, 8)
        part = pack_cols[pl.ds(start, 8), :]
        four = [rim_tile(part, part, k, 0, 16, has_left, has_right) for k in range(4)]
        put_start(tiles, start + OWN, 8, four)
        return carry

    lax.fori_loop(0, rows // 8, rim_body, 0, unroll=4)
    for left_slot, right_slot, exists, at_rows, pick in (
        (0, 1, has_up, TOP, 4),
        (2, 3, has_down, OWN + rows, 0),
    ):
        four = [
            rim_tile(
                recv_corner[left_slot],
                recv_corner[right_slot],
                k,
                16,
                0,
                has_left & exists,
                has_right & exists,
            )[pick : pick + 4]
            for k in range(4)
        ]
        put_start(tiles, at_rows, 4, four)

    shift_whole, shift_outer = shift_stage(EVERY, EVERY), shift_stage(EVERY[tiles - 1 :], (0, tiles))
    static_whole = static_stage(EVERY, EVERY, EVERY)
    static_outer = static_stage(EVERY[tiles:], (0, *EVERY[tiles - 1 :]), EVERY[tiles - 1 :])
    faces_whole, faces_outer = first_faces(EVERY, EVERY), first_faces(EVERY[tiles - 1 :], EVERY[tiles:])

    def chosen(whole_stage, outer_stage, last_inner):
        def stage(row, index):
            inside = index is None or 1 <= index <= last_inner
            (outer_stage if inside else whole_stage)(row)

        return stage

    pipeline(
        (
            chosen(shift_whole, shift_outer, chunks - 2),
            chosen(static_whole, static_outer, chunks - 2),
        ),
        0, chunks, G_OUTER, begin=2, end=chunks - 1,
    )

    def first_cells(row):
        start = row + TOP
        here, before = pl.ds(start, 8), pl.ds(start - 1, 8)
        net = [net_of(k, here) for k in range(3)]
        for c in range(wide):
            new = []
            for k in range(3):
                value = row_flux[k, c, here, :]
                change = value - row_flux[k, c, before, :] + net[k][c]
                if k > 0:
                    change = change + f_at((None, WX, WY)[k], c, here)
                new.append(f_at((H, MX, MY)[k], c, here) - change)
            h = new[0] + inflow[0, c, here, :]
            ih = 1.0 / h
            out = base_prims(h, new[1], new[2], ih)[0]
            out[IH] = ih
            for k, value in out.items():
                second[k, c, here, :] = value

    def first_shift(row):
        here = pl.ds(row + TOP, 8)
        heights = next_lanes([second[H, c, here, :] for c in range(wide)])
        flows = next_lanes([second[MY, c, here, :] for c in range(wide)])
        for c, (h, n) in enumerate(zip(heights, flows)):
            ih = 1.0 / h
            out = base_prims(h, n, n, ih)[0]
            out[IH] = ih
            for j, k in enumerate(SECOND_NEXT):
                second[SECOND_AT + j, c, here, :] = out[k]

    TERM, ADJ, ZX, ZY, TERM_R, ADJ_R, ZX_R, ZY_R = range(8)

    def last_cols(row):
        here = pl.ds(row + TOP, 8)
        for c in range(wide):
            coefs = face(
                1, 1, c, here, s_at(LMY, c, here), s_right(LMY, c, here),
                s_at(LPY, c, here), s_right(LPY, c, here),
            )
            col_flux[0, c, here, :] = crossing(
                coefs, s_at(MY, c, here), s_right(MY, c, here),
                s_at(H, c, here), s_right(H, c, here),
            )

    def last_cells(row):
        start = row + TOP
        here, after, before = pl.ds(start, 8), pl.ds(start + 1, 8), pl.ds(start - 1, 8)
        net = net_of(0, here)
        for c in range(wide):
            coefs = face(
                1, 0, c, here, s_at(LMX, c, here), s_at(LMX, c, after),
                s_at(LPX, c, here), s_at(LPX, c, after),
            )
            value = crossing(
                coefs, s_at(MX, c, here), s_at(MX, c, after),
                s_at(H, c, here), s_at(H, c, after),
            )
            row_flux[0, c, here, :] = value
            change = value - row_flux[0, c, before, :] + net[c]
            h = s_at(H, c, here) - change + inflow[1, c, here, :]
            last_h[c, here, :] = h
            adj[TERM, c, here, :] = statics[WGT, c, here, :] * h

    def adj_shift(*planes):
        def shift(row):
            here = pl.ds(row + TOP, 8)
            for k in planes:
                values = [adj[k, c, here, :] for c in range(wide)]
                for c, value in enumerate(next_lanes(values)):
                    adj[TERM_R + k, c, here, :] = value

        return shift

    pipeline(
        (chosen(faces_whole, faces_outer, chunks - 3), plain(first_cells), plain(first_shift)),
        0, chunks, G_FIRST, begin=3, end=chunks - 2,
    )
    if rounds > 1:
        learn(1)
        if rounds > 2:
            tell(2)
    pipeline((plain(last_cols), plain(last_cells), plain(adj_shift(TERM))), 0, chunks, G_LAST)

    def last_face(coefs, lm, lp, h, n, z, p, r, ih):
        alpha, beta, gamma = coefs[:3]
        gh = z[1] - z[0]
        fast_l, slow_l, fast_r, slow_r = split_speed_grads(
            *lm, *lp, coefs, gh * (n[1] - n[0]), gh * (h[1] - h[0])
        )
        jump = gamma * gh
        return (
            fast_l * p[0] - slow_l * r[0] - jump,
            alpha * gh + (fast_l + slow_l) * ih[0],
        ), (
            fast_r * p[1] - slow_r * r[1] + jump,
            (fast_r + slow_r) * ih[1] - beta * gh,
        )

    def back_cols(row):
        here = pl.ds(row + TOP, 8)
        for c in range(wide):

            def pair(k):
                return s_at(k, c, here), s_right(k, c, here)

            left, right = last_face(
                coefs_of(1, 1, c, here), pair(LMY), pair(LPY), pair(H), pair(MY),
                (adj[TERM, c, here, :], adj[TERM_R, c, here, :]), pair(PY), pair(RY), pair(IH),
            )
            for k in range(2):
                col_flux[k, c, here, :] = left[k]
                col_flux[2 + k, c, here, :] = right[k]

    def back_cells(row):
        start = row + TOP
        here, after, before = pl.ds(start, 8), pl.ds(start + 1, 8), pl.ds(start - 1, 8)
        entering = [
            last_lanes([col_flux[2 + k, c, here, :] for c in range(wide)]) for k in range(2)
        ]
        for c in range(wide):

            def pair(k):
                return s_at(k, c, here), s_at(k, c, after)

            left, right = last_face(
                coefs_of(1, 0, c, here), pair(LMX), pair(LPX), pair(H), pair(MX),
                (adj[TERM, c, here, :], adj[TERM, c, after, :]), pair(PX), pair(RX), pair(IH),
            )
            in_x = []
            for k in range(2):
                row_flux[k, c, here, :] = right[k]
                in_x.append(left[k] + row_flux[k, c, before, :])
            in_y = [col_flux[k, c, here, :] + entering[k][c] for k in range(2)]
            adj[ADJ, c, here, :] = adj[TERM, c, here, :] + (in_x[0] + in_y[0])
            adj[ZX, c, here, :] = in_x[1]
            adj[ZY, c, here, :] = in_y[1]

    pipeline(
        (plain(back_cols), plain(back_cells), plain(adj_shift(ADJ, ZX, ZY))),
        0, chunks, G_BACK_LAST,
    )

    own_hot = lax.broadcasted_iota(jnp.int32, (rows, dam_count), 0) == local_row
    hots = jnp.concatenate([col_hot[...]] * 3, axis=0)
    sums = []
    for plane in (ADJ, TERM):
        parts = [three_parts(adj[plane, c, OWN : OWN + rows, :]) for c in range(tiles)]
        picked = lax.dot_general(
            jnp.concatenate([parts[c][k] for k in range(3) for c in range(tiles)], axis=1), hots,
            (((1,), (0,)), ((), ())), preferred_element_type=jnp.float32,
        )
        sums.append(
            INFLOW_GAIN * jnp.sum(jnp.where(own_hot, picked, 0.0), axis=0, keepdims=True)
        )
    gpart[...] = jnp.concatenate(sums, axis=1)

    for level in range(2, rounds):
        learn(level)
        if level + 1 < rounds:
            tell(level + 1)

    count = n_gx * n_gy
    me = ix * n_gy + iy
    recv_all[me] = gpart[...]

    def send_grads(k, carry):
        to = k + (k >= me).astype(jnp.int32)
        pltpu.make_async_remote_copy(
            src_ref=gpart,
            dst_ref=recv_all.at[me],
            send_sem=grad_send.at[0],
            recv_sem=grad_recv.at[0],
            device_id=(lax.div(to, n_gy), lax.rem(to, n_gy)),
            device_id_type=MESH,
        ).start()
        return carry

    lax.fori_loop(0, count - 1, send_grads, 0)

    def depth_body(i, carry):
        start = pl.multiple_of(i * 8, 8)
        for c in range(tiles):
            own = pl.ds(start + OWN, 8)
            depth_out[pl.ds(start, 8), c * LANES : (c + 1) * LANES] = jnp.where(
                statics[WET, c, own, :] > 0.0, last_h[c, own, :], raw_d[c, pl.ds(start, 8), :]
            )
        return carry

    lax.fori_loop(0, rows // 8, depth_body, 0)

    def first_face(coefs, lm, lp, h, n, t, q, v, zh, zn, zt, a, uv, p, r):
        alpha, beta, gamma = coefs[:3]
        gh, gn, gt = zh[1] - zh[0], zn[1] - zn[0], zt[1] - zt[0]
        dn = n[1] - n[0]
        fast_l, slow_l, fast_r, slow_r = split_speed_grads(
            *lm, *lp, coefs,
            gh * dn + gn * (q[1] - q[0]) + gt * (v[1] - v[0]),
            gh * (h[1] - h[0]) + gn * dn + gt * (t[1] - t[0]),
        )
        jump = gamma * gh
        return (
            alpha * (gn * a[0] - gt * uv[0]) + (fast_l * p[0] - slow_l * r[0]) - jump,
            (fast_r * p[1] - slow_r * r[1]) - beta * (gn * a[1] - gt * uv[1]) + jump,
        )

    def first_row_face(c, start):
        here, after = pl.ds(start, 8), pl.ds(start + 1, 8)

        def pair(k):
            return f_at(k, c, here), f_at(k, c, after)

        def z_pair(k):
            return adj[k, c, here, :], adj[k, c, after, :]

        return first_face(
            coefs_of(0, 0, c, here), pair(LMX), pair(LPX), pair(H), pair(MX), pair(MY), pair(QX),
            pair(TT), z_pair(ADJ), z_pair(ZX), z_pair(ZY), pair(AX), pair(UV), pair(PX), pair(RX),
        )

    for c in range(tiles):
        row_flux[0, c, pl.ds(OWN - 8, 8), :] = first_row_face(c, OWN - 8)[1]

    def backward_first(row):
        start = row + OWN
        here, before = pl.ds(start, 8), pl.ds(start - 1, 8)

        def col_face(c):
            def pair(k):
                return f_at(k, c, here), f_right(k, c, here)

            def z_pair(k):
                return adj[k, c, here, :], adj[k + TERM_R - TERM, c, here, :]

            return first_face(
                coefs_of(0, 1, c, here), pair(LMY), pair(LPY), pair(H), pair(MY), pair(MX),
                pair(QY), pair(TT), z_pair(ADJ), z_pair(ZY), z_pair(ZX), pair(AY), pair(UV),
                pair(PY), pair(RY),
            )

        current = pltpu.roll(col_face(wide - 1)[1], 1, 1)
        for c in range(tiles):
            left, right = first_row_face(c, start)
            row_flux[0, c, here, :] = right
            left_y, right_y = col_face(c)
            current, last = pltpu.roll(right_y, 1, 1), current
            entering = jnp.where(lane == 0, last, current)
            across = left + row_flux[0, c, before, :] + (left_y + entering)
            walls = adj[ZX, c, here, :] * f_at(BX, c, here) + adj[ZY, c, here, :] * f_at(BY, c, here)
            adjoint_out[pl.ds(row, 8), c * LANES : (c + 1) * LANES] = (
                adj[ADJ, c, here, :] + across - walls
            )

    sweep(backward_first, 0, rows // 8, G_BACK_FIRST)

    for sem in (grad_send, grad_recv):
        others = recv_all.at[pl.ds(0, count - 1)]
        pltpu.make_async_copy(others, others, sem.at[0]).wait()
    total = jnp.sum(recv_all[...], axis=0)
    for s in range(2):
        grad_out[s : s + 1, :] = total[:, s * dam_count : (s + 1) * dam_count]


def place(*refs):
    sources, targets, sem = refs[:3], refs[3:6], refs[6]
    copies = [
        pltpu.make_async_copy(source, target, sem.at[k])
        for k, (source, target) in enumerate(zip(sources, targets))
    ]
    for copy in copies:
        copy.start()
    for copy in copies:
        copy.wait()


def on_device(
    n_gx,
    n_gy,
    water_depth,
    momentum_x,
    momentum_y,
    wet_mask,
    damage_class,
    damage_rates,
    dam_cell,
    releases,
):
    rows, cols = water_depth.shape
    tiles = cols // LANES
    wide = tiles + 1
    high = rows + 2 * HALO + 2 * TOP
    dam_count = dam_cell.shape[0]
    f32 = jnp.float32
    plane = (wide, high, LANES)
    own = (tiles, rows, LANES)
    anywhere = pl.BlockSpec(memory_space=pl.ANY)
    vmem = pl.BlockSpec(memory_space=pltpu.VMEM)
    dma = pltpu.SemaphoreType.DMA
    results = pl.pallas_call(
        functools.partial(kernel, n_gx, n_gy, cols * n_gy, damage_rates.shape[0]),
        out_shape=(
            pltpu.VMEM((rows, cols), f32),
            pltpu.VMEM((rows, cols), f32),
            pltpu.VMEM(releases.shape[::-1], f32),
        ),
        in_specs=[anywhere] * 8,
        out_specs=(vmem, vmem, vmem),
        scratch_shapes=[
            pltpu.VMEM(own, f32),
            pltpu.VMEM(own, f32),
            pltpu.VMEM(own, f32),
            pltpu.VMEM(own, jnp.int32),
            pltpu.VMEM(own, jnp.int32),
            pltpu.VMEM((32,) + plane, f32),
            pltpu.VMEM((19,) + plane, f32),
            pltpu.VMEM((4,) + plane, f32),
            pltpu.VMEM((2, 2, 7) + plane, f32),
            pltpu.VMEM((2,) + plane, f32),
            pltpu.VMEM((8,) + plane, f32),
            pltpu.VMEM(plane, f32),
            pltpu.VMEM((3,) + plane, f32),
            pltpu.VMEM((4,) + plane, f32),
            pltpu.VMEM((cols, dam_count), jnp.bfloat16),
            pltpu.VMEM((rows, LANES), f32),
            pltpu.VMEM((2, tiles, 16, LANES), f32),
            pltpu.VMEM((2, tiles, 16, LANES), f32),
            pltpu.VMEM((2, 16, rows), f32),
            pltpu.VMEM((2, 16, rows), f32),
            pltpu.VMEM((4, 8, LANES), f32),
            pltpu.VMEM((1, 2 * dam_count), f32),
            pltpu.VMEM((n_gx * n_gy, 1, 2 * dam_count), f32),
            pltpu.SMEM(damage_rates.shape, f32),
            pltpu.VMEM((1, dam_count), jnp.int32),
            pltpu.VMEM(releases.shape[::-1], f32),
            dma((3,)),
            pltpu.SemaphoreType.REGULAR((max((n_gx - 1).bit_length(), 1),)),
            dma((5, tiles)),
            dma((8,)),
            dma((8,)),
            dma((1,)),
            dma((1,)),
        ],
        compiler_params=pltpu.CompilerParams(
            collective_id=0, has_side_effects=True, vmem_limit_bytes=56 * 1024 * 1024
        ),
        name="window",
    )(
        water_depth,
        momentum_x,
        momentum_y,
        wet_mask,
        damage_class,
        damage_rates,
        dam_cell.reshape(1, dam_count),
        releases.T,
    )
    final_depth, adjoint, grad = pl.pallas_call(
        place,
        out_shape=tuple(jax.ShapeDtypeStruct(value.shape, f32) for value in results),
        in_specs=[vmem] * 3,
        out_specs=(anywhere,) * 3,
        scratch_shapes=[dma((3,))],
        name="place",
    )(*(pltpu.with_memory_space_constraint(value, pltpu.VMEM) for value in results))
    return final_depth, adjoint, grad.T


def solution(mesh):
    n_gx, n_gy = mesh.shape["gx"], mesh.shape["gy"]
    grid = P("gx", "gy")
    return jax.shard_map(
        functools.partial(on_device, n_gx, n_gy),
        mesh=mesh,
        in_specs=(grid,) * 5 + (P(),) * 3,
        out_specs=(grid, grid, P()),
        check_vma=False,
    )
```

```python
import functools

import jax
import jax.numpy as jnp
from jax import lax
from jax.experimental import pallas as pl
from jax.experimental.pallas import tpu as pltpu
from jax.sharding import PartitionSpec as P

GRAVITY = 9.81
TIME_RATIO = 0.05
INFLOW_GAIN = 0.25
HALO = 4
LANES = 128
TOP = 8
OWN = TOP + HALO
G_STATIC, G_FACES, G_OUTER, G_FIRST, G_LAST, G_BACK_LAST, G_BACK_FIRST = 2, 2, 14, 6, 15, 5, 1
MESH = pl.DeviceIdType.MESH


def sweep(body, first, last, group):
    whole = (last - first) // group

    def run(i, carry):
        base = pl.multiple_of(i * (8 * group), 8)
        for j in range(group):
            body(base + 8 * (first + j))
        return carry

    lax.fori_loop(0, whole, run, 0)
    for chunk in range(first + whole * group, last):
        body(8 * chunk)


def pipeline(stages, first, last, group=1, begin=None, end=None):
    depth = len(stages)
    begin = first + depth - 1 if begin is None else begin
    end = last if end is None else end

    def step(at, index=None):
        for k in reversed(range(depth)):
            if index is None:
                stages[k](at - 8 * k, None)
            elif first <= index - k < last:
                stages[k](at - 8 * k, index - k)

    for index in range(first, begin):
        step(8 * index, index)
    whole = (end - begin) // group

    def run(i, carry):
        base = pl.multiple_of(i * (8 * group), 8)
        for j in range(group):
            step(base + 8 * (begin + j))
        return carry

    lax.fori_loop(0, whole, run, 0)
    for index in range(begin + whole * group, last + depth - 1):
        step(8 * index, index)


def three_parts(values):
    parts = []
    for _ in range(3):
        part = values.astype(jnp.bfloat16)
        values = values - part.astype(jnp.float32)
        parts.append(part)
    return parts


def halved_on_tie(value, picks, ties):
    return jnp.where(picks, value, jnp.where(ties, 0.5 * value, 0.0))


def split_speed_grads(lm_l, lm_r, lp_l, lp_r, coefs, d_term, k_term):
    _, _, _, slow, fast, e_slow, e_fast = coefs
    g_slow = e_slow * (fast * k_term - d_term)
    g_fast = e_fast * (d_term - slow * k_term)
    slow_l = halved_on_tie(g_slow, lm_l < lm_r, lm_l == lm_r)
    fast_l = halved_on_tie(g_fast, lp_l > lp_r, lp_l == lp_r)
    return fast_l, slow_l, g_fast - fast_l, g_slow - slow_l


def kernel(
    n_gx,
    n_gy,
    total_cols,
    classes,
    depth_in,
    mx_in,
    my_in,
    wet_in,
    class_in,
    rates_in,
    dams_in,
    releases_in,
    depth_out,
    adjoint_out,
    grad_out,
    raw_d,
    raw_x,
    raw_y,
    raw_wet,
    raw_cls,
    first,
    second,
    statics,
    faces,
    inflow,
    adj,
    last_h,
    row_flux,
    col_flux,
    col_hot,
    pack_cols,
    send_rows,
    recv_rows,
    send_cols,
    recv_cols,
    recv_corner,
    gpart,
    recv_all,
    rates,
    dams,
    releases,
    small_sem,
    know_sem,
    in_sem,
    edge_send,
    edge_recv,
    grad_send,
    grad_recv,
):
    rows, cols = depth_in.shape
    tiles = cols // LANES
    wide = tiles + 1
    span = rows + 2 * HALO
    chunks = span // 8
    ix, iy = lax.axis_index("gx"), lax.axis_index("gy")
    lane = lax.broadcasted_iota(jnp.int32, (8, LANES), 1)

    has_up, has_down = ix > 0, ix < n_gx - 1
    has_left, has_right = iy > 0, iy < n_gy - 1

    barrier = pltpu.get_barrier_semaphore()
    for step in range(1, n_gy):
        pl.semaphore_signal(
            barrier, inc=1, device_id=(ix, lax.rem(iy + step, n_gy)), device_id_type=MESH
        )
    sides = (
        (has_up, -1, 0),
        (has_down, 1, 0),
        (has_left, 0, -1),
        (has_right, 0, 1),
        (has_up & has_left, -1, -1),
        (has_up & has_right, -1, 1),
        (has_down & has_left, 1, -1),
        (has_down & has_right, 1, 1),
    )
    corners = 0
    for exists, dx, dy in sides[:2] + sides[4:]:
        corners = corners + exists.astype(jnp.int32)

        @pl.when(exists)
        def _(dx=dx, dy=dy):
            pl.semaphore_signal(barrier, inc=1, device_id=(ix + dx, iy + dy), device_id_type=MESH)

    small = [
        pltpu.make_async_copy(source, target, small_sem.at[index])
        for index, (source, target) in enumerate(
            ((rates_in, rates), (dams_in, dams), (releases_in, releases))
        )
    ]
    for copy in small[:1]:
        copy.start()
    loads = []
    for c in (0, tiles - 1, *range(1, tiles - 1)):
        for index, (source, target) in enumerate(
            ((wet_in, raw_wet), (class_in, raw_cls), (depth_in, raw_d), (mx_in, raw_x), (my_in, raw_y))
        ):
            copy = pltpu.make_async_copy(
                source.at[:, pl.ds(c * LANES, LANES)], target.at[c], in_sem.at[index, c]
            )
            copy.start()
            loads.append(copy)
    for copy in small[1:]:
        copy.start()

    small[0].wait()
    for copy in loads[:10]:
        copy.wait()

    rate = [rates[k] for k in range(classes)]

    def coded_chunk(c, start, size=8):
        at = (c, pl.ds(start, size), slice(None))
        wet = raw_wet[at] > 0
        cls = raw_cls[at]
        weight = jnp.full(cls.shape, rate[0])
        for k in range(1, classes):
            weight = jnp.where(cls == k, rate[k], weight)
        return (
            jnp.where(wet, raw_d[at], -1.0),
            raw_x[at],
            raw_y[at],
            jnp.where(wet, weight, 0.0),
        )

    def pack_body(i, carry):
        start = pl.multiple_of(i * 8, 8)
        left = coded_chunk(0, start)
        right = coded_chunk(tiles - 1, start)
        packed = jnp.zeros((8, LANES), jnp.float32)
        for k in range(4):
            mine = (lane >= 4 * k) & (lane < 4 * k + 4)
            packed = jnp.where(mine, pltpu.roll(left[k], 4 * k, 1) if k else left[k], packed)
            mine = (lane >= 16 + 4 * k) & (lane < 20 + 4 * k)
            packed = jnp.where(mine, pltpu.roll(right[k], 20 + 4 * k, 1), packed)
        pack_cols[pl.ds(start, 8), :] = packed
        return carry

    lax.fori_loop(0, rows // 8, pack_body, 0, unroll=16)
    for copy in loads[10:]:
        copy.wait()
    for c in range(tiles):
        for side, start, pick in ((0, 0, 0), (1, rows - 8, 4)):
            four = coded_chunk(c, start)
            for k in range(4):
                send_rows[side, c, 4 * k : 4 * k + 4, :] = four[k][pick : pick + 4]
    turned = jnp.transpose(pack_cols[...])
    send_cols[0] = turned[0:16]
    send_cols[1] = turned[16:32]

    pl.semaphore_wait(barrier, (n_gy - 1) + corners)

    rounds = (n_gx - 1).bit_length()

    def reach(level):
        return (ix >= 2**level, -(2**level)), (ix + 2**level < n_gx, 2**level)

    def tell(level):
        for exists, offset in reach(level):

            @pl.when(exists)
            def _(offset=offset):
                pl.semaphore_signal(
                    know_sem.at[level], inc=1, device_id=(ix + offset, iy), device_id_type=MESH
                )

    def learn(level):
        pl.semaphore_wait(
            know_sem.at[level], sum(exists.astype(jnp.int32) for exists, _ in reach(level))
        )

    def edge_copy(index):
        _, dx, dy = sides[index]
        opposite = (1, 0, 3, 2, 7, 6, 5, 4)[index]
        if index < 2:
            source, target = send_rows.at[index], recv_rows.at[opposite]
        elif index < 4:
            source, target = send_cols.at[index - 2], recv_cols.at[opposite - 2]
        else:
            first = 0 if index < 6 else rows - 8
            source, target = pack_cols.at[pl.ds(first, 8), :], recv_corner.at[opposite - 4]
        return pltpu.make_async_remote_copy(
            src_ref=source,
            dst_ref=target,
            send_sem=edge_send.at[index],
            recv_sem=edge_recv.at[opposite],
            device_id=(ix + dx, iy + dy),
            device_id_type=MESH,
        )

    for index in (0, 1, 4, 5, 6, 7, 2, 3):

        @pl.when(sides[index][0])
        def _(index=index):
            edge_copy(index).start()

    if rounds > 0:
        tell(0)

    H, MX, MY, LMX, LPX, LMY, LPY, PX, RX, PY, RY = range(11)
    IH = 11
    QX, QY, TT, AX, AY, UV, WX, WY, BX, BY = range(11, 21)
    NEXT = 21
    WET, WGT, FMX, FMY = range(4)
    ALPHA, BETA, GAMMA, SLOW, FAST, ESLOW, EFAST = range(7)

    def put_start(c, at_rows, size, four):
        wet = four[0] > 0.0
        at = (c, pl.ds(at_rows, size), slice(None))
        first[(H,) + at] = jnp.where(wet, four[0], 1.0)
        first[(MX,) + at] = jnp.where(wet, four[1], 0.0)
        first[(MY,) + at] = jnp.where(wet, four[2], 0.0)
        statics[(WGT,) + at] = jnp.where(wet, four[3], 0.0)
        statics[(WET,) + at] = jnp.where(wet, 1.0, 0.0)

    def own_body(i, carry):
        start = pl.multiple_of(i * 8, 8)
        for c in range(tiles):
            put_start(c, start + OWN, 8, coded_chunk(c, start))
        return carry

    lax.fori_loop(0, rows // 8, own_body, 0)

    for copy in small[1:]:
        copy.wait()
    cell = dams[...]
    if total_cols & (total_cols - 1) == 0:
        dam_row = lax.shift_right_logical(cell, total_cols.bit_length() - 1)
    else:
        dam_row = lax.div(cell, total_cols)
    dam_col = cell - dam_row * total_cols
    dam_count = cell.shape[1]
    local_row = dam_row - ix * rows
    local_col = dam_col - iy * cols
    amounts = INFLOW_GAIN * releases[...]
    thrice = lambda values: jnp.concatenate([values] * 3, axis=1)
    amounts = jnp.concatenate(
        [part.astype(jnp.float32) for part in three_parts(amounts)], axis=1
    )
    wide_row = lax.broadcasted_iota(jnp.int32, (span, 3 * dam_count), 0) - HALO
    row_hot = wide_row == thrice(local_row)
    gain_rows = jnp.concatenate(
        [jnp.where(row_hot, amounts[s : s + 1], 0.0) for s in range(2)], axis=0
    ).astype(jnp.bfloat16)
    position = lax.broadcasted_iota(jnp.int32, (LANES, 3 * dam_count), 0)
    col_thrice = thrice(local_col)
    hots = []
    for c in range(wide):
        if c < tiles:
            column = position + c * LANES
        else:
            column = jnp.where(
                position < HALO,
                position + cols,
                jnp.where(position >= LANES - HALO, position - LANES, -2 * LANES),
            )
        hot = (column == col_thrice).astype(jnp.float32).astype(jnp.bfloat16)
        if c < tiles:
            col_hot[c * LANES : (c + 1) * LANES, :] = hot[:, :dam_count]
        hots.append(hot)
    poured = lax.dot_general(
        gain_rows, jnp.concatenate(hots, axis=0), (((1,), (1,)), ((), ())),
        preferred_element_type=jnp.float32,
    )
    for s in range(2):
        for c in range(wide):
            inflow[s, c, TOP : TOP + span, :] = poured[
                s * span : (s + 1) * span, c * LANES : (c + 1) * LANES
            ]

    def turned(get, cs, shift, step):
        needed = sorted({c for c in cs} | {(c + step) % wide for c in cs})
        values = {c: pltpu.roll(get(c), shift, 1) for c in needed}
        edge = LANES - 1 if step > 0 else 0
        return {c: jnp.where(lane == edge, values[(c + step) % wide], values[c]) for c in cs}

    def next_lanes(values, cs=None):
        cs = range(wide) if cs is None else cs
        return list(turned(lambda c: values[c], cs, LANES - 1, 1).values())

    def last_lanes(values):
        return list(turned(lambda c: values[c], range(wide), 1, -1).values())

    FIRST_NEXT = (H, MX, MY, LMY, LPY, QY, TT, AY, UV, PY, RY)
    SECOND_NEXT = (H, MY, LMY, LPY, PY, RY, IH)
    SECOND_AT = 12

    def base_prims(h, mx, my, ih):
        ux, uy = mx * ih, my * ih
        squared = GRAVITY * h
        cc = squared * lax.rsqrt(squared)
        half = 0.5 * cc
        out = {H: h, MX: mx, MY: my, LMX: ux - cc, LPX: ux + cc, LMY: uy - cc, LPY: uy + cc}
        half_i, ux_i, uy_i = half * ih, ux * ih, uy * ih
        out |= {PX: half_i - ux_i, RX: half_i + ux_i, PY: half_i - uy_i, RY: half_i + uy_i}
        return out, ux, uy, squared, cc, half

    def reader(source, keys, offset):
        def at(k, c, rows_at):
            return source[k, c, rows_at, :]

        def right(k, c, rows_at):
            return source[offset + keys.index(k), c, rows_at, :]

        return at, right

    f_at, f_right = reader(first, FIRST_NEXT, NEXT)
    s_at, s_right = reader(second, SECOND_NEXT, SECOND_AT)

    def face(step, dim, c, here, lm_l, lm_r, lp_l, lp_r):
        low, high = jnp.minimum(lm_l, lm_r), jnp.maximum(lp_l, lp_r)
        slow, fast = jnp.minimum(low, 0.0), jnp.maximum(high, 0.0)
        inverse = 1.0 / (fast - slow)
        masked = statics[FMX + dim, c, here, :] * inverse
        alpha, beta = fast * masked, slow * masked
        gamma = slow * alpha
        e_slow = halved_on_tie(alpha * inverse, low < 0.0, low == 0.0)
        e_fast = halved_on_tie(beta * inverse, high > 0.0, high == 0.0)
        for k, value in enumerate((alpha, beta, gamma, slow, fast, e_slow, e_fast)):
            faces[step, dim, k, c, here, :] = value
        return alpha, beta, gamma

    def coefs_of(step, dim, c, here):
        return [faces[step, dim, k, c, here, :] for k in range(7)]

    def crossing(coefs, flux_l, flux_r, held_l, held_r):
        alpha, beta, gamma = coefs
        return alpha * flux_l - beta * flux_r + gamma * (held_r - held_l)

    def net_of(k, here):
        values = [col_flux[k, c, here, :] for c in range(wide)]
        return [mine - entering for mine, entering in zip(values, last_lanes(values))]

    RIGHT, LEFT = 0, 1
    EVERY = tuple(range(wide))

    def shift_stage(rights, lefts):
        def shift(row):
            here = pl.ds(row + TOP, 8)

            def wet_at(c):
                return statics[WET, c, here, :]

            for c, value in turned(wet_at, rights, LANES - 1, 1).items():
                adj[RIGHT, c, here, :] = value
            for c, value in turned(wet_at, lefts, 1, -1).items():
                adj[LEFT, c, here, :] = value
            for j, k in enumerate((H, MX, MY)):
                shifted = turned(lambda c, k=k: first[k, c, here, :], rights, LANES - 1, 1)
                for c, value in shifted.items():
                    first[NEXT + j, c, here, :] = value

        return shift

    def walls_of(scale, lower, upper, u, n, q, a, cc, half):
        single = scale * (lower - upper)
        both = scale * (2.0 - (lower + upper))
        size = jnp.abs(u)
        return single * q + both * ((size + cc) * n), single * a + both * (u * (half - size))

    def static_x(c, start):
        here = pl.ds(start, 8)
        scale = TIME_RATIO * statics[WET, c, here, :]
        above = statics[WET, c, pl.ds(start - 1, 8), :]
        below = statics[WET, c, pl.ds(start + 1, 8), :]
        statics[FMX, c, here, :] = scale * below
        h, mx, my = (first[k, c, here, :] for k in (H, MX, MY))
        out, ux, uy, squared, cc, half = base_prims(h, mx, my, 1.0 / h)
        pressure = 0.5 * squared * h
        out[QX], out[QY], out[TT] = mx * ux + pressure, my * uy + pressure, mx * uy
        out[AX], out[AY], out[UV] = squared - ux * ux, squared - uy * uy, ux * uy
        out[WX], out[BX] = walls_of(scale, above, below, ux, mx, out[QX], out[AX], cc, half)
        for k, value in out.items():
            if k not in (H, MX, MY):
                first[k, c, here, :] = value
        return uy, my, out[QY], out[AY], cc, half

    def static_y(c, here, parts=None):
        scale = TIME_RATIO * statics[WET, c, here, :]
        if parts is None:
            h, my = first[H, c, here, :], first[MY, c, here, :]
            squared = GRAVITY * h
            cc = squared * lax.rsqrt(squared)
            parts = my * (1.0 / h), my, first[QY, c, here, :], first[AY, c, here, :], cc, 0.5 * cc
        first[WY, c, here, :], first[BY, c, here, :] = walls_of(
            scale, adj[LEFT, c, here, :], adj[RIGHT, c, here, :], *parts
        )

    def static_next(c, here):
        scale = TIME_RATIO * statics[WET, c, here, :]
        statics[FMY, c, here, :] = scale * adj[RIGHT, c, here, :]
        h, mx, my = (first[NEXT + k, c, here, :] for k in range(3))
        out, ux, uy, squared, cc, half = base_prims(h, mx, my, 1.0 / h)
        out[QY], out[TT] = my * uy + 0.5 * squared * h, mx * uy
        out[AY], out[UV] = squared - uy * uy, ux * uy
        for j, k in enumerate(FIRST_NEXT):
            if j >= 3:
                first[NEXT + j, c, here, :] = out[k]

    def static_stage(xs, ys, nexts):
        def static(row):
            start = row + TOP
            here = pl.ds(start, 8)
            for c in range(wide):
                parts = static_x(c, start) if c in xs else None
                if c in ys:
                    static_y(c, here, parts)
                if c in nexts:
                    static_next(c, here)

        return static

    def first_faces(cols_at, rows_at):
        def faces_of(row):
            start = row + TOP
            here, after = pl.ds(start, 8), pl.ds(start + 1, 8)
            for c in cols_at:
                coefs = face(
                    0, 1, c, here, f_at(LMY, c, here), f_right(LMY, c, here),
                    f_at(LPY, c, here), f_right(LPY, c, here),
                )
                for k, (flux, held) in enumerate(((MY, H), (TT, MX), (QY, MY))):
                    col_flux[k, c, here, :] = crossing(
                        coefs, f_at(flux, c, here), f_right(flux, c, here),
                        f_at(held, c, here), f_right(held, c, here),
                    )
            for c in rows_at:
                coefs = face(
                    0, 0, c, here, f_at(LMX, c, here), f_at(LMX, c, after),
                    f_at(LPX, c, here), f_at(LPX, c, after),
                )
                for k, (flux, held) in enumerate(((MX, H), (QX, MX), (TT, MY))):
                    row_flux[k, c, here, :] = crossing(
                        coefs, f_at(flux, c, here), f_at(flux, c, after),
                        f_at(held, c, here), f_at(held, c, after),
                    )

        return faces_of

    inner, own_tiles = EVERY[: tiles - 1], EVERY[:tiles]
    shift_inner = shift_stage(inner, EVERY[1:tiles])
    static_inner = static_stage(own_tiles, EVERY[1 : tiles - 1], inner)
    faces_inner = first_faces(inner, own_tiles)

    def plain(stage):
        return lambda row, index: stage(row)

    pipeline((plain(shift_inner), plain(static_inner)), 1, chunks - 1, G_STATIC)
    pipeline((plain(faces_inner),), 1, chunks - 2, G_FACES)

    for index in range(8):

        @pl.when(sides[index][0])
        def _(index=index):
            copy = edge_copy(index)
            copy.wait_send()
            opposite = (1, 0, 3, 2, 7, 6, 5, 4)[index]
            if index < 2:
                target = recv_rows.at[index]
            elif index < 4:
                target = recv_cols.at[index - 2]
            else:
                target = recv_corner.at[index - 4]
            pltpu.make_async_copy(target, target, edge_recv.at[index]).wait()

    if rounds > 0:
        learn(0)
        if rounds > 1:
            tell(1)

    for c in range(tiles):
        for side, exists, at_rows in ((0, has_up, TOP), (1, has_down, OWN + rows)):
            four = [recv_rows[side, c, 4 * k : 4 * k + 4, :] for k in range(4)]
            four[0] = jnp.where(exists, four[0], -1.0)
            put_start(c, at_rows, 4, four)

    halves = jnp.concatenate(
        [recv_cols[0], recv_cols[1], jnp.zeros((LANES - 32, rows), jnp.float32)], axis=0
    )
    pack_cols[...] = jnp.transpose(halves)

    def rim_tile(left_part, right_part, k, left_at, right_at, from_left, from_right):
        fill = -1.0 if k == 0 else 0.0
        on_right = (lane < HALO) & from_right
        on_left = (lane >= LANES - HALO) & from_left
        shift_r = (LANES - right_at - 4 * k) % LANES
        shift_l = (LANES - HALO - left_at - 4 * k) % LANES
        right_val = pltpu.roll(right_part, shift_r, 1) if shift_r else right_part
        left_val = pltpu.roll(left_part, shift_l, 1) if shift_l else left_part
        return jnp.where(on_right, right_val, jnp.where(on_left, left_val, fill))

    def rim_body(i, carry):
        start = pl.multiple_of(i * 8, 8)
        part = pack_cols[pl.ds(start, 8), :]
        four = [rim_tile(part, part, k, 0, 16, has_left, has_right) for k in range(4)]
        put_start(tiles, start + OWN, 8, four)
        return carry

    lax.fori_loop(0, rows // 8, rim_body, 0, unroll=16)
    for left_slot, right_slot, exists, at_rows, pick in (
        (0, 1, has_up, TOP, 4),
        (2, 3, has_down, OWN + rows, 0),
    ):
        four = [
            rim_tile(
                recv_corner[left_slot],
                recv_corner[right_slot],
                k,
                16,
                0,
                has_left & exists,
                has_right & exists,
            )[pick : pick + 4]
            for k in range(4)
        ]
        put_start(tiles, at_rows, 4, four)

    shift_whole, shift_outer = shift_stage(EVERY, EVERY), shift_stage(EVERY[tiles - 1 :], (0, tiles))
    static_whole = static_stage(EVERY, EVERY, EVERY)
    static_outer = static_stage(EVERY[tiles:], (0, *EVERY[tiles - 1 :]), EVERY[tiles - 1 :])
    faces_whole, faces_outer = first_faces(EVERY, EVERY), first_faces(EVERY[tiles - 1 :], EVERY[tiles:])

    def chosen(whole_stage, outer_stage, last_inner):
        def stage(row, index):
            inside = index is None or 1 <= index <= last_inner
            (outer_stage if inside else whole_stage)(row)

        return stage

    pipeline(
        (
            chosen(shift_whole, shift_outer, chunks - 2),
            chosen(static_whole, static_outer, chunks - 2),
        ),
        0, chunks, G_OUTER, begin=2, end=chunks - 1,
    )

    def first_cells(row):
        start = row + TOP
        here, before = pl.ds(start, 8), pl.ds(start - 1, 8)
        net = [net_of(k, here) for k in range(3)]
        for c in range(wide):
            new = []
            for k in range(3):
                value = row_flux[k, c, here, :]
                change = value - row_flux[k, c, before, :] + net[k][c]
                if k > 0:
                    change = change + f_at((None, WX, WY)[k], c, here)
                new.append(f_at((H, MX, MY)[k], c, here) - change)
            h = new[0] + inflow[0, c, here, :]
            ih = 1.0 / h
            out = base_prims(h, new[1], new[2], ih)[0]
            out[IH] = ih
            for k, value in out.items():
                second[k, c, here, :] = value

    def first_shift(row):
        here = pl.ds(row + TOP, 8)
        heights = next_lanes([second[H, c, here, :] for c in range(wide)])
        flows = next_lanes([second[MY, c, here, :] for c in range(wide)])
        for c, (h, n) in enumerate(zip(heights, flows)):
            ih = 1.0 / h
            out = base_prims(h, n, n, ih)[0]
            out[IH] = ih
            for j, k in enumerate(SECOND_NEXT):
                second[SECOND_AT + j, c, here, :] = out[k]

    TERM, ADJ, ZX, ZY, TERM_R, ADJ_R, ZX_R, ZY_R = range(8)

    def last_cols(row):
        here = pl.ds(row + TOP, 8)
        for c in range(wide):
            coefs = face(
                1, 1, c, here, s_at(LMY, c, here), s_right(LMY, c, here),
                s_at(LPY, c, here), s_right(LPY, c, here),
            )
            col_flux[0, c, here, :] = crossing(
                coefs, s_at(MY, c, here), s_right(MY, c, here),
                s_at(H, c, here), s_right(H, c, here),
            )

    def last_cells(row):
        start = row + TOP
        here, after, before = pl.ds(start, 8), pl.ds(start + 1, 8), pl.ds(start - 1, 8)
        net = net_of(0, here)
        for c in range(wide):
            coefs = face(
                1, 0, c, here, s_at(LMX, c, here), s_at(LMX, c, after),
                s_at(LPX, c, here), s_at(LPX, c, after),
            )
            value = crossing(
                coefs, s_at(MX, c, here), s_at(MX, c, after),
                s_at(H, c, here), s_at(H, c, after),
            )
            row_flux[0, c, here, :] = value
            change = value - row_flux[0, c, before, :] + net[c]
            h = s_at(H, c, here) - change + inflow[1, c, here, :]
            last_h[c, here, :] = h
            adj[TERM, c, here, :] = statics[WGT, c, here, :] * h

    def adj_shift(*planes):
        def shift(row):
            here = pl.ds(row + TOP, 8)
            for k in planes:
                values = [adj[k, c, here, :] for c in range(wide)]
                for c, value in enumerate(next_lanes(values)):
                    adj[TERM_R + k, c, here, :] = value

        return shift

    pipeline(
        (chosen(faces_whole, faces_outer, chunks - 3), plain(first_cells), plain(first_shift)),
        0, chunks, G_FIRST, begin=3, end=chunks - 2,
    )
    if rounds > 1:
        learn(1)
        if rounds > 2:
            tell(2)
    pipeline((plain(last_cols), plain(last_cells), plain(adj_shift(TERM))), 0, chunks, G_LAST)

    def last_face(coefs, lm, lp, h, n, z, p, r, ih):
        alpha, beta, gamma = coefs[:3]
        gh = z[1] - z[0]
        fast_l, slow_l, fast_r, slow_r = split_speed_grads(
            *lm, *lp, coefs, gh * (n[1] - n[0]), gh * (h[1] - h[0])
        )
        jump = gamma * gh
        return (
            fast_l * p[0] - slow_l * r[0] - jump,
            alpha * gh + (fast_l + slow_l) * ih[0],
        ), (
            fast_r * p[1] - slow_r * r[1] + jump,
            (fast_r + slow_r) * ih[1] - beta * gh,
        )

    def back_cols(row):
        here = pl.ds(row + TOP, 8)
        for c in range(wide):

            def pair(k):
                return s_at(k, c, here), s_right(k, c, here)

            left, right = last_face(
                coefs_of(1, 1, c, here), pair(LMY), pair(LPY), pair(H), pair(MY),
                (adj[TERM, c, here, :], adj[TERM_R, c, here, :]), pair(PY), pair(RY), pair(IH),
            )
            for k in range(2):
                col_flux[k, c, here, :] = left[k]
                col_flux[2 + k, c, here, :] = right[k]

    def back_cells(row):
        start = row + TOP
        here, after, before = pl.ds(start, 8), pl.ds(start + 1, 8), pl.ds(start - 1, 8)
        entering = [
            last_lanes([col_flux[2 + k, c, here, :] for c in range(wide)]) for k in range(2)
        ]
        for c in range(wide):

            def pair(k):
                return s_at(k, c, here), s_at(k, c, after)

            left, right = last_face(
                coefs_of(1, 0, c, here), pair(LMX), pair(LPX), pair(H), pair(MX),
                (adj[TERM, c, here, :], adj[TERM, c, after, :]), pair(PX), pair(RX), pair(IH),
            )
            in_x = []
            for k in range(2):
                row_flux[k, c, here, :] = right[k]
                in_x.append(left[k] + row_flux[k, c, before, :])
            in_y = [col_flux[k, c, here, :] + entering[k][c] for k in range(2)]
            adj[ADJ, c, here, :] = adj[TERM, c, here, :] + (in_x[0] + in_y[0])
            adj[ZX, c, here, :] = in_x[1]
            adj[ZY, c, here, :] = in_y[1]

    pipeline(
        (plain(back_cols), plain(back_cells), plain(adj_shift(ADJ, ZX, ZY))),
        0, chunks, G_BACK_LAST,
    )

    own_hot = lax.broadcasted_iota(jnp.int32, (rows, dam_count), 0) == local_row
    hots = jnp.concatenate([col_hot[...]] * 3, axis=0)
    sums = []
    for plane in (ADJ, TERM):
        parts = [three_parts(adj[plane, c, OWN : OWN + rows, :]) for c in range(tiles)]
        picked = lax.dot_general(
            jnp.concatenate([parts[c][k] for k in range(3) for c in range(tiles)], axis=1), hots,
            (((1,), (0,)), ((), ())), preferred_element_type=jnp.float32,
        )
        sums.append(
            INFLOW_GAIN * jnp.sum(jnp.where(own_hot, picked, 0.0), axis=0, keepdims=True)
        )
    gpart[...] = jnp.concatenate(sums, axis=1)

    for level in range(2, rounds):
        learn(level)
        if level + 1 < rounds:
            tell(level + 1)

    count = n_gx * n_gy
    me = ix * n_gy + iy
    recv_all[me] = gpart[...]

    def send_grads(k, carry):
        to = k + (k >= me).astype(jnp.int32)
        pltpu.make_async_remote_copy(
            src_ref=gpart,
            dst_ref=recv_all.at[me],
            send_sem=grad_send.at[0],
            recv_sem=grad_recv.at[0],
            device_id=(lax.div(to, n_gy), lax.rem(to, n_gy)),
            device_id_type=MESH,
        ).start()
        return carry

    lax.fori_loop(0, count - 1, send_grads, 0)

    def depth_body(i, carry):
        start = pl.multiple_of(i * 8, 8)
        for c in range(tiles):
            own = pl.ds(start + OWN, 8)
            depth_out[pl.ds(start, 8), c * LANES : (c + 1) * LANES] = jnp.where(
                statics[WET, c, own, :] > 0.0, last_h[c, own, :], raw_d[c, pl.ds(start, 8), :]
            )
        return carry

    lax.fori_loop(0, rows // 8, depth_body, 0)

    def first_face(coefs, lm, lp, h, n, t, q, v, zh, zn, zt, a, uv, p, r):
        alpha, beta, gamma = coefs[:3]
        gh, gn, gt = zh[1] - zh[0], zn[1] - zn[0], zt[1] - zt[0]
        dn = n[1] - n[0]
        fast_l, slow_l, fast_r, slow_r = split_speed_grads(
            *lm, *lp, coefs,
            gh * dn + gn * (q[1] - q[0]) + gt * (v[1] - v[0]),
            gh * (h[1] - h[0]) + gn * dn + gt * (t[1] - t[0]),
        )
        jump = gamma * gh
        return (
            alpha * (gn * a[0] - gt * uv[0]) + (fast_l * p[0] - slow_l * r[0]) - jump,
            (fast_r * p[1] - slow_r * r[1]) - beta * (gn * a[1] - gt * uv[1]) + jump,
        )

    def first_row_face(c, start):
        here, after = pl.ds(start, 8), pl.ds(start + 1, 8)

        def pair(k):
            return f_at(k, c, here), f_at(k, c, after)

        def z_pair(k):
            return adj[k, c, here, :], adj[k, c, after, :]

        return first_face(
            coefs_of(0, 0, c, here), pair(LMX), pair(LPX), pair(H), pair(MX), pair(MY), pair(QX),
            pair(TT), z_pair(ADJ), z_pair(ZX), z_pair(ZY), pair(AX), pair(UV), pair(PX), pair(RX),
        )

    for c in range(tiles):
        row_flux[0, c, pl.ds(OWN - 8, 8), :] = first_row_face(c, OWN - 8)[1]

    def backward_first(row):
        start = row + OWN
        here, before = pl.ds(start, 8), pl.ds(start - 1, 8)

        def col_face(c):
            def pair(k):
                return f_at(k, c, here), f_right(k, c, here)

            def z_pair(k):
                return adj[k, c, here, :], adj[k + TERM_R - TERM, c, here, :]

            return first_face(
                coefs_of(0, 1, c, here), pair(LMY), pair(LPY), pair(H), pair(MY), pair(MX),
                pair(QY), pair(TT), z_pair(ADJ), z_pair(ZY), z_pair(ZX), pair(AY), pair(UV),
                pair(PY), pair(RY),
            )

        current = pltpu.roll(col_face(wide - 1)[1], 1, 1)
        for c in range(tiles):
            left, right = first_row_face(c, start)
            row_flux[0, c, here, :] = right
            left_y, right_y = col_face(c)
            current, last = pltpu.roll(right_y, 1, 1), current
            entering = jnp.where(lane == 0, last, current)
            across = left + row_flux[0, c, before, :] + (left_y + entering)
            walls = adj[ZX, c, here, :] * f_at(BX, c, here) + adj[ZY, c, here, :] * f_at(BY, c, here)
            adjoint_out[pl.ds(row, 8), c * LANES : (c + 1) * LANES] = (
                adj[ADJ, c, here, :] + across - walls
            )

    sweep(backward_first, 0, rows // 8, G_BACK_FIRST)

    for sem in (grad_send, grad_recv):
        others = recv_all.at[pl.ds(0, count - 1)]
        pltpu.make_async_copy(others, others, sem.at[0]).wait()
    total = jnp.sum(recv_all[...], axis=0)
    for s in range(2):
        grad_out[s : s + 1, :] = total[:, s * dam_count : (s + 1) * dam_count]


def place(*refs):
    sources, targets, sem = refs[:3], refs[3:6], refs[6]
    copies = [
        pltpu.make_async_copy(source, target, sem.at[k])
        for k, (source, target) in enumerate(zip(sources, targets))
    ]
    for copy in copies:
        copy.start()
    for copy in copies:
        copy.wait()


def on_device(
    n_gx,
    n_gy,
    water_depth,
    momentum_x,
    momentum_y,
    wet_mask,
    damage_class,
    damage_rates,
    dam_cell,
    releases,
):
    rows, cols = water_depth.shape
    tiles = cols // LANES
    wide = tiles + 1
    high = rows + 2 * HALO + 2 * TOP
    dam_count = dam_cell.shape[0]
    f32 = jnp.float32
    plane = (wide, high, LANES)
    own = (tiles, rows, LANES)
    anywhere = pl.BlockSpec(memory_space=pl.ANY)
    vmem = pl.BlockSpec(memory_space=pltpu.VMEM)
    dma = pltpu.SemaphoreType.DMA
    results = pl.pallas_call(
        functools.partial(kernel, n_gx, n_gy, cols * n_gy, damage_rates.shape[0]),
        out_shape=(
            pltpu.VMEM((rows, cols), f32),
            pltpu.VMEM((rows, cols), f32),
            pltpu.VMEM(releases.shape[::-1], f32),
        ),
        in_specs=[anywhere] * 8,
        out_specs=(vmem, vmem, vmem),
        scratch_shapes=[
            pltpu.VMEM(own, f32),
            pltpu.VMEM(own, f32),
            pltpu.VMEM(own, f32),
            pltpu.VMEM(own, jnp.int32),
            pltpu.VMEM(own, jnp.int32),
            pltpu.VMEM((32,) + plane, f32),
            pltpu.VMEM((19,) + plane, f32),
            pltpu.VMEM((4,) + plane, f32),
            pltpu.VMEM((2, 2, 7) + plane, f32),
            pltpu.VMEM((2,) + plane, f32),
            pltpu.VMEM((8,) + plane, f32),
            pltpu.VMEM(plane, f32),
            pltpu.VMEM((3,) + plane, f32),
            pltpu.VMEM((4,) + plane, f32),
            pltpu.VMEM((cols, dam_count), jnp.bfloat16),
            pltpu.VMEM((rows, LANES), f32),
            pltpu.VMEM((2, tiles, 16, LANES), f32),
            pltpu.VMEM((2, tiles, 16, LANES), f32),
            pltpu.VMEM((2, 16, rows), f32),
            pltpu.VMEM((2, 16, rows), f32),
            pltpu.VMEM((4, 8, LANES), f32),
            pltpu.VMEM((1, 2 * dam_count), f32),
            pltpu.VMEM((n_gx * n_gy, 1, 2 * dam_count), f32),
            pltpu.SMEM(damage_rates.shape, f32),
            pltpu.VMEM((1, dam_count), jnp.int32),
            pltpu.VMEM(releases.shape[::-1], f32),
            dma((3,)),
            pltpu.SemaphoreType.REGULAR((max((n_gx - 1).bit_length(), 1),)),
            dma((5, tiles)),
            dma((8,)),
            dma((8,)),
            dma((1,)),
            dma((1,)),
        ],
        compiler_params=pltpu.CompilerParams(
            collective_id=0, has_side_effects=True, vmem_limit_bytes=56 * 1024 * 1024
        ),
        name="window",
    )(
        water_depth,
        momentum_x,
        momentum_y,
        wet_mask,
        damage_class,
        damage_rates,
        dam_cell.reshape(1, dam_count),
        releases.T,
    )
    final_depth, adjoint, grad = pl.pallas_call(
        place,
        out_shape=tuple(jax.ShapeDtypeStruct(value.shape, f32) for value in results),
        in_specs=[vmem] * 3,
        out_specs=(anywhere,) * 3,
        scratch_shapes=[dma((3,))],
        name="place",
    )(*(pltpu.with_memory_space_constraint(value, pltpu.VMEM) for value in results))
    return final_depth, adjoint, grad.T


def solution(mesh):
    n_gx, n_gy = mesh.shape["gx"], mesh.shape["gy"]
    grid = P("gx", "gy")
    return jax.shard_map(
        functools.partial(on_device, n_gx, n_gy),
        mesh=mesh,
        in_specs=(grid,) * 5 + (P(),) * 3,
        out_specs=(grid, grid, P()),
        check_vma=False,
    )
```

```python
import functools

import jax
import jax.numpy as jnp
from jax import lax
from jax.experimental import pallas as pl
from jax.experimental.pallas import tpu as pltpu
from jax.sharding import PartitionSpec as P

GRAVITY = 9.81
TIME_RATIO = 0.05
INFLOW_GAIN = 0.25
HALO = 4
LANES = 128
TOP = 8
OWN = TOP + HALO
G_STATIC, G_FACES, G_OUTER, G_FIRST, G_LAST, G_BACK_LAST, G_BACK_FIRST = 2, 2, 14, 6, 15, 5, 1
MESH = pl.DeviceIdType.MESH


def sweep(body, first, last, group):
    whole = (last - first) // group

    def run(i, carry):
        base = pl.multiple_of(i * (8 * group), 8)
        for j in range(group):
            body(base + 8 * (first + j))
        return carry

    lax.fori_loop(0, whole, run, 0)
    for chunk in range(first + whole * group, last):
        body(8 * chunk)


def pipeline(stages, first, last, group=1, begin=None, end=None):
    depth = len(stages)
    begin = first + depth - 1 if begin is None else begin
    end = last if end is None else end

    def step(at, index=None):
        for k in reversed(range(depth)):
            if index is None:
                stages[k](at - 8 * k, None)
            elif first <= index - k < last:
                stages[k](at - 8 * k, index - k)

    for index in range(first, begin):
        step(8 * index, index)
    whole = (end - begin) // group

    def run(i, carry):
        base = pl.multiple_of(i * (8 * group), 8)
        for j in range(group):
            step(base + 8 * (begin + j))
        return carry

    lax.fori_loop(0, whole, run, 0)
    for index in range(begin + whole * group, last + depth - 1):
        step(8 * index, index)


def three_parts(values):
    parts = []
    for _ in range(3):
        part = values.astype(jnp.bfloat16)
        values = values - part.astype(jnp.float32)
        parts.append(part)
    return parts


def halved_on_tie(value, picks, ties):
    return jnp.where(picks, value, jnp.where(ties, 0.5 * value, 0.0))


def split_speed_grads(lm_l, lm_r, lp_l, lp_r, coefs, d_term, k_term):
    _, _, _, slow, fast, e_slow, e_fast = coefs
    g_slow = e_slow * (fast * k_term - d_term)
    g_fast = e_fast * (d_term - slow * k_term)
    slow_l = halved_on_tie(g_slow, lm_l < lm_r, lm_l == lm_r)
    fast_l = halved_on_tie(g_fast, lp_l > lp_r, lp_l == lp_r)
    return fast_l, slow_l, g_fast - fast_l, g_slow - slow_l


def kernel(
    n_gx,
    n_gy,
    total_cols,
    classes,
    depth_in,
    mx_in,
    my_in,
    wet_in,
    class_in,
    rates_in,
    dams_in,
    releases_in,
    depth_out,
    adjoint_out,
    grad_out,
    raw_d,
    raw_x,
    raw_y,
    raw_wet,
    raw_cls,
    first,
    second,
    statics,
    faces,
    inflow,
    adj,
    last_h,
    row_flux,
    col_flux,
    col_hot,
    pack_cols,
    send_rows,
    recv_rows,
    send_cols,
    recv_cols,
    recv_corner,
    gpart,
    recv_all,
    rates,
    dams,
    releases,
    small_sem,
    know_sem,
    in_sem,
    edge_send,
    edge_recv,
    grad_send,
    grad_recv,
):
    rows, cols = depth_in.shape
    tiles = cols // LANES
    wide = tiles + 1
    span = rows + 2 * HALO
    chunks = span // 8
    ix, iy = lax.axis_index("gx"), lax.axis_index("gy")
    lane = lax.broadcasted_iota(jnp.int32, (8, LANES), 1)

    has_up, has_down = ix > 0, ix < n_gx - 1
    has_left, has_right = iy > 0, iy < n_gy - 1

    barrier = pltpu.get_barrier_semaphore()
    for step in range(1, n_gy):
        pl.semaphore_signal(
            barrier, inc=1, device_id=(ix, lax.rem(iy + step, n_gy)), device_id_type=MESH
        )
    sides = (
        (has_up, -1, 0),
        (has_down, 1, 0),
        (has_left, 0, -1),
        (has_right, 0, 1),
        (has_up & has_left, -1, -1),
        (has_up & has_right, -1, 1),
        (has_down & has_left, 1, -1),
        (has_down & has_right, 1, 1),
    )
    corners = 0
    for exists, dx, dy in sides[:2] + sides[4:]:
        corners = corners + exists.astype(jnp.int32)

        @pl.when(exists)
        def _(dx=dx, dy=dy):
            pl.semaphore_signal(barrier, inc=1, device_id=(ix + dx, iy + dy), device_id_type=MESH)

    small = [
        pltpu.make_async_copy(source, target, small_sem.at[index])
        for index, (source, target) in enumerate(
            ((rates_in, rates), (dams_in, dams), (releases_in, releases))
        )
    ]
    for copy in small[:1]:
        copy.start()
    loads = []
    for c in (0, tiles - 1, *range(1, tiles - 1)):
        for index, (source, target) in enumerate(
            ((wet_in, raw_wet), (class_in, raw_cls), (depth_in, raw_d), (mx_in, raw_x), (my_in, raw_y))
        ):
            copy = pltpu.make_async_copy(
                source.at[:, pl.ds(c * LANES, LANES)], target.at[c], in_sem.at[index, c]
            )
            copy.start()
            loads.append(copy)
    for copy in small[1:]:
        copy.start()

    small[0].wait()
    for copy in loads[:10]:
        copy.wait()

    rate = [rates[k] for k in range(classes)]

    def coded_chunk(c, start, size=8):
        at = (c, pl.ds(start, size), slice(None))
        wet = raw_wet[at] > 0
        cls = raw_cls[at]
        weight = jnp.full(cls.shape, rate[0])
        for k in range(1, classes):
            weight = jnp.where(cls == k, rate[k], weight)
        return (
            jnp.where(wet, raw_d[at], -1.0),
            raw_x[at],
            raw_y[at],
            jnp.where(wet, weight, 0.0),
        )

    def pack_body(i, carry):
        start = pl.multiple_of(i * 8, 8)
        left = coded_chunk(0, start)
        right = coded_chunk(tiles - 1, start)
        packed = jnp.zeros((8, LANES), jnp.float32)
        for k in range(4):
            mine = (lane >= 4 * k) & (lane < 4 * k + 4)
            packed = jnp.where(mine, pltpu.roll(left[k], 4 * k, 1) if k else left[k], packed)
            mine = (lane >= 16 + 4 * k) & (lane < 20 + 4 * k)
            packed = jnp.where(mine, pltpu.roll(right[k], 20 + 4 * k, 1), packed)
        pack_cols[pl.ds(start, 8), :] = packed
        return carry

    lax.fori_loop(0, rows // 8, pack_body, 0, unroll=16)
    for copy in loads[10:]:
        copy.wait()
    for c in range(tiles):
        for side, start, pick in ((0, 0, 0), (1, rows - 8, 4)):
            four = coded_chunk(c, start)
            for k in range(4):
                send_rows[side, c, 4 * k : 4 * k + 4, :] = four[k][pick : pick + 4]
    turned = jnp.transpose(pack_cols[...])
    send_cols[0] = turned[0:16]
    send_cols[1] = turned[16:32]

    pl.semaphore_wait(barrier, (n_gy - 1) + corners)

    rounds = (n_gx - 1).bit_length()

    def reach(level):
        return (ix >= 2**level, -(2**level)), (ix + 2**level < n_gx, 2**level)

    def tell(level):
        for exists, offset in reach(level):

            @pl.when(exists)
            def _(offset=offset):
                pl.semaphore_signal(
                    know_sem.at[level], inc=1, device_id=(ix + offset, iy), device_id_type=MESH
                )

    def learn(level):
        pl.semaphore_wait(
            know_sem.at[level], sum(exists.astype(jnp.int32) for exists, _ in reach(level))
        )

    def edge_copy(index):
        _, dx, dy = sides[index]
        opposite = (1, 0, 3, 2, 7, 6, 5, 4)[index]
        if index < 2:
            source, target = send_rows.at[index], recv_rows.at[opposite]
        elif index < 4:
            source, target = send_cols.at[index - 2], recv_cols.at[opposite - 2]
        else:
            first = 0 if index < 6 else rows - 8
            source, target = pack_cols.at[pl.ds(first, 8), :], recv_corner.at[opposite - 4]
        return pltpu.make_async_remote_copy(
            src_ref=source,
            dst_ref=target,
            send_sem=edge_send.at[index],
            recv_sem=edge_recv.at[opposite],
            device_id=(ix + dx, iy + dy),
            device_id_type=MESH,
        )

    for index in (0, 1, 4, 5, 6, 7, 2, 3):

        @pl.when(sides[index][0])
        def _(index=index):
            edge_copy(index).start()

    if rounds > 0:
        tell(0)

    H, MX, MY, LMX, LPX, LMY, LPY, PX, RX, PY, RY = range(11)
    IH = 11
    QX, QY, TT, AX, AY, UV, WX, WY, BX, BY = range(11, 21)
    NEXT = 21
    WET, WGT, FMX, FMY = range(4)
    ALPHA, BETA, GAMMA, SLOW, FAST, ESLOW, EFAST = range(7)

    def put_start(c, at_rows, size, four):
        wet = four[0] > 0.0
        at = (c, pl.ds(at_rows, size), slice(None))
        first[(H,) + at] = jnp.where(wet, four[0], 1.0)
        first[(MX,) + at] = jnp.where(wet, four[1], 0.0)
        first[(MY,) + at] = jnp.where(wet, four[2], 0.0)
        statics[(WGT,) + at] = jnp.where(wet, four[3], 0.0)
        statics[(WET,) + at] = jnp.where(wet, 1.0, 0.0)

    def own_body(i, carry):
        start = pl.multiple_of(i * 8, 8)
        for c in range(tiles):
            put_start(c, start + OWN, 8, coded_chunk(c, start))
        return carry

    lax.fori_loop(0, rows // 8, own_body, 0, unroll=4)

    for copy in small[1:]:
        copy.wait()
    cell = dams[...]
    if total_cols & (total_cols - 1) == 0:
        dam_row = lax.shift_right_logical(cell, total_cols.bit_length() - 1)
    else:
        dam_row = lax.div(cell, total_cols)
    dam_col = cell - dam_row * total_cols
    dam_count = cell.shape[1]
    local_row = dam_row - ix * rows
    local_col = dam_col - iy * cols
    amounts = INFLOW_GAIN * releases[...]
    thrice = lambda values: jnp.concatenate([values] * 3, axis=1)
    amounts = jnp.concatenate(
        [part.astype(jnp.float32) for part in three_parts(amounts)], axis=1
    )
    wide_row = lax.broadcasted_iota(jnp.int32, (span, 3 * dam_count), 0) - HALO
    row_hot = wide_row == thrice(local_row)
    gain_rows = jnp.concatenate(
        [jnp.where(row_hot, amounts[s : s + 1], 0.0) for s in range(2)], axis=0
    ).astype(jnp.bfloat16)
    position = lax.broadcasted_iota(jnp.int32, (LANES, 3 * dam_count), 0)
    col_thrice = thrice(local_col)
    hots = []
    for c in range(wide):
        if c < tiles:
            column = position + c * LANES
        else:
            column = jnp.where(
                position < HALO,
                position + cols,
                jnp.where(position >= LANES - HALO, position - LANES, -2 * LANES),
            )
        hot = (column == col_thrice).astype(jnp.float32).astype(jnp.bfloat16)
        if c < tiles:
            col_hot[c * LANES : (c + 1) * LANES, :] = hot[:, :dam_count]
        hots.append(hot)
    poured = lax.dot_general(
        gain_rows, jnp.concatenate(hots, axis=0), (((1,), (1,)), ((), ())),
        preferred_element_type=jnp.float32,
    )
    for s in range(2):
        for c in range(wide):
            inflow[s, c, TOP : TOP + span, :] = poured[
                s * span : (s + 1) * span, c * LANES : (c + 1) * LANES
            ]

    def turned(get, cs, shift, step):
        needed = sorted({c for c in cs} | {(c + step) % wide for c in cs})
        values = {c: pltpu.roll(get(c), shift, 1) for c in needed}
        edge = LANES - 1 if step > 0 else 0
        return {c: jnp.where(lane == edge, values[(c + step) % wide], values[c]) for c in cs}

    def next_lanes(values, cs=None):
        cs = range(wide) if cs is None else cs
        return list(turned(lambda c: values[c], cs, LANES - 1, 1).values())

    def last_lanes(values):
        return list(turned(lambda c: values[c], range(wide), 1, -1).values())

    FIRST_NEXT = (H, MX, MY, LMY, LPY, QY, TT, AY, UV, PY, RY)
    SECOND_NEXT = (H, MY, LMY, LPY, PY, RY, IH)
    SECOND_AT = 12

    def base_prims(h, mx, my, ih):
        ux, uy = mx * ih, my * ih
        squared = GRAVITY * h
        cc = squared * lax.rsqrt(squared)
        half = 0.5 * cc
        out = {H: h, MX: mx, MY: my, LMX: ux - cc, LPX: ux + cc, LMY: uy - cc, LPY: uy + cc}
        half_i, ux_i, uy_i = half * ih, ux * ih, uy * ih
        out |= {PX: half_i - ux_i, RX: half_i + ux_i, PY: half_i - uy_i, RY: half_i + uy_i}
        return out, ux, uy, squared, cc, half

    def reader(source, keys, offset):
        def at(k, c, rows_at):
            return source[k, c, rows_at, :]

        def right(k, c, rows_at):
            return source[offset + keys.index(k), c, rows_at, :]

        return at, right

    f_at, f_right = reader(first, FIRST_NEXT, NEXT)
    s_at, s_right = reader(second, SECOND_NEXT, SECOND_AT)

    def face(step, dim, c, here, lm_l, lm_r, lp_l, lp_r):
        low, high = jnp.minimum(lm_l, lm_r), jnp.maximum(lp_l, lp_r)
        slow, fast = jnp.minimum(low, 0.0), jnp.maximum(high, 0.0)
        inverse = 1.0 / (fast - slow)
        masked = statics[FMX + dim, c, here, :] * inverse
        alpha, beta = fast * masked, slow * masked
        gamma = slow * alpha
        e_slow = halved_on_tie(alpha * inverse, low < 0.0, low == 0.0)
        e_fast = halved_on_tie(beta * inverse, high > 0.0, high == 0.0)
        for k, value in enumerate((alpha, beta, gamma, slow, fast, e_slow, e_fast)):
            faces[step, dim, k, c, here, :] = value
        return alpha, beta, gamma

    def coefs_of(step, dim, c, here):
        return [faces[step, dim, k, c, here, :] for k in range(7)]

    def crossing(coefs, flux_l, flux_r, held_l, held_r):
        alpha, beta, gamma = coefs
        return alpha * flux_l - beta * flux_r + gamma * (held_r - held_l)

    def net_of(k, here):
        values = [col_flux[k, c, here, :] for c in range(wide)]
        return [mine - entering for mine, entering in zip(values, last_lanes(values))]

    RIGHT, LEFT = 0, 1
    EVERY = tuple(range(wide))

    def shift_stage(rights, lefts):
        def shift(row):
            here = pl.ds(row + TOP, 8)

            def wet_at(c):
                return statics[WET, c, here, :]

            for c, value in turned(wet_at, rights, LANES - 1, 1).items():
                adj[RIGHT, c, here, :] = value
            for c, value in turned(wet_at, lefts, 1, -1).items():
                adj[LEFT, c, here, :] = value
            for j, k in enumerate((H, MX, MY)):
                shifted = turned(lambda c, k=k: first[k, c, here, :], rights, LANES - 1, 1)
                for c, value in shifted.items():
                    first[NEXT + j, c, here, :] = value

        return shift

    def walls_of(scale, lower, upper, u, n, q, a, cc, half):
        single = scale * (lower - upper)
        both = scale * (2.0 - (lower + upper))
        size = jnp.abs(u)
        return single * q + both * ((size + cc) * n), single * a + both * (u * (half - size))

    def static_x(c, start):
        here = pl.ds(start, 8)
        scale = TIME_RATIO * statics[WET, c, here, :]
        above = statics[WET, c, pl.ds(start - 1, 8), :]
        below = statics[WET, c, pl.ds(start + 1, 8), :]
        statics[FMX, c, here, :] = scale * below
        h, mx, my = (first[k, c, here, :] for k in (H, MX, MY))
        out, ux, uy, squared, cc, half = base_prims(h, mx, my, 1.0 / h)
        pressure = 0.5 * squared * h
        out[QX], out[QY], out[TT] = mx * ux + pressure, my * uy + pressure, mx * uy
        out[AX], out[AY], out[UV] = squared - ux * ux, squared - uy * uy, ux * uy
        out[WX], out[BX] = walls_of(scale, above, below, ux, mx, out[QX], out[AX], cc, half)
        for k, value in out.items():
            if k not in (H, MX, MY):
                first[k, c, here, :] = value
        return uy, my, out[QY], out[AY], cc, half

    def static_y(c, here, parts=None):
        scale = TIME_RATIO * statics[WET, c, here, :]
        if parts is None:
            h, my = first[H, c, here, :], first[MY, c, here, :]
            squared = GRAVITY * h
            cc = squared * lax.rsqrt(squared)
            parts = my * (1.0 / h), my, first[QY, c, here, :], first[AY, c, here, :], cc, 0.5 * cc
        first[WY, c, here, :], first[BY, c, here, :] = walls_of(
            scale, adj[LEFT, c, here, :], adj[RIGHT, c, here, :], *parts
        )

    def static_next(c, here):
        scale = TIME_RATIO * statics[WET, c, here, :]
        statics[FMY, c, here, :] = scale * adj[RIGHT, c, here, :]
        h, mx, my = (first[NEXT + k, c, here, :] for k in range(3))
        out, ux, uy, squared, cc, half = base_prims(h, mx, my, 1.0 / h)
        out[QY], out[TT] = my * uy + 0.5 * squared * h, mx * uy
        out[AY], out[UV] = squared - uy * uy, ux * uy
        for j, k in enumerate(FIRST_NEXT):
            if j >= 3:
                first[NEXT + j, c, here, :] = out[k]

    def static_stage(xs, ys, nexts):
        def static(row):
            start = row + TOP
            here = pl.ds(start, 8)
            for c in range(wide):
                parts = static_x(c, start) if c in xs else None
                if c in ys:
                    static_y(c, here, parts)
                if c in nexts:
                    static_next(c, here)

        return static

    def first_faces(cols_at, rows_at):
        def faces_of(row):
            start = row + TOP
            here, after = pl.ds(start, 8), pl.ds(start + 1, 8)
            for c in cols_at:
                coefs = face(
                    0, 1, c, here, f_at(LMY, c, here), f_right(LMY, c, here),
                    f_at(LPY, c, here), f_right(LPY, c, here),
                )
                for k, (flux, held) in enumerate(((MY, H), (TT, MX), (QY, MY))):
                    col_flux[k, c, here, :] = crossing(
                        coefs, f_at(flux, c, here), f_right(flux, c, here),
                        f_at(held, c, here), f_right(held, c, here),
                    )
            for c in rows_at:
                coefs = face(
                    0, 0, c, here, f_at(LMX, c, here), f_at(LMX, c, after),
                    f_at(LPX, c, here), f_at(LPX, c, after),
                )
                for k, (flux, held) in enumerate(((MX, H), (QX, MX), (TT, MY))):
                    row_flux[k, c, here, :] = crossing(
                        coefs, f_at(flux, c, here), f_at(flux, c, after),
                        f_at(held, c, here), f_at(held, c, after),
                    )

        return faces_of

    inner, own_tiles = EVERY[: tiles - 1], EVERY[:tiles]
    shift_inner = shift_stage(inner, EVERY[1:tiles])
    static_inner = static_stage(own_tiles, EVERY[1 : tiles - 1], inner)
    faces_inner = first_faces(inner, own_tiles)

    def plain(stage):
        return lambda row, index: stage(row)

    pipeline((plain(shift_inner), plain(static_inner)), 1, chunks - 1, G_STATIC)
    pipeline((plain(faces_inner),), 1, chunks - 2, G_FACES)

    for index in range(8):

        @pl.when(sides[index][0])
        def _(index=index):
            copy = edge_copy(index)
            copy.wait_send()
            opposite = (1, 0, 3, 2, 7, 6, 5, 4)[index]
            if index < 2:
                target = recv_rows.at[index]
            elif index < 4:
                target = recv_cols.at[index - 2]
            else:
                target = recv_corner.at[index - 4]
            pltpu.make_async_copy(target, target, edge_recv.at[index]).wait()

    if rounds > 0:
        learn(0)
        if rounds > 1:
            tell(1)

    for c in range(tiles):
        for side, exists, at_rows in ((0, has_up, TOP), (1, has_down, OWN + rows)):
            four = [recv_rows[side, c, 4 * k : 4 * k + 4, :] for k in range(4)]
            four[0] = jnp.where(exists, four[0], -1.0)
            put_start(c, at_rows, 4, four)

    halves = jnp.concatenate(
        [recv_cols[0], recv_cols[1], jnp.zeros((LANES - 32, rows), jnp.float32)], axis=0
    )
    pack_cols[...] = jnp.transpose(halves)

    def rim_tile(left_part, right_part, k, left_at, right_at, from_left, from_right):
        fill = -1.0 if k == 0 else 0.0
        on_right = (lane < HALO) & from_right
        on_left = (lane >= LANES - HALO) & from_left
        shift_r = (LANES - right_at - 4 * k) % LANES
        shift_l = (LANES - HALO - left_at - 4 * k) % LANES
        right_val = pltpu.roll(right_part, shift_r, 1) if shift_r else right_part
        left_val = pltpu.roll(left_part, shift_l, 1) if shift_l else left_part
        return jnp.where(on_right, right_val, jnp.where(on_left, left_val, fill))

    def rim_body(i, carry):
        start = pl.multiple_of(i * 8, 8)
        part = pack_cols[pl.ds(start, 8), :]
        four = [rim_tile(part, part, k, 0, 16, has_left, has_right) for k in range(4)]
        put_start(tiles, start + OWN, 8, four)
        return carry

    lax.fori_loop(0, rows // 8, rim_body, 0, unroll=16)
    for left_slot, right_slot, exists, at_rows, pick in (
        (0, 1, has_up, TOP, 4),
        (2, 3, has_down, OWN + rows, 0),
    ):
        four = [
            rim_tile(
                recv_corner[left_slot],
                recv_corner[right_slot],
                k,
                16,
                0,
                has_left & exists,
                has_right & exists,
            )[pick : pick + 4]
            for k in range(4)
        ]
        put_start(tiles, at_rows, 4, four)

    shift_whole, shift_outer = shift_stage(EVERY, EVERY), shift_stage(EVERY[tiles - 1 :], (0, tiles))
    static_whole = static_stage(EVERY, EVERY, EVERY)
    static_outer = static_stage(EVERY[tiles:], (0, *EVERY[tiles - 1 :]), EVERY[tiles - 1 :])
    faces_whole, faces_outer = first_faces(EVERY, EVERY), first_faces(EVERY[tiles - 1 :], EVERY[tiles:])

    def chosen(whole_stage, outer_stage, last_inner):
        def stage(row, index):
            inside = index is None or 1 <= index <= last_inner
            (outer_stage if inside else whole_stage)(row)

        return stage

    pipeline(
        (
            chosen(shift_whole, shift_outer, chunks - 2),
            chosen(static_whole, static_outer, chunks - 2),
        ),
        0, chunks, G_OUTER, begin=2, end=chunks - 1,
    )

    def first_cells(row):
        start = row + TOP
        here, before = pl.ds(start, 8), pl.ds(start - 1, 8)
        net = [net_of(k, here) for k in range(3)]
        for c in range(wide):
            new = []
            for k in range(3):
                value = row_flux[k, c, here, :]
                change = value - row_flux[k, c, before, :] + net[k][c]
                if k > 0:
                    change = change + f_at((None, WX, WY)[k], c, here)
                new.append(f_at((H, MX, MY)[k], c, here) - change)
            h = new[0] + inflow[0, c, here, :]
            ih = 1.0 / h
            out = base_prims(h, new[1], new[2], ih)[0]
            out[IH] = ih
            for k, value in out.items():
                second[k, c, here, :] = value

    def first_shift(row):
        here = pl.ds(row + TOP, 8)
        heights = next_lanes([second[H, c, here, :] for c in range(wide)])
        flows = next_lanes([second[MY, c, here, :] for c in range(wide)])
        for c, (h, n) in enumerate(zip(heights, flows)):
            ih = 1.0 / h
            out = base_prims(h, n, n, ih)[0]
            out[IH] = ih
            for j, k in enumerate(SECOND_NEXT):
                second[SECOND_AT + j, c, here, :] = out[k]

    TERM, ADJ, ZX, ZY, TERM_R, ADJ_R, ZX_R, ZY_R = range(8)

    def last_cols(row):
        here = pl.ds(row + TOP, 8)
        for c in range(wide):
            coefs = face(
                1, 1, c, here, s_at(LMY, c, here), s_right(LMY, c, here),
                s_at(LPY, c, here), s_right(LPY, c, here),
            )
            col_flux[0, c, here, :] = crossing(
                coefs, s_at(MY, c, here), s_right(MY, c, here),
                s_at(H, c, here), s_right(H, c, here),
            )

    def last_cells(row):
        start = row + TOP
        here, after, before = pl.ds(start, 8), pl.ds(start + 1, 8), pl.ds(start - 1, 8)
        net = net_of(0, here)
        for c in range(wide):
            coefs = face(
                1, 0, c, here, s_at(LMX, c, here), s_at(LMX, c, after),
                s_at(LPX, c, here), s_at(LPX, c, after),
            )
            value = crossing(
                coefs, s_at(MX, c, here), s_at(MX, c, after),
                s_at(H, c, here), s_at(H, c, after),
            )
            row_flux[0, c, here, :] = value
            change = value - row_flux[0, c, before, :] + net[c]
            h = s_at(H, c, here) - change + inflow[1, c, here, :]
            last_h[c, here, :] = h
            adj[TERM, c, here, :] = statics[WGT, c, here, :] * h

    def adj_shift(*planes):
        def shift(row):
            here = pl.ds(row + TOP, 8)
            for k in planes:
                values = [adj[k, c, here, :] for c in range(wide)]
                for c, value in enumerate(next_lanes(values)):
                    adj[TERM_R + k, c, here, :] = value

        return shift

    pipeline(
        (chosen(faces_whole, faces_outer, chunks - 3), plain(first_cells), plain(first_shift)),
        0, chunks, G_FIRST, begin=3, end=chunks - 2,
    )
    if rounds > 1:
        learn(1)
        if rounds > 2:
            tell(2)
    pipeline((plain(last_cols), plain(last_cells), plain(adj_shift(TERM))), 0, chunks, G_LAST)

    def last_face(coefs, lm, lp, h, n, z, p, r, ih):
        alpha, beta, gamma = coefs[:3]
        gh = z[1] - z[0]
        fast_l, slow_l, fast_r, slow_r = split_speed_grads(
            *lm, *lp, coefs, gh * (n[1] - n[0]), gh * (h[1] - h[0])
        )
        jump = gamma * gh
        return (
            fast_l * p[0] - slow_l * r[0] - jump,
            alpha * gh + (fast_l + slow_l) * ih[0],
        ), (
            fast_r * p[1] - slow_r * r[1] + jump,
            (fast_r + slow_r) * ih[1] - beta * gh,
        )

    def back_cols(row):
        here = pl.ds(row + TOP, 8)
        for c in range(wide):

            def pair(k):
                return s_at(k, c, here), s_right(k, c, here)

            left, right = last_face(
                coefs_of(1, 1, c, here), pair(LMY), pair(LPY), pair(H), pair(MY),
                (adj[TERM, c, here, :], adj[TERM_R, c, here, :]), pair(PY), pair(RY), pair(IH),
            )
            for k in range(2):
                col_flux[k, c, here, :] = left[k]
                col_flux[2 + k, c, here, :] = right[k]

    def back_cells(row):
        start = row + TOP
        here, after, before = pl.ds(start, 8), pl.ds(start + 1, 8), pl.ds(start - 1, 8)
        entering = [
            last_lanes([col_flux[2 + k, c, here, :] for c in range(wide)]) for k in range(2)
        ]
        for c in range(wide):

            def pair(k):
                return s_at(k, c, here), s_at(k, c, after)

            left, right = last_face(
                coefs_of(1, 0, c, here), pair(LMX), pair(LPX), pair(H), pair(MX),
                (adj[TERM, c, here, :], adj[TERM, c, after, :]), pair(PX), pair(RX), pair(IH),
            )
            in_x = []
            for k in range(2):
                row_flux[k, c, here, :] = right[k]
                in_x.append(left[k] + row_flux[k, c, before, :])
            in_y = [col_flux[k, c, here, :] + entering[k][c] for k in range(2)]
            adj[ADJ, c, here, :] = adj[TERM, c, here, :] + (in_x[0] + in_y[0])
            adj[ZX, c, here, :] = in_x[1]
            adj[ZY, c, here, :] = in_y[1]

    pipeline(
        (plain(back_cols), plain(back_cells), plain(adj_shift(ADJ, ZX, ZY))),
        0, chunks, G_BACK_LAST,
    )

    own_hot = lax.broadcasted_iota(jnp.int32, (rows, dam_count), 0) == local_row
    hots = jnp.concatenate([col_hot[...]] * 3, axis=0)
    sums = []
    for plane in (ADJ, TERM):
        parts = [three_parts(adj[plane, c, OWN : OWN + rows, :]) for c in range(tiles)]
        picked = lax.dot_general(
            jnp.concatenate([parts[c][k] for k in range(3) for c in range(tiles)], axis=1), hots,
            (((1,), (0,)), ((), ())), preferred_element_type=jnp.float32,
        )
        sums.append(
            INFLOW_GAIN * jnp.sum(jnp.where(own_hot, picked, 0.0), axis=0, keepdims=True)
        )
    gpart[...] = jnp.concatenate(sums, axis=1)

    for level in range(2, rounds):
        learn(level)
        if level + 1 < rounds:
            tell(level + 1)

    count = n_gx * n_gy
    me = ix * n_gy + iy
    recv_all[me] = gpart[...]

    def send_grads(k, carry):
        to = k + (k >= me).astype(jnp.int32)
        pltpu.make_async_remote_copy(
            src_ref=gpart,
            dst_ref=recv_all.at[me],
            send_sem=grad_send.at[0],
            recv_sem=grad_recv.at[0],
            device_id=(lax.div(to, n_gy), lax.rem(to, n_gy)),
            device_id_type=MESH,
        ).start()
        return carry

    lax.fori_loop(0, count - 1, send_grads, 0)

    def depth_body(i, carry):
        start = pl.multiple_of(i * 8, 8)
        for c in range(tiles):
            own = pl.ds(start + OWN, 8)
            depth_out[pl.ds(start, 8), c * LANES : (c + 1) * LANES] = jnp.where(
                statics[WET, c, own, :] > 0.0, last_h[c, own, :], raw_d[c, pl.ds(start, 8), :]
            )
        return carry

    lax.fori_loop(0, rows // 8, depth_body, 0)

    def first_face(coefs, lm, lp, h, n, t, q, v, zh, zn, zt, a, uv, p, r):
        alpha, beta, gamma = coefs[:3]
        gh, gn, gt = zh[1] - zh[0], zn[1] - zn[0], zt[1] - zt[0]
        dn = n[1] - n[0]
        fast_l, slow_l, fast_r, slow_r = split_speed_grads(
            *lm, *lp, coefs,
            gh * dn + gn * (q[1] - q[0]) + gt * (v[1] - v[0]),
            gh * (h[1] - h[0]) + gn * dn + gt * (t[1] - t[0]),
        )
        jump = gamma * gh
        return (
            alpha * (gn * a[0] - gt * uv[0]) + (fast_l * p[0] - slow_l * r[0]) - jump,
            (fast_r * p[1] - slow_r * r[1]) - beta * (gn * a[1] - gt * uv[1]) + jump,
        )

    def first_row_face(c, start):
        here, after = pl.ds(start, 8), pl.ds(start + 1, 8)

        def pair(k):
            return f_at(k, c, here), f_at(k, c, after)

        def z_pair(k):
            return adj[k, c, here, :], adj[k, c, after, :]

        return first_face(
            coefs_of(0, 0, c, here), pair(LMX), pair(LPX), pair(H), pair(MX), pair(MY), pair(QX),
            pair(TT), z_pair(ADJ), z_pair(ZX), z_pair(ZY), pair(AX), pair(UV), pair(PX), pair(RX),
        )

    for c in range(tiles):
        row_flux[0, c, pl.ds(OWN - 8, 8), :] = first_row_face(c, OWN - 8)[1]

    def backward_first(row):
        start = row + OWN
        here, before = pl.ds(start, 8), pl.ds(start - 1, 8)

        def col_face(c):
            def pair(k):
                return f_at(k, c, here), f_right(k, c, here)

            def z_pair(k):
                return adj[k, c, here, :], adj[k + TERM_R - TERM, c, here, :]

            return first_face(
                coefs_of(0, 1, c, here), pair(LMY), pair(LPY), pair(H), pair(MY), pair(MX),
                pair(QY), pair(TT), z_pair(ADJ), z_pair(ZY), z_pair(ZX), pair(AY), pair(UV),
                pair(PY), pair(RY),
            )

        current = pltpu.roll(col_face(wide - 1)[1], 1, 1)
        for c in range(tiles):
            left, right = first_row_face(c, start)
            row_flux[0, c, here, :] = right
            left_y, right_y = col_face(c)
            current, last = pltpu.roll(right_y, 1, 1), current
            entering = jnp.where(lane == 0, last, current)
            across = left + row_flux[0, c, before, :] + (left_y + entering)
            walls = adj[ZX, c, here, :] * f_at(BX, c, here) + adj[ZY, c, here, :] * f_at(BY, c, here)
            adjoint_out[pl.ds(row, 8), c * LANES : (c + 1) * LANES] = (
                adj[ADJ, c, here, :] + across - walls
            )

    sweep(backward_first, 0, rows // 8, G_BACK_FIRST)

    for sem in (grad_send, grad_recv):
        others = recv_all.at[pl.ds(0, count - 1)]
        pltpu.make_async_copy(others, others, sem.at[0]).wait()
    total = jnp.sum(recv_all[...], axis=0)
    for s in range(2):
        grad_out[s : s + 1, :] = total[:, s * dam_count : (s + 1) * dam_count]


def place(*refs):
    sources, targets, sem = refs[:3], refs[3:6], refs[6]
    copies = [
        pltpu.make_async_copy(source, target, sem.at[k])
        for k, (source, target) in enumerate(zip(sources, targets))
    ]
    for copy in copies:
        copy.start()
    for copy in copies:
        copy.wait()


def on_device(
    n_gx,
    n_gy,
    water_depth,
    momentum_x,
    momentum_y,
    wet_mask,
    damage_class,
    damage_rates,
    dam_cell,
    releases,
):
    rows, cols = water_depth.shape
    tiles = cols // LANES
    wide = tiles + 1
    high = rows + 2 * HALO + 2 * TOP
    dam_count = dam_cell.shape[0]
    f32 = jnp.float32
    plane = (wide + 1, high, LANES)
    own = (tiles, rows, LANES)
    anywhere = pl.BlockSpec(memory_space=pl.ANY)
    vmem = pl.BlockSpec(memory_space=pltpu.VMEM)
    dma = pltpu.SemaphoreType.DMA
    results = pl.pallas_call(
        functools.partial(kernel, n_gx, n_gy, cols * n_gy, damage_rates.shape[0]),
        out_shape=(
            pltpu.VMEM((rows, cols), f32),
            pltpu.VMEM((rows, cols), f32),
            pltpu.VMEM(releases.shape[::-1], f32),
        ),
        in_specs=[anywhere] * 8,
        out_specs=(vmem, vmem, vmem),
        scratch_shapes=[
            pltpu.VMEM(own, f32),
            pltpu.VMEM(own, f32),
            pltpu.VMEM(own, f32),
            pltpu.VMEM(own, jnp.int32),
            pltpu.VMEM(own, jnp.int32),
            pltpu.VMEM((32,) + plane, f32),
            pltpu.VMEM((19,) + plane, f32),
            pltpu.VMEM((4,) + plane, f32),
            pltpu.VMEM((2, 2, 7) + plane, f32),
            pltpu.VMEM((2,) + plane, f32),
            pltpu.VMEM((8,) + plane, f32),
            pltpu.VMEM(plane, f32),
            pltpu.VMEM((3,) + plane, f32),
            pltpu.VMEM((4,) + plane, f32),
            pltpu.VMEM((cols, dam_count), jnp.bfloat16),
            pltpu.VMEM((rows, LANES), f32),
            pltpu.VMEM((2, tiles, 16, LANES), f32),
            pltpu.VMEM((2, tiles, 16, LANES), f32),
            pltpu.VMEM((2, 16, rows), f32),
            pltpu.VMEM((2, 16, rows), f32),
            pltpu.VMEM((4, 8, LANES), f32),
            pltpu.VMEM((1, 2 * dam_count), f32),
            pltpu.VMEM((n_gx * n_gy, 1, 2 * dam_count), f32),
            pltpu.SMEM(damage_rates.shape, f32),
            pltpu.VMEM((1, dam_count), jnp.int32),
            pltpu.VMEM(releases.shape[::-1], f32),
            dma((3,)),
            pltpu.SemaphoreType.REGULAR((max((n_gx - 1).bit_length(), 1),)),
            dma((5, tiles)),
            dma((8,)),
            dma((8,)),
            dma((1,)),
            dma((1,)),
        ],
        compiler_params=pltpu.CompilerParams(
            collective_id=0, has_side_effects=True, vmem_limit_bytes=56 * 1024 * 1024
        ),
        name="window",
    )(
        water_depth,
        momentum_x,
        momentum_y,
        wet_mask,
        damage_class,
        damage_rates,
        dam_cell.reshape(1, dam_count),
        releases.T,
    )
    final_depth, adjoint, grad = pl.pallas_call(
        place,
        out_shape=tuple(jax.ShapeDtypeStruct(value.shape, f32) for value in results),
        in_specs=[vmem] * 3,
        out_specs=(anywhere,) * 3,
        scratch_shapes=[dma((3,))],
        name="place",
    )(*(pltpu.with_memory_space_constraint(value, pltpu.VMEM) for value in results))
    return final_depth, adjoint, grad.T


def solution(mesh):
    n_gx, n_gy = mesh.shape["gx"], mesh.shape["gy"]
    grid = P("gx", "gy")
    return jax.shard_map(
        functools.partial(on_device, n_gx, n_gy),
        mesh=mesh,
        in_specs=(grid,) * 5 + (P(),) * 3,
        out_specs=(grid, grid, P()),
        check_vma=False,
    )
```
